32 devices in a mesh: seq: 16 (over z, y, core), ctx: 2 (over x).
Axes of the slice: x: 2, y: 2, z: 4, core: 2. Of those that a mesh axis runs over, the one named last changes fastest.
Arguments:
- tokens: bfloat16 [16, 1024, 512], P('seq', 'ctx'), may hold values from -6 to 6
- cotangent: bfloat16 [16, 1024, 512], P('seq', 'ctx'), may hold values from -6 to 6
- attn_norm_gain: bfloat16 [512], P(('seq', 'ctx')), may hold values from 0.099609375 to 1.8984375
- attn_norm_bias: bfloat16 [512], P(('seq', 'ctx')), may hold values from -2 to 2
- mlp_norm_gain: bfloat16 [512], P(('seq', 'ctx')), may hold values from 0.099609375 to 1.8984375
- mlp_norm_bias: bfloat16 [512], P(('seq', 'ctx')), may hold values from -2 to 2
- qkv_weight: bfloat16 [786432], P(('seq', 'ctx')), may hold values from -0.25 to 0.25
- qkv_bias: bfloat16 [1536], P(('seq', 'ctx')), may hold values from -2 to 2
- dense_weight: bfloat16 [262144], P(('seq', 'ctx')), may hold values from -3 to 3
- dense_bias: bfloat16 [512], P(('seq', 'ctx')), may hold values from -2 to 2
- fc_in_weight: bfloat16 [1048576], P(('seq', 'ctx')), may hold values from -0.25 to 0.25
- fc_in_bias: bfloat16 [2048], P(('seq', 'ctx')), may hold values from -2 to 2
- fc_out_weight: bfloat16 [1048576], P(('seq', 'ctx')), may hold values from -0.125 to 0.125
- fc_out_bias: bfloat16 [512], P(('seq', 'ctx')), may hold values from -2 to 2
Outputs:
- layer_out: bfloat16 [16, 1024, 512], P('seq', 'ctx')
- grad_tokens: bfloat16 [16, 1024, 512], P('seq', 'ctx')
- grad_attn_norm_gain: float32 [512], P(('seq', 'ctx'))
- grad_attn_norm_bias: float32 [512], P(('seq', 'ctx'))
- grad_mlp_norm_gain: float32 [512], P(('seq', 'ctx'))
- grad_mlp_norm_bias: float32 [512], P(('seq', 'ctx'))
- grad_qkv_weight: float32 [786432], P(('seq', 'ctx'))
- grad_qkv_bias: float32 [1536], P(('seq', 'ctx'))
- grad_dense_weight: float32 [262144], P(('seq', 'ctx'))
- grad_dense_bias: float32 [512], P(('seq', 'ctx'))
- grad_fc_in_weight: float32 [1048576], P(('seq', 'ctx'))
- grad_fc_in_bias: float32 [2048], P(('seq', 'ctx'))
- grad_fc_out_weight: float32 [1048576], P(('seq', 'ctx'))
- grad_fc_out_bias: float32 [512], P(('seq', 'ctx'))
The draws below stay inside these ranges and needn't reach their ends.
All inputs are finite; a program needn't handle non-finite values.
Results may differ from the reference program's by a relative error of at most 0.0096.
Values may be sent and summed in bfloat16 or wider, within the bound.
A program may use at most 128 MiB of HBM per device.

```python
import jax
import jax.numpy as jnp
from jax import lax

D = 512
HEADS = 8
FF = 2048
HEAD_DIM = 64
ROT = 16
LENGTH = 1024
SEQS = 16


def level_of(rng, extent, pieces, least, top_value):
    level, own = 1.0, jax.random.fold_in(rng, 6)
    for axis_at, blocks in pieces:
        steps = jnp.exp(jax.random.uniform(jax.random.fold_in(own, axis_at), (blocks,), jnp.float32, least / len(pieces), top_value / len(pieces)))
        level = level * jnp.repeat(steps, extent[axis_at] // blocks).reshape([-1 if axis == axis_at else 1 for axis in range(len(extent))])
    return level


def normal_values(own_key, shape, deviation, most, shards=(), kind=jnp.bfloat16):
    drawn = deviation * jax.random.normal(own_key, shape, jnp.float32)
    if shards:
        drawn = drawn * level_of(own_key, shape, shards, -0.22, 0.18)
    return jnp.clip(drawn, -most, most).astype(kind)


def setup_inputs(seed: int = 0) -> dict:
    seeds = jax.random.split(jax.random.key(seed), 15)
    return {
        "tokens": normal_values(seeds[0], (SEQS, LENGTH, D), 1.0, 6.0, ((0, 16), (1, 2))),
        "cotangent": normal_values(seeds[1], (SEQS, LENGTH, D), 1.0, 6.0, ((0, 16), (1, 2))),
        "attn_norm_gain": jnp.clip(1.0 + 0.18 * jax.random.normal(seeds[2], (D,), jnp.float32), 0.099609375, 1.8984375).astype(jnp.bfloat16),
        "attn_norm_bias": normal_values(seeds[3], (D,), 0.3, 2.0, ((0, 32),)),
        "mlp_norm_gain": jnp.clip(1.0 + 0.18 * jax.random.normal(seeds[4], (D,), jnp.float32), 0.099609375, 1.8984375).astype(jnp.bfloat16),
        "mlp_norm_bias": normal_values(seeds[5], (D,), 0.3, 2.0, ((0, 32),)),
        "qkv_weight": normal_values(seeds[6], (3 * D * D,), D ** -0.5, 0.25, ((0, 32),)),
        "qkv_bias": normal_values(seeds[7], (3 * D,), 0.3, 2.0, ((0, 32),)),
        "dense_weight": normal_values(seeds[8], (D * D,), 4 ** -0.5, 3.0, ((0, 32),)),
        "dense_bias": normal_values(seeds[9], (D,), 0.3, 2.0, ((0, 32),)),
        "fc_in_weight": normal_values(seeds[10], (D * FF,), D ** -0.5, 0.25, ((0, 32),)),
        "fc_in_bias": normal_values(seeds[11], (FF,), 0.3, 2.0, ((0, 32),)),
        "fc_out_weight": normal_values(seeds[12], (FF * D,), FF ** -0.5, 0.125, ((0, 32),)),
        "fc_out_bias": normal_values(seeds[13], (D,), 0.3, 2.0, ((0, 32),)),
    }


@jax.custom_vjp
def low(v):
    return lax.optimization_barrier(v.astype(jnp.bfloat16)).astype(jnp.float32)

@jax.custom_vjp
def low_back(v):
    return v

def low_keep(v):
    return (low(v), None)

def low_pass(kept, grad):
    return (grad,)

def back_keep(v):
    return (v, None)

def back_low(kept, grad):
    return (low(grad),)
low.defvjp(low_keep, low_pass)
low_back.defvjp(back_keep, back_low)
EPS = 1e-05
ROPE_BASE = 10000.0
NEG = -1e+30

def layer_normalize(values, gain, bias):
    mean = lax.optimization_barrier(jnp.mean(values, axis=-1, keepdims=True))
    centered = values - mean
    var = lax.optimization_barrier(jnp.mean(centered * centered, axis=-1, keepdims=True))
    return centered * lax.rsqrt(var + EPS) * gain + bias

def rotate(values, cosine, sine):
    width = cosine.shape[-1]
    half = width // 2
    part = values[..., :width]
    turned = jnp.concatenate([-part[..., half:], part[..., :half]], axis=-1)
    return jnp.concatenate([part * cosine + turned * sine, values[..., width:]], axis=-1)

def matmul(left_operand, right_operand):
    return jnp.einsum('xtr,rf->xtf', left_operand, right_operand, precision=lax.Precision.HIGHEST, preferred_element_type=jnp.float32)

def attend(operands):
    query, key, value = operands
    scores = low_back(jnp.einsum('qhd,khd->hqk', query, key, precision=lax.Precision.HIGHEST, preferred_element_type=jnp.float32))
    place = jnp.arange(LENGTH, dtype=jnp.int32)
    allowed = place[None, :] <= place[:, None]
    probs = jax.nn.softmax(jnp.where(allowed[None], scores, NEG), axis=-1)
    return jnp.einsum('hqk,khd->qhd', low(probs), value, precision=lax.Precision.HIGHEST, preferred_element_type=jnp.float32)

def forward(rows, gain_attn, attention_shift, gain_mlp, shift_mlp, mix_weight, mix_bias, proj_weight, proj_bias, expand_weight, expand_bias, reduce_weight, reduce_bias):
    attn_in = low(layer_normalize(rows, gain_attn, attention_shift))
    mlp_in = low(layer_normalize(rows, gain_mlp, shift_mlp))
    mixed = low_back(matmul(attn_in, mix_weight) + mix_bias)
    mixed = mixed.reshape(SEQS, LENGTH, HEADS, 3, HEAD_DIM)
    positions = jnp.arange(LENGTH, dtype=jnp.int32).astype(jnp.float32)
    inverse = 1.0 / ROPE_BASE ** (jnp.arange(0, ROT, 2, dtype=jnp.int32).astype(jnp.float32) / ROT)
    angles = positions[:, None] * inverse[None, :]
    angles = jnp.concatenate([angles, angles], axis=-1)
    cosine = jnp.cos(angles)[:, None, :]
    sine = jnp.sin(angles)[:, None, :]
    query = low(rotate(mixed[:, :, :, 0], cosine, sine) * HEAD_DIM ** (-0.5))
    key = low(rotate(mixed[:, :, :, 1], cosine, sine))
    value = low(mixed[:, :, :, 2])
    heads_out = lax.map(jax.checkpoint(attend), (query, key, value))
    attn_out = low(low_back(heads_out.reshape(SEQS, LENGTH, D)))
    branch_attn = matmul(attn_out, proj_weight) + proj_bias
    expand = low_back(matmul(mlp_in, expand_weight) + expand_bias)
    active_rows = low(jax.nn.gelu(expand, approximate=False))
    branch_mlp = matmul(active_rows, reduce_weight) + reduce_bias
    return rows + branch_attn + branch_mlp

def reference(tokens, cotangent, attn_norm_gain, attn_norm_bias, mlp_norm_gain, mlp_norm_bias, qkv_weight, qkv_bias, dense_weight, dense_bias, fc_in_weight, fc_in_bias, fc_out_weight, fc_out_bias):
    params = (attn_norm_gain.astype(jnp.float32), attn_norm_bias.astype(jnp.float32), mlp_norm_gain.astype(jnp.float32), mlp_norm_bias.astype(jnp.float32), qkv_weight.astype(jnp.float32).reshape(D, 3 * D), qkv_bias.astype(jnp.float32), dense_weight.astype(jnp.float32).reshape(D, D), dense_bias.astype(jnp.float32), fc_in_weight.astype(jnp.float32).reshape(D, FF), fc_in_bias.astype(jnp.float32), fc_out_weight.astype(jnp.float32).reshape(FF, D), fc_out_bias.astype(jnp.float32))
    result, pullback = jax.vjp(forward, tokens.astype(jnp.float32), *params)
    grads = pullback(cotangent.astype(jnp.float32))
    return (result.astype(jnp.bfloat16), grads[0].astype(jnp.bfloat16), grads[1], grads[2], grads[3], grads[4], grads[5].reshape(-1), grads[6], grads[7].reshape(-1), grads[8], grads[9].reshape(-1), grads[10], grads[11].reshape(-1), grads[12])
```

```python
import functools
import types

import jax
import jax.numpy as jnp
import numpy as np
from jax import lax
from jax.experimental import pallas as pl
from jax.experimental.pallas import tpu as pltpu
from jax.sharding import PartitionSpec as P

D = 512
HEADS = 8
FF = 2048


EPS = 1e-05
BOTH = ("seq", "ctx")
ROPE_BASE = 10000.0
NEG = -1e30


def layer_normalize(values, gain, bias):
    mean = jnp.mean(values, axis=-1, keepdims=True)
    centered = values - mean
    var = jnp.mean(centered * centered, axis=-1, keepdims=True)
    return centered * lax.rsqrt(var + EPS) * gain + bias


def rotate(values, cosine, sine):
    width = cosine.shape[-1]
    half = width // 2
    part = values[..., :width]
    turned = jnp.concatenate([-part[..., half:], part[..., :half]], axis=-1)
    return jnp.concatenate([part * cosine + turned * sine, values[..., width:]], axis=-1)


def gelu_exact(values):
    return jax.nn.gelu(values, approximate=False)


def matrices(mix_flat, proj_flat, expand_flat, reduce_flat):
    return (
        mix_flat.reshape(D, 3 * D),
        proj_flat.reshape(D, D),
        expand_flat.reshape(D, FF),
        reduce_flat.reshape(FF, D),
    )


def body(
    tokens,
    cotangent,
    attn_norm_gain,
    attn_norm_bias,
    mlp_norm_gain,
    mlp_norm_bias,
    qkv_weight,
    qkv_bias,
    dense_weight,
    dense_bias,
    fc_in_weight,
    fc_in_bias,
    fc_out_weight,
    fc_out_bias,
):
    (
        gain_attn,
        attention_shift,
        gain_mlp,
        shift_mlp,
        mix_flat,
        mix_bias,
        proj_flat,
        proj_bias,
        expand_flat,
        expand_bias,
        reduce_flat,
        reduce_bias,
    ) = (
        lax.all_gather(attn_norm_gain, BOTH, axis=0, tiled=True),
        lax.all_gather(attn_norm_bias, BOTH, axis=0, tiled=True),
        lax.all_gather(mlp_norm_gain, BOTH, axis=0, tiled=True),
        lax.all_gather(mlp_norm_bias, BOTH, axis=0, tiled=True),
        lax.all_gather(qkv_weight, BOTH, axis=0, tiled=True),
        lax.all_gather(qkv_bias, BOTH, axis=0, tiled=True),
        lax.all_gather(dense_weight, BOTH, axis=0, tiled=True),
        lax.all_gather(dense_bias, BOTH, axis=0, tiled=True),
        lax.all_gather(fc_in_weight, BOTH, axis=0, tiled=True),
        lax.all_gather(fc_in_bias, BOTH, axis=0, tiled=True),
        lax.all_gather(fc_out_weight, BOTH, axis=0, tiled=True),
        lax.all_gather(fc_out_bias, BOTH, axis=0, tiled=True),
    )
    mix_weight, proj_weight, expand_weight, reduce_weight = matrices(
        mix_flat, proj_flat, expand_flat, reduce_flat
    )
    shape = tokens.shape
    group = shape[1]
    width = shape[2]
    heads = HEADS
    head_dim = width // heads
    rows = tokens.reshape(group, width).astype(jnp.float32)
    attn_in, attn_norm_back = jax.vjp(
        layer_normalize, rows, gain_attn.astype(jnp.float32), attention_shift.astype(jnp.float32)
    )
    mlp_in, mlp_norm_back = jax.vjp(
        layer_normalize, rows, gain_mlp.astype(jnp.float32), shift_mlp.astype(jnp.float32)
    )
    attn_low = attn_in.astype(jnp.bfloat16)
    mlp_low = mlp_in.astype(jnp.bfloat16)
    mixed = jnp.dot(attn_low, mix_weight, preferred_element_type=jnp.float32) + mix_bias.astype(
        jnp.float32
    )
    mixed = mixed.reshape(group, heads, 3, head_dim)
    place = lax.axis_index("ctx")
    blocks_total = lax.axis_size("ctx")
    local_pos = jnp.arange(group, dtype=jnp.int32)
    query_pos = place * group + local_pos
    rot_dims = head_dim // 4
    inverse = 1.0 / ROPE_BASE ** (
        jnp.arange(0, rot_dims, 2, dtype=jnp.int32).astype(jnp.float32) / rot_dims
    )
    angles = query_pos.astype(jnp.float32)[:, None] * inverse[None, :]
    angles = jnp.concatenate([angles, angles], axis=-1)
    cosine = jnp.cos(angles)[:, None, :]
    sine = jnp.sin(angles)[:, None, :]
    scale = head_dim ** (-0.5)

    def turn(query_unrotated, key_raw):
        return (rotate(query_unrotated, cosine, sine) * scale, rotate(key_raw, cosine, sine))

    (query_f, key_f), turn_back = jax.vjp(turn, mixed[:, :, 0], mixed[:, :, 1])
    query = query_f.astype(jnp.bfloat16)
    key_own = key_f.astype(jnp.bfloat16).reshape(group, width)
    value_own = mixed[:, :, 2].astype(jnp.bfloat16).reshape(group, width)
    all_keys, all_values = (
        lax.all_gather(key_own, "ctx", axis=0, tiled=True),
        lax.all_gather(value_own, "ctx", axis=0, tiled=True),
    )
    count = place + 1

    def block(index):
        keys = lax.dynamic_slice_in_dim(all_keys, index * group, group, 0).reshape(
            group, heads, head_dim
        )
        values = lax.dynamic_slice_in_dim(all_values, index * group, group, 0).reshape(
            group, heads, head_dim
        )
        scores = jnp.einsum("qhd,khd->hqk", query, keys, preferred_element_type=jnp.float32)
        allowed = (index * group + local_pos)[None, :] <= query_pos[:, None]
        return (keys, values, scores, allowed[None])

    def max_step(index, carry):
        top, total = carry
        _, _, scores, allowed = block(index)
        new_top = jnp.maximum(top, jnp.max(jnp.where(allowed, scores, NEG), axis=-1))
        terms = jnp.where(allowed, jnp.exp(scores - new_top[:, :, None]), 0.0)
        return (new_top, total * jnp.exp(top - new_top) + jnp.sum(terms, axis=-1))

    start = (jnp.full((heads, group), NEG, jnp.float32), jnp.zeros((heads, group), jnp.float32))
    top, total = lax.fori_loop(0, count, max_step, start)
    log_total = top + jnp.log(total)

    def probs_of(scores, allowed):
        return jnp.where(allowed, jnp.exp(scores - log_total[:, :, None]), 0.0)

    def out_step(index, acc):
        _, values, scores, allowed = block(index)
        probs = probs_of(scores, allowed).astype(jnp.bfloat16)
        return acc + jnp.einsum("hqk,khd->qhd", probs, values, preferred_element_type=jnp.float32)

    heads_out = lax.fori_loop(0, count, out_step, jnp.zeros((group, heads, head_dim), jnp.float32))
    attn_out = heads_out.reshape(group, width).astype(jnp.bfloat16)
    branch_attn = jnp.dot(
        attn_out, proj_weight, preferred_element_type=jnp.float32
    ) + proj_bias.astype(jnp.float32)
    expand = jnp.dot(
        mlp_low, expand_weight, preferred_element_type=jnp.float32
    ) + expand_bias.astype(jnp.float32)
    active_rows, active_back = jax.vjp(gelu_exact, expand)
    active_low = active_rows.astype(jnp.bfloat16)
    branch_mlp = jnp.dot(
        active_low, reduce_weight, preferred_element_type=jnp.float32
    ) + reduce_bias.astype(jnp.float32)
    layer_out = (rows + branch_attn + branch_mlp).astype(jnp.bfloat16).reshape(shape)
    back_mix, back_proj, back_expand, back_reduce = (
        lax.all_gather(qkv_weight, BOTH, axis=0, tiled=True),
        lax.all_gather(dense_weight, BOTH, axis=0, tiled=True),
        lax.all_gather(fc_in_weight, BOTH, axis=0, tiled=True),
        lax.all_gather(fc_out_weight, BOTH, axis=0, tiled=True),
    )
    back_mix, back_proj, back_expand, back_reduce = matrices(
        back_mix, back_proj, back_expand, back_reduce
    )
    grad_rows = cotangent.reshape(group, width)
    grad_float = grad_rows.astype(jnp.float32)
    grad_reduce = jnp.einsum("tf,td->fd", active_low, grad_rows, preferred_element_type=jnp.float32)
    grad_out_bias = jnp.sum(grad_float, axis=0)
    grad_proj = jnp.einsum("te,td->ed", attn_out, grad_rows, preferred_element_type=jnp.float32)
    grad_active = jnp.einsum(
        "td,fd->tf", grad_rows, back_reduce, preferred_element_type=jnp.float32
    )
    grad_expand = active_back(grad_active)[0].astype(jnp.bfloat16)
    grad_expand_w = jnp.einsum(
        "td,tf->df", mlp_low, grad_expand, preferred_element_type=jnp.float32
    )
    grad_expand_b = jnp.sum(grad_expand.astype(jnp.float32), axis=0)
    grad_mlp_in = jnp.einsum(
        "tf,df->td", grad_expand, back_expand, preferred_element_type=jnp.float32
    )
    grad_heads = jnp.einsum("td,ed->te", grad_rows, back_proj, preferred_element_type=jnp.float32)
    grad_heads = grad_heads.astype(jnp.bfloat16).reshape(group, heads, head_dim)

    def delta_step(index, acc):
        _, values, scores, allowed = block(index)
        probs = probs_of(scores, allowed)
        grad_probs = jnp.einsum(
            "qhd,khd->hqk", grad_heads, values, preferred_element_type=jnp.float32
        )
        return acc + jnp.sum(probs * grad_probs, axis=-1)

    delta = lax.fori_loop(0, count, delta_step, jnp.zeros((heads, group), jnp.float32))

    def query_step(index, grad_query):
        keys, values, scores, allowed = block(index)
        probs = probs_of(scores, allowed)
        grad_probs = jnp.einsum(
            "qhd,khd->hqk", grad_heads, values, preferred_element_type=jnp.float32
        )
        grad_scores = (probs * (grad_probs - delta[:, :, None])).astype(jnp.bfloat16)
        return grad_query + jnp.einsum(
            "hqk,khd->qhd", grad_scores, keys, preferred_element_type=jnp.float32
        )

    grad_query = lax.fori_loop(
        0, count, query_step, jnp.zeros((group, heads, head_dim), jnp.float32)
    )
    all_queries, all_grad_heads = (
        lax.all_gather(query.reshape(group, width), "ctx", axis=0, tiled=True),
        lax.all_gather(grad_heads.reshape(group, width), "ctx", axis=0, tiled=True),
    )
    gathered_log_sums, all_delta = (
        lax.all_gather(jnp.transpose(log_total), "ctx", axis=0, tiled=True),
        lax.all_gather(jnp.transpose(delta), "ctx", axis=0, tiled=True),
    )
    keys_mine = key_own.reshape(group, heads, head_dim)
    values_mine = value_own.reshape(group, heads, head_dim)

    def owner_step(index, carry):
        key_acc, value_accumulator = carry
        queries = lax.dynamic_slice_in_dim(all_queries, index * group, group, 0).reshape(
            group, heads, head_dim
        )
        outer_grads = lax.dynamic_slice_in_dim(all_grad_heads, index * group, group, 0).reshape(
            group, heads, head_dim
        )
        lse_rows = jnp.transpose(
            lax.dynamic_slice_in_dim(gathered_log_sums, index * group, group, 0)
        )
        delta_rows = jnp.transpose(lax.dynamic_slice_in_dim(all_delta, index * group, group, 0))
        scores = jnp.einsum("qhd,khd->hqk", queries, keys_mine, preferred_element_type=jnp.float32)
        allowed = (query_pos[None, :] <= (index * group + local_pos)[:, None])[None]
        probs = jnp.where(allowed, jnp.exp(scores - lse_rows[:, :, None]), 0.0)
        grad_probs = jnp.einsum(
            "qhd,khd->hqk", outer_grads, values_mine, preferred_element_type=jnp.float32
        )
        grad_scores = (probs * (grad_probs - delta_rows[:, :, None])).astype(jnp.bfloat16)
        key_acc = key_acc + jnp.einsum(
            "hqk,qhd->khd", grad_scores, queries, preferred_element_type=jnp.float32
        )
        value_accumulator = value_accumulator + jnp.einsum(
            "hqk,qhd->khd",
            probs.astype(jnp.bfloat16),
            outer_grads,
            preferred_element_type=jnp.float32,
        )
        return (key_acc, value_accumulator)

    empty_heads = jnp.zeros((group, heads, head_dim), jnp.float32)
    own_key_grad, own_value_grad = lax.fori_loop(
        place, blocks_total, owner_step, (empty_heads, empty_heads)
    )
    grad_query_raw, grad_key_raw = turn_back((grad_query, own_key_grad))
    grad_mixed = jnp.stack([grad_query_raw, grad_key_raw, own_value_grad], axis=2)
    grad_mixed = grad_mixed.reshape(group, 3 * width).astype(jnp.bfloat16)
    grad_mix_w = jnp.einsum("td,te->de", attn_low, grad_mixed, preferred_element_type=jnp.float32)
    grad_mix_b = jnp.sum(grad_mixed.astype(jnp.float32), axis=0)
    grad_attn_in = jnp.einsum("te,de->td", grad_mixed, back_mix, preferred_element_type=jnp.float32)
    input_attn, gain_attn_grad, shift_attn_grad = attn_norm_back(grad_attn_in)
    input_mlp, gain_mlp_grad, shift_mlp_grad = mlp_norm_back(grad_mlp_in)
    grad_tokens = (grad_float + input_attn + input_mlp).astype(jnp.bfloat16).reshape(shape)
    sums = (
        lax.psum_scatter(gain_attn_grad, BOTH, scatter_dimension=0, tiled=True),
        lax.psum_scatter(shift_attn_grad, BOTH, scatter_dimension=0, tiled=True),
        lax.psum_scatter(gain_mlp_grad, BOTH, scatter_dimension=0, tiled=True),
        lax.psum_scatter(shift_mlp_grad, BOTH, scatter_dimension=0, tiled=True),
        lax.psum_scatter(grad_mix_w.reshape(-1), BOTH, scatter_dimension=0, tiled=True),
        lax.psum_scatter(grad_mix_b, BOTH, scatter_dimension=0, tiled=True),
        lax.psum_scatter(grad_proj.reshape(-1), BOTH, scatter_dimension=0, tiled=True),
        lax.psum_scatter(grad_out_bias, BOTH, scatter_dimension=0, tiled=True),
        lax.psum_scatter(
            grad_expand_w.reshape(-1), BOTH, scatter_dimension=0, tiled=True
        ),
        lax.psum_scatter(grad_expand_b, BOTH, scatter_dimension=0, tiled=True),
        lax.psum_scatter(grad_reduce.reshape(-1), BOTH, scatter_dimension=0, tiled=True),
        lax.psum_scatter(grad_out_bias, BOTH, scatter_dimension=0, tiled=True),
    )
    return (
        layer_out,
        grad_tokens,
        sums[0],
        sums[1],
        sums[2],
        sums[3],
        sums[4],
        sums[5],
        sums[6],
        sums[7],
        sums[8],
        sums[9],
        sums[10],
        sums[11],
    )


def general(mesh):
    return jax.shard_map(
        body,
        mesh=mesh,
        in_specs=(
            P("seq", "ctx", None),
            P("seq", "ctx", None),
            P(BOTH),
            P(BOTH),
            P(BOTH),
            P(BOTH),
            P(BOTH),
            P(BOTH),
            P(BOTH),
            P(BOTH),
            P(BOTH),
            P(BOTH),
            P(BOTH),
            P(BOTH),
        ),
        out_specs=(
            P("seq", "ctx", None),
            P("seq", "ctx", None),
            P(BOTH),
            P(BOTH),
            P(BOTH),
            P(BOTH),
            P(BOTH),
            P(BOTH),
            P(BOTH),
            P(BOTH),
            P(BOTH),
            P(BOTH),
            P(BOTH),
            P(BOTH),
        ),
        check_vma=False,
    )


MESH = pl.DeviceIdType.MESH
F32, BF16 = jnp.float32, jnp.bfloat16
HD = D // HEADS
AX = "zycx"
NN = (((1,), (0,)), ((), ()))
NT = (((1,), (1,)), ((), ()))
TN = (((0,), (0,)), ((), ()))
QB = 256


def mm(a, b, dims=NN):
    return lax.dot_general(a, b, dims, preferred_element_type=F32)


def iota(shape, dim):
    return lax.broadcasted_iota(jnp.int32, shape, dim)


def fused(sizes, names, *refs):
    held = dict(zip(names, refs))
    r = types.SimpleNamespace(**held)
    X = sizes["x"]
    C = sizes["c"]
    Y = sizes["y"]
    Z = sizes["z"]
    N = Z * Y * C * X
    T = r.tokens.shape[0]
    S = T * X
    HC = HEADS // X
    HW = HC * HD
    s = lax.axis_index("seq")
    me = {"x": lax.axis_index("ctx"), "c": s % C, "y": (s // C) % Y, "z": s // (C * Y)}
    x = me["x"]
    xo = 1 - x

    def device(at):
        return ((at["z"] * Y + at["y"]) * C + at["c"], at["x"])

    def others(axis):
        n = sizes[axis]
        return [dict(me, **{axis: (me[axis] + d) % n}) for d in range(1, n)]

    flight = {}
    count = [0]

    def push(key, src, dst, at):
        k = count[0]
        count[0] += 1
        cp = pltpu.make_async_remote_copy(
            src_ref=src,
            dst_ref=dst,
            send_sem=r.send.at[k],
            recv_sem=r.recv.at[k],
            device_id=device(at),
            device_id_type=MESH,
        )
        cp.start()
        flight.setdefault(key, []).append(cp)

    def wait(key):
        for cp in flight.pop(key):
            cp.wait()

    def where_at(at, free):
        return tuple(slice(None) if a in free else at[a] for a in AX)

    def gather(name, axis, known):
        ref = held[name]
        part = ref.at[where_at(me, known)]
        for at in others(axis):
            push(name + axis, part, part, at)

    def scatter(name, axis, done):
        ref = held["g" + name]
        free = [a for a in AX if a not in done and a != axis]
        for k, at in enumerate(others(axis)):
            push("g" + name + axis, ref.at[where_at(at, free)], held["r" + name + axis].at[k], at)

    def add_parts(name, axis, done, finish=None):
        wait("g" + name + axis)
        ref, got = held["g" + name], held["r" + name + axis]
        free = [a for a in AX if a not in done and a != axis]
        total = 1
        for a in free:
            total *= sizes[a]

        def one(i, _):
            at, rest = dict(me), i
            for a in reversed(free):
                at[a] = rest % sizes[a]
                rest = rest // sizes[a]
            spot = tuple(at[a] for a in AX)
            inner = tuple(at[a] for a in free)
            acc = ref[spot].astype(F32)
            for k in range(sizes[axis] - 1):
                acc = acc + got[(k,) + inner].astype(F32)
            if finish is None:
                ref[spot] = acc.astype(ref.dtype)
            else:
                finish(acc)
            return 0

        if total == 1:
            one(0, 0)
        else:
            lax.fori_loop(0, total, one, 0)

    barrier = pltpu.get_barrier_semaphore()
    greet = [at for a in AX for at in others(a)]
    for at in greet:
        pl.semaphore_signal(barrier, inc=1, device_id=device(at), device_id_type=MESH)

    tmp = r.tmp
    lane = iota((1, 128), 1)

    def own(name):
        return held[name].at[me["z"], me["y"], me["c"], x]

    tmp[0 : r.fq.shape[0], :] = r.fq[...].astype(F32)
    rows = r.fq.shape[0] * 128 // (3 * D)
    per = 3 * D // 128

    def block64(b, to_high):
        v = tmp[pl.ds(b // 2, rows, stride=per), :]
        return pltpu.roll(v, 64, 1) if (b % 2 == 1) != to_high else v

    for half in range(X):
        for jj in range(3):
            for pair in range(HC // 2):
                h0 = half * HC + 2 * pair
                low = block64(3 * h0 + jj, False)
                high = block64(3 * (h0 + 1) + jj, True)
                at = jj * HW + pair * 128
                r.sq[half, :, at : at + 128] = jnp.where(lane < 64, low, high).astype(BF16)

    def reshard(src, name, width):
        n = held[src].shape[0]
        k = width // 128
        tmp[0:n, :] = held[src][...].astype(F32)
        dst = own(name)
        for j in range(k):
            dst[:, j * 128 : (j + 1) * 128] = tmp[pl.ds(j, n // k, stride=k), :].astype(BF16)

    reshard("fd", "wd", D)
    own("vec")[...] = r.vin[...]
    own("wq")[...] = r.sq[x]

    pl.semaphore_wait(barrier, len(greet))

    at_x = others("x")[0]
    push("wqx", r.sq.at[xo], own("wq"), at_x)
    gather("vec", "x", "")
    gather("wd", "x", "")
    push("tok", r.tokens, r.tok2, at_x)
    reshard("fi", "wi", FF)
    reshard("fo", "wo", D)

    rope = r.rope
    mod = lane % HD

    def rope_rows(i, _):
        ch, sh = rope[0, pl.ds(i, 1), :], rope[1, pl.ds(i, 1), :]
        cl, sl = rope[2], rope[3]
        sine = sh * cl + ch * sl
        at = pl.ds(pl.multiple_of(i * 32, 32), 32)
        r.cos[at, :] = ch * cl - sh * sl
        r.sinl[at, :] = jnp.where(mod < 8, -sine, 0.0)
        r.sinh[at, :] = jnp.where(mod < 8, 0.0, sine)
        return 0

    def turn(u, at, sign):
        return (
            u * r.cos[at, :]
            + sign * (pltpu.roll(u, 120, 1) * r.sinl[at, :] + pltpu.roll(u, 8, 1) * r.sinh[at, :])
        )

    wait("wqx")
    gather("wq", "z", "x")
    gather("wi", "z", "")
    gather("wo", "z", "")
    wait("vecx")
    gather("vec", "y", "x")
    wait("wdx")
    gather("wd", "y", "x")

    lax.fori_loop(0, S // 32, rope_rows, 0)

    RC = 128

    def norm_rows(src, base, keep):
        def one(i, _):
            v = src[pl.ds(pl.multiple_of(i * RC, RC), RC), :].astype(F32)
            c = v - jnp.mean(v, axis=-1, keepdims=True)
            scale = lax.rsqrt(jnp.mean(c * c, axis=-1, keepdims=True) + EPS)
            r.n[pl.ds(pl.multiple_of(base + i * RC, RC), RC), :] = c * scale
            if keep:
                r.scale[pl.ds(pl.multiple_of(i * RC, RC), RC), :] = jnp.broadcast_to(scale, (RC, 128))
            return 0

        lax.fori_loop(0, T // RC, one, 0)

    norm_rows(r.tokens, x * T, True)

    wait("wqz")
    gather("wq", "y", "xz")
    wait("vecy")
    gather("vec", "z", "xy")
    wait("wdy")
    gather("wd", "z", "xy")
    wait("wiz")
    gather("wi", "x", "z")
    wait("vecz")
    gather("vec", "c", "xyz")
    wait("wdz")
    gather("wd", "c", "xyz")
    wait("wqy")
    gather("wq", "c", "xyz")
    wait("woz")
    gather("wo", "x", "z")
    wait("vecc")

    widths = [D // N, D // N, D // N, D // N, 3 * D // N, D // N, FF // N, D // N]

    def column(v, n):
        j = iota((1, n), 1)
        if v != 4:
            return j
        hh = (j % HW) // HD
        return (x * HC + hh) * (3 * HD) + (j // HW) * HD + j % HD

    def lengths(v):
        return 3 * HW if v == 4 else widths[v] * N

    vec2 = r.vec.reshape(N * 8, 128)

    def expand(v):
        n = lengths(v)
        j = column(v, n)
        pick = (iota((128, n), 0) == j % widths[v]).astype(F32).astype(BF16)
        rows_v = vec2[pl.ds(v, N, stride=8), :].astype(BF16)
        spread = mm(rows_v, pick)
        r.vrow[v : v + 1, 0:n] = jnp.sum(
            jnp.where(iota((N, n), 0) == j // widths[v], spread, 0.0), axis=0, keepdims=True
        )

    for v in range(8):
        expand(v)

    def row(v, n=D, off=0):
        return r.vrow[v : v + 1, off : off + n]

    def affine_attn(base):
        def one(i, _):
            at = pl.ds(pl.multiple_of(base + i * RC, RC), RC)
            r.ha[at, :] = (r.n[at, :] * row(0) + row(1)).astype(BF16)
            return 0

        lax.fori_loop(0, T // RC, one, 0)

    affine_attn(x * T)

    def affine_mlp(i, _):
        at = pl.ds(pl.multiple_of(x * T + i * RC, RC), RC)
        to = pl.ds(pl.multiple_of(i * RC, RC), RC)
        r.hm[to, :] = (r.n[at, :] * row(2) + row(3)).astype(BF16)
        return 0

    lax.fori_loop(0, T // RC, affine_mlp, 0)

    wait("wdc")
    wd = r.wd.reshape(D, D)
    for k in range(D // QB):
        r.do1[:, k * QB : (k + 1) * QB] = mm(
            r.cot[...], wd[k * QB : (k + 1) * QB, :], NT
        ).astype(BF16)
    mine = pl.ds(pl.multiple_of(x * HW, HW), HW)
    theirs = pl.ds(pl.multiple_of(xo * HW, HW), HW)
    rows_mine = pl.ds(pl.multiple_of(x * T, T), T)
    rows_theirs = pl.ds(pl.multiple_of(xo * T, T), T)
    push("do", r.do1.at[:, theirs], r.do2.at[rows_mine, :], at_x)
    r.do2[rows_mine, :] = r.do1[:, mine]

    wait("wix")
    gather("wi", "y", "zx")
    wait("wox")
    gather("wo", "y", "zx")

    wait("tok")
    norm_rows(r.tok2, xo * T, False)
    affine_attn(xo * T)

    wait("wqc")
    wq = r.wq.reshape(D, 3 * HW)

    def qkv_rows(i, _):
        at = pl.ds(pl.multiple_of(i * QB, QB), QB)
        h = r.ha[at, :]
        for jj, name in enumerate("qkv"):
            u = mm(h, wq[:, jj * HW : (jj + 1) * HW]) + row(4, HW, jj * HW)
            for b in range(HW // 128):
                w = u[:, b * 128 : (b + 1) * 128]
                if jj < 2:
                    w = turn(w, at, 1.0)
                if jj == 0:
                    w = w * HD**-0.5
                w = w.astype(BF16)
                held[name][at, b * 128 : (b + 1) * 128] = w
                if jj >= 1:
                    held[name + "t"][b * 128 : (b + 1) * 128, at] = w.T
        return 0

    lax.fori_loop(0, S // QB, qkv_rows, 0)

    wait("wiy")
    gather("wi", "c", "zxy")
    wait("do")

    r.dk[...] = jnp.zeros_like(r.dk)
    r.dv[...] = jnp.zeros_like(r.dv)
    causal = iota((QB, QB), 0) <= iota((QB, QB), 1)

    def head(h, _):
        lanes = pl.ds(pl.multiple_of((h // 2) * 128, 128), 128)
        ours = (lane // HD) == h % 2
        head_rows = pl.ds(pl.multiple_of(h * HD, HD), HD)
        for i in range(S // QB):
            here = slice(i * QB, (i + 1) * QB)
            qm = jnp.where(ours, r.q[here, lanes], jnp.zeros((), BF16))
            dom = jnp.where(ours, r.do2[here, lanes], jnp.zeros((), BF16))
            top = None
            for j in range(i + 1):
                st = mm(r.k[j * QB : (j + 1) * QB, lanes], qm, NT)
                if j == i:
                    st = jnp.where(causal, st, NEG)
                r.st[j] = st
                part = jnp.max(st, axis=0, keepdims=True)
                top = part if top is None else jnp.maximum(top, part)
            total = None
            for j in range(i + 1):
                e = jnp.exp(r.st[j] - top)
                r.st[j] = e
                part = jnp.sum(e, axis=0, keepdims=True)
                total = part if total is None else total + part
            scale = 1.0 / total
            delta = None
            for j in range(i + 1):
                p = r.st[j] * scale
                r.st[j] = p
                r.pb[j * QB : (j + 1) * QB, :] = p.astype(BF16)
                dp = mm(r.v[j * QB : (j + 1) * QB, lanes], dom, NT)
                r.dp[j] = dp
                part = jnp.sum(p * dp, axis=0, keepdims=True)
                delta = part if delta is None else delta + part
            for j in range(i + 1):
                ds = r.st[j] * (r.dp[j] - delta)
                r.ds[j * QB : (j + 1) * QB, :] = ds.astype(BF16)
            n = (i + 1) * QB
            pb, ds = r.pb[0:n, :], r.ds[0:n, :]
            r.ot[head_rows, here] = mm(r.vt[head_rows, 0:n], pb).astype(BF16)
            r.dqt[head_rows, here] = mm(r.kt[head_rows, 0:n], ds)
            r.dk[0:n, lanes] += mm(ds, qm)
            r.dv[0:n, lanes] += mm(pb, dom)
        return 0

    lax.fori_loop(0, HC, head, 0)

    push("o", r.ot.at[:, rows_theirs], r.of.at[mine, :], at_x)
    r.of[mine, :] = r.ot[:, rows_mine]
    wait("woy")
    gather("wo", "c", "zxy")

    r.vg[...] = jnp.zeros_like(r.vg)

    def dqkv_rows(i, _):
        at = pl.ds(pl.multiple_of(i * QB, QB), QB)
        for b in range(HW // 128):
            cols = slice(b * 128, (b + 1) * 128)
            dq = r.dqt[cols, at].T
            out = (
                turn(dq, at, -1.0) * HD**-0.5,
                turn(r.dk[at, cols], at, -1.0),
                r.dv[at, cols],
            )
            for jj in range(3):
                w = out[jj].astype(BF16)
                to = slice(jj * HW + b * 128, jj * HW + (b + 1) * 128)
                r.dqkv[at, to] = w
                r.vg[4:5, to] += jnp.sum(w.astype(F32), axis=0, keepdims=True)
        return 0

    lax.fori_loop(0, S // QB, dqkv_rows, 0)

    gq = r.gq.reshape(D, 3 * HW)
    for k in range(D // QB):
        gq[k * QB : (k + 1) * QB, :] = mm(
            r.ha[:, k * QB : (k + 1) * QB], r.dqkv[...], TN
        ).astype(BF16)
    scatter("q", "c", "")

    def dh_rows(base, mine_too):
        def one(i, _):
            at = pl.ds(pl.multiple_of(base + i * QB, QB), QB)
            to = pl.ds(pl.multiple_of(i * QB, QB), QB)
            dh = mm(r.dqkv[at, :], wq[...], NT)
            r.vg[0:1, 0:D] += jnp.sum(dh * r.n[at, :], axis=0, keepdims=True)
            r.vg[1:2, 0:D] += jnp.sum(dh, axis=0, keepdims=True)
            u = dh * row(0)
            if mine_too:
                r.u[to, :] = u
            else:
                r.us[to, :] = u.astype(BF16)
            return 0

        lax.fori_loop(0, T // QB, one, 0)

    dh_rows(xo * T, False)
    push("u", r.us, r.ur, at_x)
    add_parts("q", "c", "")
    scatter("q", "y", "c")
    dh_rows(x * T, True)

    wait("wic")
    wait("woc")
    wi = r.wi.reshape(D, FF)
    wo = r.wo.reshape(FF, D)
    gi = r.gi.reshape(D, FF)
    go = r.go.reshape(FF, D)
    r.hmt[...] = r.hm[...].T
    r.mo[...] = jnp.zeros_like(r.mo)
    r.dm[...] = jnp.zeros_like(r.dm)
    FB = 512

    def ff_block(b, _):
        cols = pl.ds(pl.multiple_of(b * FB, FB), FB)
        f = mm(r.hm[...], wi[:, cols]) + r.vrow[6:7, cols]
        phi = 0.5 + 0.5 * lax.erf(f * (0.5**0.5))
        a = (f * phi).astype(BF16)
        slope = phi + f * (jnp.exp(-0.5 * f * f) * (0.5 / np.pi) ** 0.5)
        df = (mm(r.cot[...], wo[cols, :], NT) * slope).astype(BF16)
        r.vg[6:7, cols] = jnp.sum(df.astype(F32), axis=0, keepdims=True)
        r.mo[...] += mm(a, wo[cols, :])
        r.dm[...] += mm(df, wi[:, cols], NT)
        go[cols, :] = mm(a, r.cot[...], TN).astype(BF16)
        gi[:, cols] = mm(r.hmt[...], df).astype(BF16)
        return 0

    lax.fori_loop(0, FF // FB, ff_block, 0)
    scatter("i", "c", "")
    scatter("o", "c", "")
    add_parts("q", "y", "c")
    scatter("q", "z", "cy")

    wait("o")
    r.gd.reshape(D, D)[...] = mm(r.of[...], r.cot[...]).astype(BF16)
    scatter("d", "c", "")
    g_sum = jnp.sum(r.cot[...].astype(F32), axis=0, keepdims=True)
    r.vg[5:6, 0:D] = g_sum
    r.vg[7:8, 0:D] = g_sum
    own_n = r.n[rows_mine, :]
    r.vg[2:3, 0:D] = jnp.sum(r.dm[...] * own_n, axis=0, keepdims=True)
    r.vg[3:4, 0:D] = jnp.sum(r.dm[...], axis=0, keepdims=True)

    gv2 = r.gv.reshape(N * 8, 128)

    def collapse(v):
        n = lengths(v)
        j = column(v, n)
        pick = (iota((128, n), 0) == j % widths[v]).astype(F32).astype(BF16)
        left = jnp.where(iota((N, n), 0) == j // widths[v], r.vg[v : v + 1, 0:n], 0.0)
        acc = None
        for _ in range(3):
            low = left.astype(BF16)
            part = mm(low, pick, NT)
            acc = part if acc is None else acc + part
            left = left - low.astype(F32)
        gv2[pl.ds(v, N, stride=8), :] = acc

    for v in range(8):
        collapse(v)
    scatter("v", "c", "")

    add_parts("i", "c", "")
    scatter("i", "y", "c")
    add_parts("o", "c", "")
    scatter("o", "y", "c")
    add_parts("d", "c", "")
    scatter("d", "z", "c")
    add_parts("v", "c", "")
    scatter("v", "z", "c")

    r.out[...] = (
        r.tokens[...].astype(F32)
        + mm(r.of[...], wd[...], TN)
        + row(5)
        + (r.mo[...] + row(7))
    ).astype(BF16)

    add_parts("q", "z", "cy")
    wait_q = r.gq.at[me["z"], me["y"], me["c"], xo]
    push("gqx", wait_q, r.rqx, at_x)

    wait("u")

    def final_rows(i, _):
        at = pl.ds(pl.multiple_of(i * RC, RC), RC)
        far = pl.ds(pl.multiple_of(x * T + i * RC, RC), RC)
        u = r.u[at, :] + r.ur[at, :].astype(F32) + r.dm[at, :] * row(2)
        n = r.n[far, :]
        back = u - jnp.mean(u, axis=-1, keepdims=True) - n * jnp.mean(u * n, axis=-1, keepdims=True)
        r.gtok[at, :] = (r.cot[at, :].astype(F32) + back * r.scale[at, 0:1]).astype(BF16)
        return 0

    lax.fori_loop(0, T // RC, final_rows, 0)

    add_parts("i", "y", "c")
    scatter("i", "x", "cy")
    add_parts("o", "y", "c")
    scatter("o", "x", "cy")
    add_parts("d", "z", "c")
    scatter("d", "y", "cz")
    add_parts("v", "z", "c")
    scatter("v", "y", "cz")
    add_parts("d", "y", "cz")
    scatter("d", "x", "czy")
    add_parts("v", "y", "cz")
    scatter("v", "x", "czy")
    add_parts("i", "x", "cy")
    scatter("i", "z", "cyx")
    add_parts("o", "x", "cy")
    scatter("o", "z", "cyx")

    def flat(name, width):
        out = held[name]
        k = width // 128
        n = out.shape[0] // k

        def put(acc):
            for j in range(k):
                out[pl.ds(j, n, stride=k), :] = acc[:, j * 128 : (j + 1) * 128]

        return put

    wait("gqx")
    half_own = r.gq[me["z"], me["y"], me["c"], x].astype(F32)
    half_got = r.rqx[...].astype(F32)
    lo_half = jnp.where(x == 0, half_own, half_got)
    hi_half = jnp.where(x == 0, half_got, half_own)
    halves = (lo_half, hi_half)

    def piece(b, to_high):
        h, jj = b // 3, b % 3
        half, hh = h // HC, h % HC
        at = jj * HW + (hh // 2) * 128
        v = halves[half][:, at : at + 128]
        return pltpu.roll(v, 64, 1) if (hh % 2 == 1) != to_high else v

    for j in range(per):
        both = jnp.where(lane < 64, piece(2 * j, False), piece(2 * j + 1, True))
        r.oq[pl.ds(j, rows, stride=per), :] = both

    def put_vec(acc):
        r.ov[...] = acc

    add_parts("d", "x", "czy", flat("od", D))
    add_parts("v", "x", "czy", put_vec)
    add_parts("i", "z", "cyx", flat("oi", FF))
    add_parts("o", "z", "cyx", flat("oo", D))


def rope_table(length):
    lanes = np.arange(128) % HD
    rot = HD // 4
    inverse = np.where(lanes < rot, 1.0 / ROPE_BASE ** (2.0 * (lanes % (rot // 2)) / rot), 0.0)
    high = 32.0 * np.arange(length // 32)[:, None] * inverse
    low = np.arange(32)[:, None] * inverse
    return np.stack([np.cos(high), np.sin(high), np.cos(low), np.sin(low)]).astype(np.float32)


def layer(sizes, tokens, cotangent, *params):
    Z, Y, C, X = (sizes[a] for a in AX)
    N = Z * Y * C * X
    T = tokens.shape[1]
    S = T * X
    HW = HEADS // X * HD
    vectors = [params[i] for i in (0, 1, 2, 3, 5, 7, 9, 11)]
    weights = [params[i] for i in (4, 6, 8, 10)]
    vin = jnp.stack([jnp.pad(v.astype(F32), (0, 128 - v.shape[0])) for v in vectors])
    flats = [w.reshape(-1, 128) for w in weights]
    full = dict(z=Z, y=Y, c=C, x=X)

    def parts(axis, done, slab, dtype, last=False):
        free = [full[a] for a in AX if a not in done and a != axis]
        return pltpu.VMEM((full[axis] - 1, *free, *slab), dtype)

    slabs = {
        "q": (D // N, 3 * HW),
        "d": (D // N, D),
        "i": (D // N, FF),
        "o": (FF // N, D),
        "v": (8, 128),
    }
    orders = {"q": "cyz", "d": "czyx", "i": "cyxz", "o": "cyxz", "v": "czyx"}
    keep = types.SimpleNamespace()
    scratch = vars(keep)
    for k, slab in slabs.items():
        kind = F32 if k == "v" else BF16
        scratch["vec" if k == "v" else "w" + k] = pltpu.VMEM((Z, Y, C, X, *slab), kind)
        scratch["g" + k] = pltpu.VMEM((Z, Y, C, X, *slab), kind)
        for n, axis in enumerate(orders[k]):
            scratch["r" + k + axis] = parts(axis, orders[k][:n], slab, kind)
    keep.rqx = pltpu.VMEM(slabs["q"], BF16)
    keep.sq = pltpu.VMEM((X, *slabs["q"]), BF16)
    keep.tmp = pltpu.VMEM((max(f.shape[0] for f in flats), 128), F32)
    keep.cos = keep.sinl = keep.sinh = pltpu.VMEM((S, 128), F32)
    keep.tok2 = pltpu.VMEM((T, D), BF16)
    keep.n = pltpu.VMEM((S, D), F32)
    keep.scale = pltpu.VMEM((T, 128), F32)
    keep.vrow = pltpu.VMEM((8, FF), F32)
    keep.vg = pltpu.VMEM((8, FF), F32)
    keep.ha = pltpu.VMEM((S, D), BF16)
    keep.hm = pltpu.VMEM((T, D), BF16)
    keep.hmt = pltpu.VMEM((D, T), BF16)
    keep.do1 = pltpu.VMEM((T, D), BF16)
    keep.q = keep.k = keep.v = keep.do2 = pltpu.VMEM((S, HW), BF16)
    keep.kt = keep.vt = keep.ot = pltpu.VMEM((HW, S), BF16)
    keep.dqt = pltpu.VMEM((HW, S), F32)
    keep.dk = pltpu.VMEM((S, HW), F32)
    keep.dv = pltpu.VMEM((S, HW), F32)
    keep.st = pltpu.VMEM((S // QB, QB, QB), F32)
    keep.dp = pltpu.VMEM((S // QB, QB, QB), F32)
    keep.pb = pltpu.VMEM((S, QB), BF16)
    keep.ds = pltpu.VMEM((S, QB), BF16)
    keep.dqkv = pltpu.VMEM((S, 3 * HW), BF16)
    keep.of = pltpu.VMEM((D, T), BF16)
    keep.u = pltpu.VMEM((T, D), F32)
    keep.us = pltpu.VMEM((T, D), BF16)
    keep.ur = pltpu.VMEM((T, D), BF16)
    keep.mo = pltpu.VMEM((T, D), F32)
    keep.dm = pltpu.VMEM((T, D), F32)
    copies = 4 * (2 * (Z - 1) + 2 * 3) + 2 * (Z + 2) + 16
    keep.send = pltpu.SemaphoreType.DMA((copies,))
    keep.recv = pltpu.SemaphoreType.DMA((copies,))
    ins = "tokens cot fq fd".split() + "fi fo vin rope".split()
    outs = dict(
        out=jax.ShapeDtypeStruct((T, D), BF16),
        gtok=jax.ShapeDtypeStruct((T, D), BF16),
        oq=jax.ShapeDtypeStruct(flats[0].shape, F32),
        od=jax.ShapeDtypeStruct(flats[1].shape, F32),
        oi=jax.ShapeDtypeStruct(flats[2].shape, F32),
        oo=jax.ShapeDtypeStruct(flats[3].shape, F32),
        ov=jax.ShapeDtypeStruct((8, 128), F32),
    )
    vmem = pl.BlockSpec(memory_space=pltpu.VMEM)
    names = ins + list(outs) + list(scratch)
    out, gtok, gq, gd, gi, go, gv = pl.pallas_call(
        functools.partial(fused, sizes, names),
        out_shape=list(outs.values()),
        in_specs=[vmem] * len(ins),
        out_specs=[vmem] * len(outs),
        scratch_shapes=list(scratch.values()),
        compiler_params=pltpu.CompilerParams(
            collective_id=0, has_side_effects=True, vmem_limit_bytes=67043328
        ),
        name="layer",
    )(
        tokens.reshape(T, D),
        cotangent.reshape(T, D),
        *flats,
        vin,
        jnp.asarray(rope_table(S)),
    )
    v = [gv[i, : p.shape[0]] for i, p in enumerate(vectors)]
    return (
        out.reshape(tokens.shape),
        gtok.reshape(tokens.shape),
        v[0],
        v[1],
        v[2],
        v[3],
        gq.reshape(-1),
        v[4],
        gd.reshape(-1),
        v[5],
        gi.reshape(-1),
        v[6],
        go.reshape(-1),
        v[7],
    )


def solution(mesh):
    n_seq, n_ctx = mesh.shape["seq"], mesh.shape["ctx"]
    if n_ctx != 2 or n_seq % 4 or (D // (n_seq * n_ctx)) % 16:
        return general(mesh)
    sizes = {"z": n_seq // 4, "y": 2, "c": 2, "x": n_ctx}
    flat = P(("seq", "ctx"))
    rows = P("seq", "ctx", None)
    return jax.shard_map(
        functools.partial(layer, sizes),
        mesh=mesh,
        in_specs=(rows, rows) + (flat,) * 12,
        out_specs=(rows, rows) + (flat,) * 12,
        check_vma=False,
    )
```

```python
import functools
import types

import jax
import jax.numpy as jnp
import numpy as np
from jax import lax
from jax.experimental import pallas as pl
from jax.experimental.pallas import tpu as pltpu
from jax.sharding import PartitionSpec as P

D = 512
HEADS = 8
FF = 2048


EPS = 1e-05
BOTH = ("seq", "ctx")
ROPE_BASE = 10000.0
NEG = -1e30


def layer_normalize(values, gain, bias):
    mean = jnp.mean(values, axis=-1, keepdims=True)
    centered = values - mean
    var = jnp.mean(centered * centered, axis=-1, keepdims=True)
    return centered * lax.rsqrt(var + EPS) * gain + bias


def rotate(values, cosine, sine):
    width = cosine.shape[-1]
    half = width // 2
    part = values[..., :width]
    turned = jnp.concatenate([-part[..., half:], part[..., :half]], axis=-1)
    return jnp.concatenate([part * cosine + turned * sine, values[..., width:]], axis=-1)


def gelu_exact(values):
    return jax.nn.gelu(values, approximate=False)


def matrices(mix_flat, proj_flat, expand_flat, reduce_flat):
    return (
        mix_flat.reshape(D, 3 * D),
        proj_flat.reshape(D, D),
        expand_flat.reshape(D, FF),
        reduce_flat.reshape(FF, D),
    )


def body(
    tokens,
    cotangent,
    attn_norm_gain,
    attn_norm_bias,
    mlp_norm_gain,
    mlp_norm_bias,
    qkv_weight,
    qkv_bias,
    dense_weight,
    dense_bias,
    fc_in_weight,
    fc_in_bias,
    fc_out_weight,
    fc_out_bias,
):
    (
        gain_attn,
        attention_shift,
        gain_mlp,
        shift_mlp,
        mix_flat,
        mix_bias,
        proj_flat,
        proj_bias,
        expand_flat,
        expand_bias,
        reduce_flat,
        reduce_bias,
    ) = (
        lax.all_gather(attn_norm_gain, BOTH, axis=0, tiled=True),
        lax.all_gather(attn_norm_bias, BOTH, axis=0, tiled=True),
        lax.all_gather(mlp_norm_gain, BOTH, axis=0, tiled=True),
        lax.all_gather(mlp_norm_bias, BOTH, axis=0, tiled=True),
        lax.all_gather(qkv_weight, BOTH, axis=0, tiled=True),
        lax.all_gather(qkv_bias, BOTH, axis=0, tiled=True),
        lax.all_gather(dense_weight, BOTH, axis=0, tiled=True),
        lax.all_gather(dense_bias, BOTH, axis=0, tiled=True),
        lax.all_gather(fc_in_weight, BOTH, axis=0, tiled=True),
        lax.all_gather(fc_in_bias, BOTH, axis=0, tiled=True),
        lax.all_gather(fc_out_weight, BOTH, axis=0, tiled=True),
        lax.all_gather(fc_out_bias, BOTH, axis=0, tiled=True),
    )
    mix_weight, proj_weight, expand_weight, reduce_weight = matrices(
        mix_flat, proj_flat, expand_flat, reduce_flat
    )
    shape = tokens.shape
    group = shape[1]
    width = shape[2]
    heads = HEADS
    head_dim = width // heads
    rows = tokens.reshape(group, width).astype(jnp.float32)
    attn_in, attn_norm_back = jax.vjp(
        layer_normalize, rows, gain_attn.astype(jnp.float32), attention_shift.astype(jnp.float32)
    )
    mlp_in, mlp_norm_back = jax.vjp(
        layer_normalize, rows, gain_mlp.astype(jnp.float32), shift_mlp.astype(jnp.float32)
    )
    attn_low = attn_in.astype(jnp.bfloat16)
    mlp_low = mlp_in.astype(jnp.bfloat16)
    mixed = jnp.dot(attn_low, mix_weight, preferred_element_type=jnp.float32) + mix_bias.astype(
        jnp.float32
    )
    mixed = mixed.reshape(group, heads, 3, head_dim)
    place = lax.axis_index("ctx")
    blocks_total = lax.axis_size("ctx")
    local_pos = jnp.arange(group, dtype=jnp.int32)
    query_pos = place * group + local_pos
    rot_dims = head_dim // 4
    inverse = 1.0 / ROPE_BASE ** (
        jnp.arange(0, rot_dims, 2, dtype=jnp.int32).astype(jnp.float32) / rot_dims
    )
    angles = query_pos.astype(jnp.float32)[:, None] * inverse[None, :]
    angles = jnp.concatenate([angles, angles], axis=-1)
    cosine = jnp.cos(angles)[:, None, :]
    sine = jnp.sin(angles)[:, None, :]
    scale = head_dim ** (-0.5)

    def turn(query_unrotated, key_raw):
        return (rotate(query_unrotated, cosine, sine) * scale, rotate(key_raw, cosine, sine))

    (query_f, key_f), turn_back = jax.vjp(turn, mixed[:, :, 0], mixed[:, :, 1])
    query = query_f.astype(jnp.bfloat16)
    key_own = key_f.astype(jnp.bfloat16).reshape(group, width)
    value_own = mixed[:, :, 2].astype(jnp.bfloat16).reshape(group, width)
    all_keys, all_values = (
        lax.all_gather(key_own, "ctx", axis=0, tiled=True),
        lax.all_gather(value_own, "ctx", axis=0, tiled=True),
    )
    count = place + 1

    def block(index):
        keys = lax.dynamic_slice_in_dim(all_keys, index * group, group, 0).reshape(
            group, heads, head_dim
        )
        values = lax.dynamic_slice_in_dim(all_values, index * group, group, 0).reshape(
            group, heads, head_dim
        )
        scores = jnp.einsum("qhd,khd->hqk", query, keys, preferred_element_type=jnp.float32)
        allowed = (index * group + local_pos)[None, :] <= query_pos[:, None]
        return (keys, values, scores, allowed[None])

    def max_step(index, carry):
        top, total = carry
        _, _, scores, allowed = block(index)
        new_top = jnp.maximum(top, jnp.max(jnp.where(allowed, scores, NEG), axis=-1))
        terms = jnp.where(allowed, jnp.exp(scores - new_top[:, :, None]), 0.0)
        return (new_top, total * jnp.exp(top - new_top) + jnp.sum(terms, axis=-1))

    start = (jnp.full((heads, group), NEG, jnp.float32), jnp.zeros((heads, group), jnp.float32))
    top, total = lax.fori_loop(0, count, max_step, start)
    log_total = top + jnp.log(total)

    def probs_of(scores, allowed):
        return jnp.where(allowed, jnp.exp(scores - log_total[:, :, None]), 0.0)

    def out_step(index, acc):
        _, values, scores, allowed = block(index)
        probs = probs_of(scores, allowed).astype(jnp.bfloat16)
        return acc + jnp.einsum("hqk,khd->qhd", probs, values, preferred_element_type=jnp.float32)

    heads_out = lax.fori_loop(0, count, out_step, jnp.zeros((group, heads, head_dim), jnp.float32))
    attn_out = heads_out.reshape(group, width).astype(jnp.bfloat16)
    branch_attn = jnp.dot(
        attn_out, proj_weight, preferred_element_type=jnp.float32
    ) + proj_bias.astype(jnp.float32)
    expand = jnp.dot(
        mlp_low, expand_weight, preferred_element_type=jnp.float32
    ) + expand_bias.astype(jnp.float32)
    active_rows, active_back = jax.vjp(gelu_exact, expand)
    active_low = active_rows.astype(jnp.bfloat16)
    branch_mlp = jnp.dot(
        active_low, reduce_weight, preferred_element_type=jnp.float32
    ) + reduce_bias.astype(jnp.float32)
    layer_out = (rows + branch_attn + branch_mlp).astype(jnp.bfloat16).reshape(shape)
    back_mix, back_proj, back_expand, back_reduce = (
        lax.all_gather(qkv_weight, BOTH, axis=0, tiled=True),
        lax.all_gather(dense_weight, BOTH, axis=0, tiled=True),
        lax.all_gather(fc_in_weight, BOTH, axis=0, tiled=True),
        lax.all_gather(fc_out_weight, BOTH, axis=0, tiled=True),
    )
    back_mix, back_proj, back_expand, back_reduce = matrices(
        back_mix, back_proj, back_expand, back_reduce
    )
    grad_rows = cotangent.reshape(group, width)
    grad_float = grad_rows.astype(jnp.float32)
    grad_reduce = jnp.einsum("tf,td->fd", active_low, grad_rows, preferred_element_type=jnp.float32)
    grad_out_bias = jnp.sum(grad_float, axis=0)
    grad_proj = jnp.einsum("te,td->ed", attn_out, grad_rows, preferred_element_type=jnp.float32)
    grad_active = jnp.einsum(
        "td,fd->tf", grad_rows, back_reduce, preferred_element_type=jnp.float32
    )
    grad_expand = active_back(grad_active)[0].astype(jnp.bfloat16)
    grad_expand_w = jnp.einsum(
        "td,tf->df", mlp_low, grad_expand, preferred_element_type=jnp.float32
    )
    grad_expand_b = jnp.sum(grad_expand.astype(jnp.float32), axis=0)
    grad_mlp_in = jnp.einsum(
        "tf,df->td", grad_expand, back_expand, preferred_element_type=jnp.float32
    )
    grad_heads = jnp.einsum("td,ed->te", grad_rows, back_proj, preferred_element_type=jnp.float32)
    grad_heads = grad_heads.astype(jnp.bfloat16).reshape(group, heads, head_dim)

    def delta_step(index, acc):
        _, values, scores, allowed = block(index)
        probs = probs_of(scores, allowed)
        grad_probs = jnp.einsum(
            "qhd,khd->hqk", grad_heads, values, preferred_element_type=jnp.float32
        )
        return acc + jnp.sum(probs * grad_probs, axis=-1)

    delta = lax.fori_loop(0, count, delta_step, jnp.zeros((heads, group), jnp.float32))

    def query_step(index, grad_query):
        keys, values, scores, allowed = block(index)
        probs = probs_of(scores, allowed)
        grad_probs = jnp.einsum(
            "qhd,khd->hqk", grad_heads, values, preferred_element_type=jnp.float32
        )
        grad_scores = (probs * (grad_probs - delta[:, :, None])).astype(jnp.bfloat16)
        return grad_query + jnp.einsum(
            "hqk,khd->qhd", grad_scores, keys, preferred_element_type=jnp.float32
        )

    grad_query = lax.fori_loop(
        0, count, query_step, jnp.zeros((group, heads, head_dim), jnp.float32)
    )
    all_queries, all_grad_heads = (
        lax.all_gather(query.reshape(group, width), "ctx", axis=0, tiled=True),
        lax.all_gather(grad_heads.reshape(group, width), "ctx", axis=0, tiled=True),
    )
    gathered_log_sums, all_delta = (
        lax.all_gather(jnp.transpose(log_total), "ctx", axis=0, tiled=True),
        lax.all_gather(jnp.transpose(delta), "ctx", axis=0, tiled=True),
    )
    keys_mine = key_own.reshape(group, heads, head_dim)
    values_mine = value_own.reshape(group, heads, head_dim)

    def owner_step(index, carry):
        key_acc, value_accumulator = carry
        queries = lax.dynamic_slice_in_dim(all_queries, index * group, group, 0).reshape(
            group, heads, head_dim
        )
        outer_grads = lax.dynamic_slice_in_dim(all_grad_heads, index * group, group, 0).reshape(
            group, heads, head_dim
        )
        lse_rows = jnp.transpose(
            lax.dynamic_slice_in_dim(gathered_log_sums, index * group, group, 0)
        )
        delta_rows = jnp.transpose(lax.dynamic_slice_in_dim(all_delta, index * group, group, 0))
        scores = jnp.einsum("qhd,khd->hqk", queries, keys_mine, preferred_element_type=jnp.float32)
        allowed = (query_pos[None, :] <= (index * group + local_pos)[:, None])[None]
        probs = jnp.where(allowed, jnp.exp(scores - lse_rows[:, :, None]), 0.0)
        grad_probs = jnp.einsum(
            "qhd,khd->hqk", outer_grads, values_mine, preferred_element_type=jnp.float32
        )
        grad_scores = (probs * (grad_probs - delta_rows[:, :, None])).astype(jnp.bfloat16)
        key_acc = key_acc + jnp.einsum(
            "hqk,qhd->khd", grad_scores, queries, preferred_element_type=jnp.float32
        )
        value_accumulator = value_accumulator + jnp.einsum(
            "hqk,qhd->khd",
            probs.astype(jnp.bfloat16),
            outer_grads,
            preferred_element_type=jnp.float32,
        )
        return (key_acc, value_accumulator)

    empty_heads = jnp.zeros((group, heads, head_dim), jnp.float32)
    own_key_grad, own_value_grad = lax.fori_loop(
        place, blocks_total, owner_step, (empty_heads, empty_heads)
    )
    grad_query_raw, grad_key_raw = turn_back((grad_query, own_key_grad))
    grad_mixed = jnp.stack([grad_query_raw, grad_key_raw, own_value_grad], axis=2)
    grad_mixed = grad_mixed.reshape(group, 3 * width).astype(jnp.bfloat16)
    grad_mix_w = jnp.einsum("td,te->de", attn_low, grad_mixed, preferred_element_type=jnp.float32)
    grad_mix_b = jnp.sum(grad_mixed.astype(jnp.float32), axis=0)
    grad_attn_in = jnp.einsum("te,de->td", grad_mixed, back_mix, preferred_element_type=jnp.float32)
    input_attn, gain_attn_grad, shift_attn_grad = attn_norm_back(grad_attn_in)
    input_mlp, gain_mlp_grad, shift_mlp_grad = mlp_norm_back(grad_mlp_in)
    grad_tokens = (grad_float + input_attn + input_mlp).astype(jnp.bfloat16).reshape(shape)
    sums = (
        lax.psum_scatter(gain_attn_grad, BOTH, scatter_dimension=0, tiled=True),
        lax.psum_scatter(shift_attn_grad, BOTH, scatter_dimension=0, tiled=True),
        lax.psum_scatter(gain_mlp_grad, BOTH, scatter_dimension=0, tiled=True),
        lax.psum_scatter(shift_mlp_grad, BOTH, scatter_dimension=0, tiled=True),
        lax.psum_scatter(grad_mix_w.reshape(-1), BOTH, scatter_dimension=0, tiled=True),
        lax.psum_scatter(grad_mix_b, BOTH, scatter_dimension=0, tiled=True),
        lax.psum_scatter(grad_proj.reshape(-1), BOTH, scatter_dimension=0, tiled=True),
        lax.psum_scatter(grad_out_bias, BOTH, scatter_dimension=0, tiled=True),
        lax.psum_scatter(
            grad_expand_w.reshape(-1), BOTH, scatter_dimension=0, tiled=True
        ),
        lax.psum_scatter(grad_expand_b, BOTH, scatter_dimension=0, tiled=True),
        lax.psum_scatter(grad_reduce.reshape(-1), BOTH, scatter_dimension=0, tiled=True),
        lax.psum_scatter(grad_out_bias, BOTH, scatter_dimension=0, tiled=True),
    )
    return (
        layer_out,
        grad_tokens,
        sums[0],
        sums[1],
        sums[2],
        sums[3],
        sums[4],
        sums[5],
        sums[6],
        sums[7],
        sums[8],
        sums[9],
        sums[10],
        sums[11],
    )


def general(mesh):
    return jax.shard_map(
        body,
        mesh=mesh,
        in_specs=(
            P("seq", "ctx", None),
            P("seq", "ctx", None),
            P(BOTH),
            P(BOTH),
            P(BOTH),
            P(BOTH),
            P(BOTH),
            P(BOTH),
            P(BOTH),
            P(BOTH),
            P(BOTH),
            P(BOTH),
            P(BOTH),
            P(BOTH),
        ),
        out_specs=(
            P("seq", "ctx", None),
            P("seq", "ctx", None),
            P(BOTH),
            P(BOTH),
            P(BOTH),
            P(BOTH),
            P(BOTH),
            P(BOTH),
            P(BOTH),
            P(BOTH),
            P(BOTH),
            P(BOTH),
            P(BOTH),
            P(BOTH),
        ),
        check_vma=False,
    )


MESH = pl.DeviceIdType.MESH
F32, BF16 = jnp.float32, jnp.bfloat16
HD = D // HEADS
AX = "zycx"
NN = (((1,), (0,)), ((), ()))
NT = (((1,), (1,)), ((), ()))
TN = (((0,), (0,)), ((), ()))
QB = 256


def mm(a, b, dims=NN):
    return lax.dot_general(a, b, dims, preferred_element_type=F32)


def iota(shape, dim):
    return lax.broadcasted_iota(jnp.int32, shape, dim)


def fused(sizes, names, *refs):
    held = dict(zip(names, refs))
    r = types.SimpleNamespace(**held)
    X = sizes["x"]
    C = sizes["c"]
    Y = sizes["y"]
    Z = sizes["z"]
    N = Z * Y * C * X
    T = r.tokens.shape[0]
    S = T * X
    HC = HEADS // X
    HW = HC * HD
    FH = FF // X
    CH = dict(q=384, i=FH // 2, o=D // 2)
    s = lax.axis_index("seq")
    me = {"x": lax.axis_index("ctx"), "c": s % C, "y": (s // C) % Y, "z": s // (C * Y)}
    x = me["x"]
    xo = 1 - x

    def device(at):
        return ((at["z"] * Y + at["y"]) * C + at["c"], at["x"])

    def others(axis):
        n = sizes[axis]
        return [dict(me, **{axis: (me[axis] + d) % n}) for d in range(1, n)]

    flight = {}
    count = [0]

    def push(key, src, dst, at):
        k = count[0]
        count[0] += 1
        cp = pltpu.make_async_remote_copy(
            src_ref=src,
            dst_ref=dst,
            send_sem=r.send.at[k],
            recv_sem=r.recv.at[k],
            device_id=device(at),
            device_id_type=MESH,
        )
        cp.start()
        flight.setdefault(key, []).append(cp)

    def wait(key):
        for cp in flight.pop(key):
            cp.wait()

    def axes(name):
        return AX[: 3 if name == "o" else 4]

    def chunk(name, k):
        if k is None:
            return slice(None)
        w = CH[name]
        return slice(k * w, (k + 1) * w)

    def gather(name, axis, known, k=None):
        ref = held["w" + name]
        spot = tuple(slice(None) if a in known else me[a] for a in axes(name))
        part = ref.at[spot + (slice(None), chunk(name, k))]
        for at in others(axis):
            push(("w", name, axis, k), part, part, at)

    def relay(name, axis, nxt, known, k=None):
        wait(("w", name, axis, k))
        gather(name, nxt, known + axis, k)

    def arrived(name, k=None):
        wait(("w", name, "c", k))

    def scatter(name, axis, done, k=None):
        ref, got = held["g" + name], held["r" + name + axis]
        free = [a for a in axes(name) if a not in done and a != axis]
        cols = (slice(None), chunk(name, k))
        for n, at in enumerate(others(axis)):
            spot = tuple(slice(None) if a in free else at[a] for a in axes(name))
            to = (n,) + (slice(None),) * len(free)
            push(("g", name, axis, k), ref.at[spot + cols], got.at[to + cols], at)

    def add_parts(name, axis, done, k=None, finish=None):
        wait(("g", name, axis, k))
        ref, got = held["g" + name], held["r" + name + axis]
        free = [a for a in axes(name) if a not in done and a != axis]
        cols = (slice(None), chunk(name, k))
        total = 1
        for a in free:
            total *= sizes[a]

        def one(i, _):
            at, rest = dict(me), i
            for a in reversed(free):
                at[a] = rest % sizes[a]
                rest = rest // sizes[a]
            spot = tuple(at[a] for a in axes(name))
            inner = tuple(at[a] for a in free)
            acc = ref[spot + cols].astype(F32)
            for n in range(sizes[axis] - 1):
                acc = acc + got[(n,) + inner + cols].astype(F32)
            if finish is None:
                ref[spot + cols] = acc.astype(ref.dtype)
            else:
                finish(acc)
            return 0

        if total == 1:
            one(0, 0)
        else:
            lax.fori_loop(0, total, one, 0)

    def step(name, axis, nxt, done="", k=None):
        add_parts(name, axis, done, k)
        scatter(name, nxt, done + axis, k)

    barrier = pltpu.get_barrier_semaphore()
    greet = [at for a in AX for at in others(a)]
    for at in greet:
        pl.semaphore_signal(barrier, inc=1, device_id=device(at), device_id_type=MESH)

    tmp = r.tmp
    lane = iota((1, 128), 1)

    def own(name):
        return held[name].at[me["z"], me["y"], me["c"], x]

    def block64(b, per, rows, to_high):
        v = tmp[pl.ds(b // 2, rows, stride=per), :]
        return pltpu.roll(v, 64, 1) if (b % 2 == 1) != to_high else v

    def split(src, dst, width, table):
        n = held[src].shape[0]
        per = width // 128
        tmp[0:n, :] = held[src][...].astype(F32)
        for half in range(X):
            for m in range(per // X):
                low, high = table(half, m)
                low = block64(low, per, n // per, False)
                high = block64(high, per, n // per, True)
                dst[half, :, m * 128 : (m + 1) * 128] = jnp.where(lane < 64, low, high).astype(BF16)

    def table_q(half, m):
        h0 = half * HC + 2 * (m // 3)
        return 3 * h0 + m % 3, 3 * (h0 + 1) + m % 3

    def table_i(half, m):
        return 4 * m + half, 4 * m + 2 + half

    def reshard(src, dst, width):
        n = held[src].shape[0]
        k = width // 128
        tmp[0:n, :] = held[src][...].astype(F32)
        for j in range(k):
            dst[:, j * 128 : (j + 1) * 128] = tmp[pl.ds(j, n // k, stride=k), :].astype(BF16)

    split("fq", r.sq, 3 * D, table_q)
    split("fi", r.si, FF, table_i)
    reshard("fd", own("wd"), D)
    own("wv")[...] = r.vin[...]
    own("wq")[...] = r.sq[x]
    own("wi")[...] = r.si[x]

    pl.semaphore_wait(barrier, len(greet))

    rows_mine = pl.ds(pl.multiple_of(x * T, T), T)
    rows_theirs = pl.ds(pl.multiple_of(xo * T, T), T)
    at_x = others("x")[0]
    gather("v", "x", "")
    push("sq", r.sq.at[xo], own("wq"), at_x)
    push("si", r.si.at[xo], own("wi"), at_x)
    gather("d", "x", "")
    push("tok", r.tokens, r.tok2, at_x)
    push("cot", r.cot, r.cots.at[rows_mine, :], at_x)
    reshard("fo", r.wo.at[me["z"], me["y"], me["c"]], D)

    rope = r.rope
    mod = lane % HD

    def rope_rows(i, _):
        ch, sh = rope[0, pl.ds(i, 1), :], rope[1, pl.ds(i, 1), :]
        cl, sl = rope[2], rope[3]
        sine = sh * cl + ch * sl
        at = pl.ds(pl.multiple_of(i * 32, 32), 32)
        r.cos[at, :] = ch * cl - sh * sl
        r.sinl[at, :] = jnp.where(mod < 8, -sine, 0.0)
        r.sinh[at, :] = jnp.where(mod < 8, 0.0, sine)
        return 0

    def turn(u, at, sign):
        return (
            u * r.cos[at, :]
            + sign * (pltpu.roll(u, 120, 1) * r.sinl[at, :] + pltpu.roll(u, 8, 1) * r.sinh[at, :])
        )

    relay("v", "x", "z", "")
    wait("sq")
    gather("q", "z", "x")
    wait("si")
    gather("i", "z", "x", 0)
    gather("i", "z", "x", 1)
    relay("d", "x", "z", "")
    gather("o", "z", "", 0)
    gather("o", "z", "", 1)
    r.cots[rows_mine, :] = r.cot[...]
    lax.fori_loop(0, S // 32, rope_rows, 0)

    RC = 128

    def norm_rows(src, base, keep):
        def one(i, _):
            v = src[pl.ds(pl.multiple_of(i * RC, RC), RC), :].astype(F32)
            c = v - jnp.mean(v, axis=-1, keepdims=True)
            scale = lax.rsqrt(jnp.mean(c * c, axis=-1, keepdims=True) + EPS)
            r.n[pl.ds(pl.multiple_of(base + i * RC, RC), RC), :] = c * scale
            if keep:
                r.scale[pl.ds(pl.multiple_of(i * RC, RC), RC), :] = jnp.broadcast_to(scale, (RC, 128))
            return 0

        lax.fori_loop(0, T // RC, one, 0)

    norm_rows(r.tokens, x * T, True)

    relay("v", "z", "y", "x")
    relay("v", "y", "c", "xz")
    relay("q", "z", "y", "x")
    arrived("v")

    widths = [D // N, D // N, D // N, D // N, 3 * D // N, D // N, FF // N, D // N]

    def column(v, n):
        j = iota((1, n), 1)
        if v == 4:
            head_at = x * HC + 2 * (j // 384) + (j % 128) // HD
            return head_at * (3 * HD) + ((j % 384) // 128) * HD + j % HD
        if v == 6:
            return (j // 64) * 128 + x * 64 + j % 64
        return j

    def lengths(v):
        return {4: 3 * HW, 6: FH}.get(v, D)

    vec2 = r.wv.reshape(N * 8, 128)

    def expand(v):
        n = lengths(v)
        j = column(v, n)
        pick = (iota((128, n), 0) == j % widths[v]).astype(F32).astype(BF16)
        rows_v = vec2[pl.ds(v, N, stride=8), :].astype(BF16)
        spread = mm(rows_v, pick)
        r.vrow[v : v + 1, 0:n] = jnp.sum(
            jnp.where(iota((N, n), 0) == j // widths[v], spread, 0.0), axis=0, keepdims=True
        )

    for v in range(8):
        expand(v)

    def row(v, n=D, off=0):
        return r.vrow[v : v + 1, off : off + n]

    def affine_attn(base):
        def one(i, _):
            at = pl.ds(pl.multiple_of(base + i * RC, RC), RC)
            r.ha[at, :] = (r.n[at, :] * row(0) + row(1)).astype(BF16)
            return 0

        lax.fori_loop(0, T // RC, one, 0)

    def affine_mlp(base):
        def one(i, _):
            at = pl.ds(pl.multiple_of(base + i * RC, RC), RC)
            r.hm[at, :] = (r.n[at, :] * row(2) + row(3)).astype(BF16)
            return 0

        lax.fori_loop(0, T // RC, one, 0)

    affine_attn(x * T)
    affine_mlp(x * T)
    relay("i", "z", "y", "x", 0)

    wait("tok")
    norm_rows(r.tok2, xo * T, False)
    affine_attn(xo * T)
    affine_mlp(xo * T)
    relay("i", "z", "y", "x", 1)
    relay("q", "y", "c", "xz")
    r.hmt[...] = r.hm[...].T
    relay("d", "z", "y", "x")

    arrived("q")
    wq = r.wq.reshape(D, 3 * HW)

    def qkv_rows(i, _):
        at = pl.ds(pl.multiple_of(i * QB, QB), QB)
        h = r.ha[at, :]
        u = mm(h, wq[...]) + row(4, 3 * HW)
        for b in range(HW // 128):
            for jj, name in enumerate("qkv"):
                w = u[:, b * 384 + jj * 128 : b * 384 + (jj + 1) * 128]
                if jj < 2:
                    w = turn(w, at, 1.0)
                if jj == 0:
                    w = w * HD**-0.5
                w = w.astype(BF16)
                held[name][at, b * 128 : (b + 1) * 128] = w
                if jj >= 1:
                    held[name + "t"][b * 128 : (b + 1) * 128, at] = w.T
        return 0

    lax.fori_loop(0, S // QB, qkv_rows, 0)

    wi = r.wi.reshape(D, FH)
    wo = r.wo.reshape(FH, D)
    gi = r.gi.reshape(D, FH)
    go = r.go.reshape(FH, D)
    FB = 256

    def ff_cols(b):
        return pl.ds(pl.multiple_of(b * FB, FB), FB)

    def ff_forward(b, _):
        cols = ff_cols(b)
        f = mm(r.hm[...], wi[:, cols]) + r.vrow[6:7, cols]
        phi = 0.5 + 0.5 * lax.erf(f * (0.5**0.5))
        r.act[:, cols] = (f * phi).astype(BF16)
        r.slope[:, cols] = phi + f * (jnp.exp(-0.5 * f * f) * (0.5 / np.pi) ** 0.5)
        return 0

    relay("i", "y", "c", "xz", 0)
    relay("o", "z", "y", "", 0)
    arrived("i", 0)
    lax.fori_loop(0, FH // FB // 2, ff_forward, 0)
    relay("i", "y", "c", "xz", 1)
    relay("o", "z", "y", "", 1)
    arrived("i", 1)
    lax.fori_loop(FH // FB // 2, FH // FB, ff_forward, 0)
    relay("d", "y", "c", "xz")
    arrived("d")

    wait("cot")
    wd = r.wd.reshape(D, D)
    mine = pl.ds(pl.multiple_of(x * HW, HW), HW)
    r.do2[...] = mm(r.cots[...], wd[mine, :], NT).astype(BF16)

    def out_grad(k):
        cols = chunk("o", k)

        def one(b, _):
            at = ff_cols(b)
            go[at, cols] = mm(r.act[:, at], r.cots[:, cols], TN).astype(BF16)
            return 0

        lax.fori_loop(0, FH // FB, one, 0)
        scatter("o", "c", "", k)

    out_grad(0)
    out_grad(1)
    relay("o", "y", "c", "z", 0)

    r.dk[...] = jnp.zeros_like(r.dk)
    r.dv[...] = jnp.zeros_like(r.dv)
    causal = iota((QB, QB), 0) <= iota((QB, QB), 1)

    def head(h, _):
        lanes = pl.ds(pl.multiple_of((h // 2) * 128, 128), 128)
        ours = (lane // HD) == h % 2
        head_rows = pl.ds(pl.multiple_of(h * HD, HD), HD)
        for i in range(S // QB):
            here = slice(i * QB, (i + 1) * QB)
            qm = jnp.where(ours, r.q[here, lanes], jnp.zeros((), BF16))
            dom = jnp.where(ours, r.do2[here, lanes], jnp.zeros((), BF16))
            top = None
            for j in range(i + 1):
                st = mm(r.k[j * QB : (j + 1) * QB, lanes], qm, NT)
                if j == i:
                    st = jnp.where(causal, st, NEG)
                r.st[j] = st
                part = jnp.max(st, axis=0, keepdims=True)
                top = part if top is None else jnp.maximum(top, part)
            total = None
            for j in range(i + 1):
                e = jnp.exp(r.st[j] - top)
                r.st[j] = e
                part = jnp.sum(e, axis=0, keepdims=True)
                total = part if total is None else total + part
            scale = 1.0 / total
            delta = None
            for j in range(i + 1):
                p = r.st[j] * scale
                r.st[j] = p
                r.pb[j * QB : (j + 1) * QB, :] = p.astype(BF16)
                dp = mm(r.v[j * QB : (j + 1) * QB, lanes], dom, NT)
                r.dp[j] = dp
                part = jnp.sum(p * dp, axis=0, keepdims=True)
                delta = part if delta is None else delta + part
            for j in range(i + 1):
                ds = r.st[j] * (r.dp[j] - delta)
                r.ds[j * QB : (j + 1) * QB, :] = ds.astype(BF16)
            n = (i + 1) * QB
            pb, ds = r.pb[0:n, :], r.ds[0:n, :]
            r.ot[head_rows, here] = mm(r.vt[head_rows, 0:n], pb).astype(BF16)
            r.dqt[head_rows, here] = mm(r.kt[head_rows, 0:n], ds)
            r.dk[0:n, lanes] += mm(ds, qm)
            r.dv[0:n, lanes] += mm(pb, dom)
        return 0

    def send_o(b):
        own_rows = slice(b * 128, (b + 1) * 128)
        to = pl.ds(pl.multiple_of(x * HW + b * 128, 128), 128)
        push(("o", b), r.ot.at[own_rows, rows_theirs], r.of.at[to, :], at_x)
        r.of[to, :] = r.ot[own_rows, rows_mine]

    r.vg[...] = jnp.zeros_like(r.vg)
    gq = r.gq.reshape(D, 3 * HW)

    def qkv_back(b):
        def one(i, _):
            at = pl.ds(pl.multiple_of(i * QB, QB), QB)
            cols = slice(b * 128, (b + 1) * 128)
            dq = r.dqt[cols, at].T
            out = (
                turn(dq, at, -1.0) * HD**-0.5,
                turn(r.dk[at, cols], at, -1.0),
                r.dv[at, cols],
            )
            for jj in range(3):
                w = out[jj].astype(BF16)
                to = slice(b * 384 + jj * 128, b * 384 + (jj + 1) * 128)
                r.dqkv[at, to] = w
                r.vg[4:5, to] += jnp.sum(w.astype(F32), axis=0, keepdims=True)
            return 0

        lax.fori_loop(0, S // QB, one, 0)
        cols = chunk("q", b)
        for k in range(D // QB):
            gq[k * QB : (k + 1) * QB, cols] = mm(
                r.ha[:, k * QB : (k + 1) * QB], r.dqkv[:, cols], TN
            ).astype(BF16)
        scatter("q", "c", "", b)

    lax.fori_loop(0, 1, head, 0)
    relay("o", "y", "c", "z", 1)
    step("o", "c", "y", "", 0)
    step("o", "c", "y", "", 1)
    lax.fori_loop(1, 2, head, 0)
    send_o(0)
    qkv_back(0)
    step("o", "y", "z", "c", 0)

    arrived("o", 0)
    arrived("o", 1)
    r.mos[...] = mm(r.act[rows_theirs, :], wo[...]).astype(BF16)
    push("mo", r.mos, r.mor, at_x)
    step("o", "y", "z", "c", 1)

    def ff_backward(b, _):
        cols = ff_cols(b)
        df = (mm(r.cots[...], wo[cols, :], NT) * r.slope[:, cols]).astype(BF16)
        r.vg[6:7, cols] = jnp.sum(df.astype(F32), axis=0, keepdims=True)
        r.df[:, cols] = df
        gi[:, cols] = mm(r.hmt[...], df).astype(BF16)
        return 0

    lax.fori_loop(0, FH // FB // 2, ff_backward, 0)
    scatter("i", "c", "", 0)
    step("q", "c", "y", "", 0)
    lax.fori_loop(FH // FB // 2, FH // FB, ff_backward, 0)
    scatter("i", "c", "", 1)
    r.mo[...] = mm(r.act[rows_mine, :], wo[...])
    step("i", "c", "y", "", 0)

    def dm_rows(i, _):
        at = pl.ds(pl.multiple_of(i * QB, QB), QB)
        dm = mm(r.df[at, :], wi[...], NT)
        r.vg[2:3, 0:D] += jnp.sum(dm * r.n[at, :], axis=0, keepdims=True)
        r.vg[3:4, 0:D] += jnp.sum(dm, axis=0, keepdims=True)
        r.um[at, :] = dm * row(2)
        return 0

    lax.fori_loop(0, S // QB, dm_rows, 0)
    step("i", "c", "y", "", 1)
    step("q", "y", "z", "c", 0)

    lax.fori_loop(2, 3, head, 0)
    step("i", "y", "z", "c", 0)
    step("i", "y", "z", "c", 1)
    lax.fori_loop(3, 4, head, 0)
    send_o(1)
    half_z = pl.ds(x * (Z // X), Z // X)
    r.gd.reshape(D, D)[mine, :] = mm(r.ot[...], r.cots[...]).astype(BF16)
    gd_part = r.gd.at[half_z, :, :, xo]
    push("gd", gd_part, gd_part, at_x)
    qkv_back(1)

    def dh_rows(base, mine_too):
        def one(i, _):
            at = pl.ds(pl.multiple_of(base + i * QB, QB), QB)
            to = pl.ds(pl.multiple_of(i * QB, QB), QB)
            dh = mm(r.dqkv[at, :], wq[...], NT)
            r.vg[0:1, 0:D] += jnp.sum(dh * r.n[at, :], axis=0, keepdims=True)
            r.vg[1:2, 0:D] += jnp.sum(dh, axis=0, keepdims=True)
            u = dh * row(0) + r.um[at, :]
            if mine_too:
                r.u[to, :] = u
            else:
                r.us[to, :] = u.astype(BF16)
            return 0

        lax.fori_loop(0, T // QB, one, 0)

    dh_rows(xo * T, False)
    push("u", r.us, r.ur, at_x)
    step("q", "c", "y", "", 1)
    dh_rows(x * T, True)

    g_sum = jnp.sum(r.cot[...].astype(F32), axis=0, keepdims=True)
    r.vg[5:6, 0:D] = g_sum
    r.vg[7:8, 0:D] = g_sum
    gv2 = r.gv.reshape(N * 8, 128)

    def collapse(v):
        n = lengths(v)
        j = column(v, n)
        pick = (iota((128, n), 0) == j % widths[v]).astype(F32).astype(BF16)
        left = jnp.where(iota((N, n), 0) == j // widths[v], r.vg[v : v + 1, 0:n], 0.0)
        acc = None
        for _ in range(3):
            low = left.astype(BF16)
            part = mm(low, pick, NT)
            acc = part if acc is None else acc + part
            left = left - low.astype(F32)
        gv2[pl.ds(v, N, stride=8), :] = acc

    for v in range(8):
        collapse(v)
    scatter("v", "c", "")
    wait("gd")
    scatter("d", "c", "x")
    step("q", "y", "z", "c", 1)

    def flat(out, width, k=None, part=D):
        per = width // 128
        n = out.shape[0] // per
        lo = 0 if k is None else k * (part // 128)

        def put(acc):
            for j in range(acc.shape[1] // 128):
                out[pl.ds(lo + j, n, stride=per), :] = acc[:, j * 128 : (j + 1) * 128]

        return put

    add_parts("o", "z", "cy", 0, flat(r.oo, D, 0, CH["o"]))
    add_parts("o", "z", "cy", 1, flat(r.oo, D, 1, CH["o"]))
    add_parts("q", "z", "cy", 0)
    add_parts("i", "z", "cy", 0)
    add_parts("i", "z", "cy", 1)
    at_me = (me["z"], me["y"], me["c"])
    push("si", r.gi.at[at_me + (xo,)], r.xi, at_x)
    step("v", "c", "y")
    step("d", "c", "y", "x")

    wait(("o", 0))
    wait(("o", 1))
    wait("mo")
    r.out[...] = (
        r.tokens[...].astype(F32)
        + mm(r.of[...], wd[...], TN)
        + row(5)
        + (r.mo[...] + r.mor[...].astype(F32) + row(7))
    ).astype(BF16)
    step("v", "y", "z", "c")
    step("d", "y", "z", "cx")
    add_parts("q", "z", "cy", 1)
    push("sq", r.gq.at[at_me + (xo,)], r.xq, at_x)
    step("v", "z", "x", "cy")
    add_parts("d", "z", "cyx", None, flat(r.od, D))

    wait("u")

    def final_rows(i, _):
        at = pl.ds(pl.multiple_of(i * RC, RC), RC)
        far = pl.ds(pl.multiple_of(x * T + i * RC, RC), RC)
        u = r.u[at, :] + r.ur[at, :].astype(F32)
        n = r.n[far, :]
        back = u - jnp.mean(u, axis=-1, keepdims=True) - n * jnp.mean(u * n, axis=-1, keepdims=True)
        r.gtok[at, :] = (r.cot[at, :].astype(F32) + back * r.scale[at, 0:1]).astype(BF16)
        return 0

    lax.fori_loop(0, T // RC, final_rows, 0)

    def join(mine_ref, got, out, width, place):
        per = width // 128
        n = out.shape[0] // per
        here = mine_ref[at_me + (x,)].astype(F32)
        there = got[...].astype(F32)
        halves = (jnp.where(x == 0, here, there), jnp.where(x == 0, there, here))

        def piece(b, to_high):
            half, m, odd = place(b)
            v = halves[half][:, m * 128 : (m + 1) * 128]
            return pltpu.roll(v, 64, 1) if odd != to_high else v

        for j in range(per):
            both = jnp.where(lane < 64, piece(2 * j, False), piece(2 * j + 1, True))
            out[pl.ds(j, n, stride=per), :] = both

    def place_q(b):
        h, jj = b // 3, b % 3
        return h // HC, (h % HC) // 2 * 3 + jj, h % 2 == 1

    def place_i(b):
        return b % 2, b // 4, (b // 2) % 2 == 1

    wait("si")
    join(r.gi, r.xi, r.oi, FF, place_i)
    wait("sq")
    join(r.gq, r.xq, r.oq, 3 * D, place_q)

    def put_vec(acc):
        r.ov[...] = acc

    add_parts("v", "x", "cyz", None, put_vec)


def rope_table(length):
    lanes = np.arange(128) % HD
    rot = HD // 4
    inverse = np.where(lanes < rot, 1.0 / ROPE_BASE ** (2.0 * (lanes % (rot // 2)) / rot), 0.0)
    high = 32.0 * np.arange(length // 32)[:, None] * inverse
    low = np.arange(32)[:, None] * inverse
    return np.stack([np.cos(high), np.sin(high), np.cos(low), np.sin(low)]).astype(np.float32)


def layer(sizes, tokens, cotangent, *params):
    Z, Y, C, X = (sizes[a] for a in AX)
    N = Z * Y * C * X
    T = tokens.shape[1]
    S = T * X
    HW = HEADS // X * HD
    vectors = [params[i] for i in (0, 1, 2, 3, 5, 7, 9, 11)]
    weights = [params[i] for i in (4, 6, 8, 10)]
    vin = jnp.stack([jnp.pad(v.astype(F32), (0, 128 - v.shape[0])) for v in vectors])
    flats = [w.reshape(-1, 128) for w in weights]
    full = dict(z=Z, y=Y, c=C, x=X)

    FH = FF // X

    def parts(name, axis, done, slab, dtype):
        free = [full[a] for a in AX if a not in done and a != axis and (a != "x" or name != "o")]
        return pltpu.VMEM((full[axis] - 1, *free, *slab), dtype)

    slabs = {
        "q": (D // N, 3 * HW),
        "d": (D // N, D),
        "i": (D // N, FH),
        "o": (FF // N, D),
        "v": (8, 128),
    }
    orders = {"q": "cyz", "d": "cyz", "i": "cyz", "o": "cyz", "v": "cyzx"}
    keep = types.SimpleNamespace()
    scratch = vars(keep)
    for k, slab in slabs.items():
        kind = F32 if k == "v" else BF16
        devs = (Z, Y, C) if k == "o" else (Z, Y, C, X)
        scratch["w" + k] = pltpu.VMEM((*devs, *slab), kind)
        scratch["g" + k] = pltpu.VMEM((*devs, *slab), kind)
        for n, axis in enumerate(orders[k]):
            done = orders[k][:n] + ("x" if k == "d" else "")
            scratch["r" + k + axis] = parts(k, axis, done, slab, kind)
    keep.xq = pltpu.VMEM(slabs["q"], BF16)
    keep.xi = pltpu.VMEM(slabs["i"], BF16)
    keep.sq = pltpu.VMEM((X, *slabs["q"]), BF16)
    keep.si = pltpu.VMEM((X, *slabs["i"]), BF16)
    keep.tmp = pltpu.VMEM((max(f.shape[0] for f in flats), 128), F32)
    keep.cos = keep.sinl = keep.sinh = pltpu.VMEM((S, 128), F32)
    keep.tok2 = pltpu.VMEM((T, D), BF16)
    keep.cots = pltpu.VMEM((S, D), BF16)
    keep.n = pltpu.VMEM((S, D), F32)
    keep.scale = pltpu.VMEM((T, 128), F32)
    keep.vrow = pltpu.VMEM((8, FH), F32)
    keep.vg = pltpu.VMEM((8, FH), F32)
    keep.ha = keep.hm = pltpu.VMEM((S, D), BF16)
    keep.hmt = pltpu.VMEM((D, S), BF16)
    keep.q = keep.k = keep.v = keep.do2 = pltpu.VMEM((S, HW), BF16)
    keep.kt = keep.vt = keep.ot = pltpu.VMEM((HW, S), BF16)
    keep.dqt = pltpu.VMEM((HW, S), F32)
    keep.dk = pltpu.VMEM((S, HW), F32)
    keep.dv = pltpu.VMEM((S, HW), F32)
    keep.st = pltpu.VMEM((S // QB, QB, QB), F32)
    keep.dp = pltpu.VMEM((S // QB, QB, QB), F32)
    keep.pb = pltpu.VMEM((S, QB), BF16)
    keep.ds = pltpu.VMEM((S, QB), BF16)
    keep.dqkv = pltpu.VMEM((S, 3 * HW), BF16)
    keep.of = pltpu.VMEM((D, T), BF16)
    keep.act = keep.df = pltpu.VMEM((S, FH), BF16)
    keep.slope = pltpu.VMEM((S, FH), F32)
    keep.um = pltpu.VMEM((S, D), F32)
    keep.u = keep.mo = pltpu.VMEM((T, D), F32)
    keep.us = keep.ur = keep.mos = keep.mor = pltpu.VMEM((T, D), BF16)
    copies = 128
    keep.send = pltpu.SemaphoreType.DMA((copies,))
    keep.recv = pltpu.SemaphoreType.DMA((copies,))
    ins = "tokens cot fq fd".split() + "fi fo vin rope".split()
    outs = dict(
        out=jax.ShapeDtypeStruct((T, D), BF16),
        gtok=jax.ShapeDtypeStruct((T, D), BF16),
        oq=jax.ShapeDtypeStruct(flats[0].shape, F32),
        od=jax.ShapeDtypeStruct(flats[1].shape, F32),
        oi=jax.ShapeDtypeStruct(flats[2].shape, F32),
        oo=jax.ShapeDtypeStruct(flats[3].shape, F32),
        ov=jax.ShapeDtypeStruct((8, 128), F32),
    )
    vmem = pl.BlockSpec(memory_space=pltpu.VMEM)
    names = ins + list(outs) + list(scratch)
    out, gtok, gq, gd, gi, go, gv = pl.pallas_call(
        functools.partial(fused, sizes, names),
        out_shape=list(outs.values()),
        in_specs=[vmem] * len(ins),
        out_specs=[vmem] * len(outs),
        scratch_shapes=list(scratch.values()),
        compiler_params=pltpu.CompilerParams(
            collective_id=0, has_side_effects=True, vmem_limit_bytes=67043328
        ),
        name="layer",
    )(
        tokens.reshape(T, D),
        cotangent.reshape(T, D),
        *flats,
        vin,
        jnp.asarray(rope_table(S)),
    )
    v = [gv[i, : p.shape[0]] for i, p in enumerate(vectors)]
    return (
        out.reshape(tokens.shape),
        gtok.reshape(tokens.shape),
        v[0],
        v[1],
        v[2],
        v[3],
        gq.reshape(-1),
        v[4],
        gd.reshape(-1),
        v[5],
        gi.reshape(-1),
        v[6],
        go.reshape(-1),
        v[7],
    )


def solution(mesh):
    n_seq, n_ctx = mesh.shape["seq"], mesh.shape["ctx"]
    if n_ctx != 2 or n_seq % 8 or (D // (n_seq * n_ctx)) % 16:
        return general(mesh)
    sizes = {"z": n_seq // 4, "y": 2, "c": 2, "x": n_ctx}
    flat = P(("seq", "ctx"))
    rows = P("seq", "ctx", None)
    return jax.shard_map(
        functools.partial(layer, sizes),
        mesh=mesh,
        in_specs=(rows, rows) + (flat,) * 12,
        out_specs=(rows, rows) + (flat,) * 12,
        check_vma=False,
    )
```

```python
import functools
import types

import jax
import jax.numpy as jnp
import numpy as np
from jax import lax
from jax.experimental import pallas as pl
from jax.experimental.pallas import tpu as pltpu
from jax.sharding import PartitionSpec as P

D = 512
HEADS = 8
FF = 2048


EPS = 1e-05
BOTH = ("seq", "ctx")
ROPE_BASE = 10000.0
NEG = -1e30


def layer_normalize(values, gain, bias):
    mean = jnp.mean(values, axis=-1, keepdims=True)
    centered = values - mean
    var = jnp.mean(centered * centered, axis=-1, keepdims=True)
    return centered * lax.rsqrt(var + EPS) * gain + bias


def rotate(values, cosine, sine):
    width = cosine.shape[-1]
    half = width // 2
    part = values[..., :width]
    turned = jnp.concatenate([-part[..., half:], part[..., :half]], axis=-1)
    return jnp.concatenate([part * cosine + turned * sine, values[..., width:]], axis=-1)


def gelu_exact(values):
    return jax.nn.gelu(values, approximate=False)


def matrices(mix_flat, proj_flat, expand_flat, reduce_flat):
    return (
        mix_flat.reshape(D, 3 * D),
        proj_flat.reshape(D, D),
        expand_flat.reshape(D, FF),
        reduce_flat.reshape(FF, D),
    )


def body(
    tokens,
    cotangent,
    attn_norm_gain,
    attn_norm_bias,
    mlp_norm_gain,
    mlp_norm_bias,
    qkv_weight,
    qkv_bias,
    dense_weight,
    dense_bias,
    fc_in_weight,
    fc_in_bias,
    fc_out_weight,
    fc_out_bias,
):
    (
        gain_attn,
        attention_shift,
        gain_mlp,
        shift_mlp,
        mix_flat,
        mix_bias,
        proj_flat,
        proj_bias,
        expand_flat,
        expand_bias,
        reduce_flat,
        reduce_bias,
    ) = (
        lax.all_gather(attn_norm_gain, BOTH, axis=0, tiled=True),
        lax.all_gather(attn_norm_bias, BOTH, axis=0, tiled=True),
        lax.all_gather(mlp_norm_gain, BOTH, axis=0, tiled=True),
        lax.all_gather(mlp_norm_bias, BOTH, axis=0, tiled=True),
        lax.all_gather(qkv_weight, BOTH, axis=0, tiled=True),
        lax.all_gather(qkv_bias, BOTH, axis=0, tiled=True),
        lax.all_gather(dense_weight, BOTH, axis=0, tiled=True),
        lax.all_gather(dense_bias, BOTH, axis=0, tiled=True),
        lax.all_gather(fc_in_weight, BOTH, axis=0, tiled=True),
        lax.all_gather(fc_in_bias, BOTH, axis=0, tiled=True),
        lax.all_gather(fc_out_weight, BOTH, axis=0, tiled=True),
        lax.all_gather(fc_out_bias, BOTH, axis=0, tiled=True),
    )
    mix_weight, proj_weight, expand_weight, reduce_weight = matrices(
        mix_flat, proj_flat, expand_flat, reduce_flat
    )
    shape = tokens.shape
    group = shape[1]
    width = shape[2]
    heads = HEADS
    head_dim = width // heads
    rows = tokens.reshape(group, width).astype(jnp.float32)
    attn_in, attn_norm_back = jax.vjp(
        layer_normalize, rows, gain_attn.astype(jnp.float32), attention_shift.astype(jnp.float32)
    )
    mlp_in, mlp_norm_back = jax.vjp(
        layer_normalize, rows, gain_mlp.astype(jnp.float32), shift_mlp.astype(jnp.float32)
    )
    attn_low = attn_in.astype(jnp.bfloat16)
    mlp_low = mlp_in.astype(jnp.bfloat16)
    mixed = jnp.dot(attn_low, mix_weight, preferred_element_type=jnp.float32) + mix_bias.astype(
        jnp.float32
    )
    mixed = mixed.reshape(group, heads, 3, head_dim)
    place = lax.axis_index("ctx")
    blocks_total = lax.axis_size("ctx")
    local_pos = jnp.arange(group, dtype=jnp.int32)
    query_pos = place * group + local_pos
    rot_dims = head_dim // 4
    inverse = 1.0 / ROPE_BASE ** (
        jnp.arange(0, rot_dims, 2, dtype=jnp.int32).astype(jnp.float32) / rot_dims
    )
    angles = query_pos.astype(jnp.float32)[:, None] * inverse[None, :]
    angles = jnp.concatenate([angles, angles], axis=-1)
    cosine = jnp.cos(angles)[:, None, :]
    sine = jnp.sin(angles)[:, None, :]
    scale = head_dim ** (-0.5)

    def turn(query_unrotated, key_raw):
        return (rotate(query_unrotated, cosine, sine) * scale, rotate(key_raw, cosine, sine))

    (query_f, key_f), turn_back = jax.vjp(turn, mixed[:, :, 0], mixed[:, :, 1])
    query = query_f.astype(jnp.bfloat16)
    key_own = key_f.astype(jnp.bfloat16).reshape(group, width)
    value_own = mixed[:, :, 2].astype(jnp.bfloat16).reshape(group, width)
    all_keys, all_values = (
        lax.all_gather(key_own, "ctx", axis=0, tiled=True),
        lax.all_gather(value_own, "ctx", axis=0, tiled=True),
    )
    count = place + 1

    def block(index):
        keys = lax.dynamic_slice_in_dim(all_keys, index * group, group, 0).reshape(
            group, heads, head_dim
        )
        values = lax.dynamic_slice_in_dim(all_values, index * group, group, 0).reshape(
            group, heads, head_dim
        )
        scores = jnp.einsum("qhd,khd->hqk", query, keys, preferred_element_type=jnp.float32)
        allowed = (index * group + local_pos)[None, :] <= query_pos[:, None]
        return (keys, values, scores, allowed[None])

    def max_step(index, carry):
        top, total = carry
        _, _, scores, allowed = block(index)
        new_top = jnp.maximum(top, jnp.max(jnp.where(allowed, scores, NEG), axis=-1))
        terms = jnp.where(allowed, jnp.exp(scores - new_top[:, :, None]), 0.0)
        return (new_top, total * jnp.exp(top - new_top) + jnp.sum(terms, axis=-1))

    start = (jnp.full((heads, group), NEG, jnp.float32), jnp.zeros((heads, group), jnp.float32))
    top, total = lax.fori_loop(0, count, max_step, start)
    log_total = top + jnp.log(total)

    def probs_of(scores, allowed):
        return jnp.where(allowed, jnp.exp(scores - log_total[:, :, None]), 0.0)

    def out_step(index, acc):
        _, values, scores, allowed = block(index)
        probs = probs_of(scores, allowed).astype(jnp.bfloat16)
        return acc + jnp.einsum("hqk,khd->qhd", probs, values, preferred_element_type=jnp.float32)

    heads_out = lax.fori_loop(0, count, out_step, jnp.zeros((group, heads, head_dim), jnp.float32))
    attn_out = heads_out.reshape(group, width).astype(jnp.bfloat16)
    branch_attn = jnp.dot(
        attn_out, proj_weight, preferred_element_type=jnp.float32
    ) + proj_bias.astype(jnp.float32)
    expand = jnp.dot(
        mlp_low, expand_weight, preferred_element_type=jnp.float32
    ) + expand_bias.astype(jnp.float32)
    active_rows, active_back = jax.vjp(gelu_exact, expand)
    active_low = active_rows.astype(jnp.bfloat16)
    branch_mlp = jnp.dot(
        active_low, reduce_weight, preferred_element_type=jnp.float32
    ) + reduce_bias.astype(jnp.float32)
    layer_out = (rows + branch_attn + branch_mlp).astype(jnp.bfloat16).reshape(shape)
    back_mix, back_proj, back_expand, back_reduce = (
        lax.all_gather(qkv_weight, BOTH, axis=0, tiled=True),
        lax.all_gather(dense_weight, BOTH, axis=0, tiled=True),
        lax.all_gather(fc_in_weight, BOTH, axis=0, tiled=True),
        lax.all_gather(fc_out_weight, BOTH, axis=0, tiled=True),
    )
    back_mix, back_proj, back_expand, back_reduce = matrices(
        back_mix, back_proj, back_expand, back_reduce
    )
    grad_rows = cotangent.reshape(group, width)
    grad_float = grad_rows.astype(jnp.float32)
    grad_reduce = jnp.einsum("tf,td->fd", active_low, grad_rows, preferred_element_type=jnp.float32)
    grad_out_bias = jnp.sum(grad_float, axis=0)
    grad_proj = jnp.einsum("te,td->ed", attn_out, grad_rows, preferred_element_type=jnp.float32)
    grad_active = jnp.einsum(
        "td,fd->tf", grad_rows, back_reduce, preferred_element_type=jnp.float32
    )
    grad_expand = active_back(grad_active)[0].astype(jnp.bfloat16)
    grad_expand_w = jnp.einsum(
        "td,tf->df", mlp_low, grad_expand, preferred_element_type=jnp.float32
    )
    grad_expand_b = jnp.sum(grad_expand.astype(jnp.float32), axis=0)
    grad_mlp_in = jnp.einsum(
        "tf,df->td", grad_expand, back_expand, preferred_element_type=jnp.float32
    )
    grad_heads = jnp.einsum("td,ed->te", grad_rows, back_proj, preferred_element_type=jnp.float32)
    grad_heads = grad_heads.astype(jnp.bfloat16).reshape(group, heads, head_dim)

    def delta_step(index, acc):
        _, values, scores, allowed = block(index)
        probs = probs_of(scores, allowed)
        grad_probs = jnp.einsum(
            "qhd,khd->hqk", grad_heads, values, preferred_element_type=jnp.float32
        )
        return acc + jnp.sum(probs * grad_probs, axis=-1)

    delta = lax.fori_loop(0, count, delta_step, jnp.zeros((heads, group), jnp.float32))

    def query_step(index, grad_query):
        keys, values, scores, allowed = block(index)
        probs = probs_of(scores, allowed)
        grad_probs = jnp.einsum(
            "qhd,khd->hqk", grad_heads, values, preferred_element_type=jnp.float32
        )
        grad_scores = (probs * (grad_probs - delta[:, :, None])).astype(jnp.bfloat16)
        return grad_query + jnp.einsum(
            "hqk,khd->qhd", grad_scores, keys, preferred_element_type=jnp.float32
        )

    grad_query = lax.fori_loop(
        0, count, query_step, jnp.zeros((group, heads, head_dim), jnp.float32)
    )
    all_queries, all_grad_heads = (
        lax.all_gather(query.reshape(group, width), "ctx", axis=0, tiled=True),
        lax.all_gather(grad_heads.reshape(group, width), "ctx", axis=0, tiled=True),
    )
    gathered_log_sums, all_delta = (
        lax.all_gather(jnp.transpose(log_total), "ctx", axis=0, tiled=True),
        lax.all_gather(jnp.transpose(delta), "ctx", axis=0, tiled=True),
    )
    keys_mine = key_own.reshape(group, heads, head_dim)
    values_mine = value_own.reshape(group, heads, head_dim)

    def owner_step(index, carry):
        key_acc, value_accumulator = carry
        queries = lax.dynamic_slice_in_dim(all_queries, index * group, group, 0).reshape(
            group, heads, head_dim
        )
        outer_grads = lax.dynamic_slice_in_dim(all_grad_heads, index * group, group, 0).reshape(
            group, heads, head_dim
        )
        lse_rows = jnp.transpose(
            lax.dynamic_slice_in_dim(gathered_log_sums, index * group, group, 0)
        )
        delta_rows = jnp.transpose(lax.dynamic_slice_in_dim(all_delta, index * group, group, 0))
        scores = jnp.einsum("qhd,khd->hqk", queries, keys_mine, preferred_element_type=jnp.float32)
        allowed = (query_pos[None, :] <= (index * group + local_pos)[:, None])[None]
        probs = jnp.where(allowed, jnp.exp(scores - lse_rows[:, :, None]), 0.0)
        grad_probs = jnp.einsum(
            "qhd,khd->hqk", outer_grads, values_mine, preferred_element_type=jnp.float32
        )
        grad_scores = (probs * (grad_probs - delta_rows[:, :, None])).astype(jnp.bfloat16)
        key_acc = key_acc + jnp.einsum(
            "hqk,qhd->khd", grad_scores, queries, preferred_element_type=jnp.float32
        )
        value_accumulator = value_accumulator + jnp.einsum(
            "hqk,qhd->khd",
            probs.astype(jnp.bfloat16),
            outer_grads,
            preferred_element_type=jnp.float32,
        )
        return (key_acc, value_accumulator)

    empty_heads = jnp.zeros((group, heads, head_dim), jnp.float32)
    own_key_grad, own_value_grad = lax.fori_loop(
        place, blocks_total, owner_step, (empty_heads, empty_heads)
    )
    grad_query_raw, grad_key_raw = turn_back((grad_query, own_key_grad))
    grad_mixed = jnp.stack([grad_query_raw, grad_key_raw, own_value_grad], axis=2)
    grad_mixed = grad_mixed.reshape(group, 3 * width).astype(jnp.bfloat16)
    grad_mix_w = jnp.einsum("td,te->de", attn_low, grad_mixed, preferred_element_type=jnp.float32)
    grad_mix_b = jnp.sum(grad_mixed.astype(jnp.float32), axis=0)
    grad_attn_in = jnp.einsum("te,de->td", grad_mixed, back_mix, preferred_element_type=jnp.float32)
    input_attn, gain_attn_grad, shift_attn_grad = attn_norm_back(grad_attn_in)
    input_mlp, gain_mlp_grad, shift_mlp_grad = mlp_norm_back(grad_mlp_in)
    grad_tokens = (grad_float + input_attn + input_mlp).astype(jnp.bfloat16).reshape(shape)
    sums = (
        lax.psum_scatter(gain_attn_grad, BOTH, scatter_dimension=0, tiled=True),
        lax.psum_scatter(shift_attn_grad, BOTH, scatter_dimension=0, tiled=True),
        lax.psum_scatter(gain_mlp_grad, BOTH, scatter_dimension=0, tiled=True),
        lax.psum_scatter(shift_mlp_grad, BOTH, scatter_dimension=0, tiled=True),
        lax.psum_scatter(grad_mix_w.reshape(-1), BOTH, scatter_dimension=0, tiled=True),
        lax.psum_scatter(grad_mix_b, BOTH, scatter_dimension=0, tiled=True),
        lax.psum_scatter(grad_proj.reshape(-1), BOTH, scatter_dimension=0, tiled=True),
        lax.psum_scatter(grad_out_bias, BOTH, scatter_dimension=0, tiled=True),
        lax.psum_scatter(
            grad_expand_w.reshape(-1), BOTH, scatter_dimension=0, tiled=True
        ),
        lax.psum_scatter(grad_expand_b, BOTH, scatter_dimension=0, tiled=True),
        lax.psum_scatter(grad_reduce.reshape(-1), BOTH, scatter_dimension=0, tiled=True),
        lax.psum_scatter(grad_out_bias, BOTH, scatter_dimension=0, tiled=True),
    )
    return (
        layer_out,
        grad_tokens,
        sums[0],
        sums[1],
        sums[2],
        sums[3],
        sums[4],
        sums[5],
        sums[6],
        sums[7],
        sums[8],
        sums[9],
        sums[10],
        sums[11],
    )


def general(mesh):
    return jax.shard_map(
        body,
        mesh=mesh,
        in_specs=(
            P("seq", "ctx", None),
            P("seq", "ctx", None),
            P(BOTH),
            P(BOTH),
            P(BOTH),
            P(BOTH),
            P(BOTH),
            P(BOTH),
            P(BOTH),
            P(BOTH),
            P(BOTH),
            P(BOTH),
            P(BOTH),
            P(BOTH),
        ),
        out_specs=(
            P("seq", "ctx", None),
            P("seq", "ctx", None),
            P(BOTH),
            P(BOTH),
            P(BOTH),
            P(BOTH),
            P(BOTH),
            P(BOTH),
            P(BOTH),
            P(BOTH),
            P(BOTH),
            P(BOTH),
            P(BOTH),
            P(BOTH),
        ),
        check_vma=False,
    )


MESH = pl.DeviceIdType.MESH
F32, BF16 = jnp.float32, jnp.bfloat16
HD = D // HEADS
AX = "zycx"
NN = (((1,), (0,)), ((), ()))
NT = (((1,), (1,)), ((), ()))
TN = (((0,), (0,)), ((), ()))
QB = 256


def mm(a, b, dims=NN):
    return lax.dot_general(a, b, dims, preferred_element_type=F32)


def iota(shape, dim):
    return lax.broadcasted_iota(jnp.int32, shape, dim)


def fused(sizes, names, *refs):
    held = dict(zip(names, refs))
    r = types.SimpleNamespace(**held)
    X = sizes["x"]
    C = sizes["c"]
    Y = sizes["y"]
    Z = sizes["z"]
    N = Z * Y * C * X
    T = r.tokens.shape[0]
    S = T * X
    HC = HEADS // X
    HW = HC * HD
    FH = FF // X
    CH = dict(q=384, i=FH // 2, o=D // 2)
    s = lax.axis_index("seq")
    me = {"x": lax.axis_index("ctx"), "c": s % C, "y": (s // C) % Y, "z": s // (C * Y)}
    x = me["x"]
    xo = 1 - x

    def device(at):
        return ((at["z"] * Y + at["y"]) * C + at["c"], at["x"])

    def others(axis):
        n = sizes[axis]
        return [dict(me, **{axis: (me[axis] + d) % n}) for d in range(1, n)]

    flight = {}
    count = [0]

    def push(key, src, dst, at):
        k = count[0]
        count[0] += 1
        cp = pltpu.make_async_remote_copy(
            src_ref=src,
            dst_ref=dst,
            send_sem=r.send.at[k],
            recv_sem=r.recv.at[k],
            device_id=device(at),
            device_id_type=MESH,
        )
        cp.start()
        flight.setdefault(key, []).append(cp)

    def wait(key):
        for cp in flight.pop(key):
            cp.wait()

    def axes(name):
        return AX[: 3 if name == "o" else 4]

    def chunk(name, k):
        if k is None:
            return slice(None)
        w = CH[name]
        return slice(k * w, (k + 1) * w)

    def gather(name, axis, known, k=None):
        ref = held["w" + name]
        spot = tuple(slice(None) if a in known else me[a] for a in axes(name))
        part = ref.at[spot + (slice(None), chunk(name, k))]
        for at in others(axis):
            push(("w", name, axis, k), part, part, at)

    def relay(name, axis, nxt, known, k=None):
        wait(("w", name, axis, k))
        gather(name, nxt, known + axis, k)

    def arrived(name, k=None):
        wait(("w", name, "c", k))

    def scatter(name, axis, done, k=None):
        ref, got = held["g" + name], held["r" + name + axis]
        free = [a for a in axes(name) if a not in done and a != axis]
        cols = (slice(None), chunk(name, k))
        for n, at in enumerate(others(axis)):
            spot = tuple(slice(None) if a in free else at[a] for a in axes(name))
            to = (n,) + (slice(None),) * len(free)
            push(("g", name, axis, k), ref.at[spot + cols], got.at[to + cols], at)

    def add_parts(name, axis, done, k=None, finish=None):
        wait(("g", name, axis, k))
        ref, got = held["g" + name], held["r" + name + axis]
        free = [a for a in axes(name) if a not in done and a != axis]
        cols = (slice(None), chunk(name, k))
        total = 1
        for a in free:
            total *= sizes[a]

        def one(i, _):
            at, rest = dict(me), i
            for a in reversed(free):
                at[a] = rest % sizes[a]
                rest = rest // sizes[a]
            spot = tuple(at[a] for a in axes(name))
            inner = tuple(at[a] for a in free)
            acc = ref[spot + cols].astype(F32)
            for n in range(sizes[axis] - 1):
                acc = acc + got[(n,) + inner + cols].astype(F32)
            if finish is None:
                ref[spot + cols] = acc.astype(ref.dtype)
            else:
                finish(acc)
            return 0

        if total == 1:
            one(0, 0)
        else:
            lax.fori_loop(0, total, one, 0)

    def step(name, axis, nxt, done="", k=None):
        add_parts(name, axis, done, k)
        scatter(name, nxt, done + axis, k)

    barrier = pltpu.get_barrier_semaphore()
    greet = [at for a in AX for at in others(a)]
    for at in greet:
        pl.semaphore_signal(barrier, inc=1, device_id=device(at), device_id_type=MESH)

    tmp = r.tmp
    lane = iota((1, 128), 1)

    def own(name):
        return held[name].at[me["z"], me["y"], me["c"], x]

    def block64(b, per, rows, to_high):
        v = tmp[pl.ds(b // 2, rows, stride=per), :]
        return pltpu.roll(v, 64, 1) if (b % 2 == 1) != to_high else v

    def split(src, dst, width, table):
        n = held[src].shape[0]
        per = width // 128
        tmp[0:n, :] = held[src][...].astype(F32)
        for half in range(X):
            for m in range(per // X):
                low, high = table(half, m)
                low = block64(low, per, n // per, False)
                high = block64(high, per, n // per, True)
                dst[half, :, m * 128 : (m + 1) * 128] = jnp.where(lane < 64, low, high).astype(BF16)

    def table_q(half, m):
        h0 = half * HC + 2 * (m // 3)
        return 3 * h0 + m % 3, 3 * (h0 + 1) + m % 3

    def table_i(half, m):
        return 4 * m + half, 4 * m + 2 + half

    def reshard(src, dst, width):
        n = held[src].shape[0]
        k = width // 128
        tmp[0:n, :] = held[src][...].astype(F32)
        for j in range(k):
            dst[:, j * 128 : (j + 1) * 128] = tmp[pl.ds(j, n // k, stride=k), :].astype(BF16)

    split("fq", r.sq, 3 * D, table_q)
    split("fi", r.si, FF, table_i)
    reshard("fd", own("wd"), D)
    vecs = own("wv")
    vecs[...] = jnp.zeros_like(vecs)
    for v in range(8):
        vin = held["v%d" % v]
        vecs[v : v + 1, 0 : vin.shape[1]] = vin[...].astype(F32)
    own("wq")[...] = r.sq[x]
    own("wi")[...] = r.si[x]

    pl.semaphore_wait(barrier, len(greet))

    rows_mine = pl.ds(pl.multiple_of(x * T, T), T)
    rows_theirs = pl.ds(pl.multiple_of(xo * T, T), T)
    at_x = others("x")[0]
    gather("v", "x", "")
    push("sq", r.sq.at[xo], own("wq"), at_x)
    push("si", r.si.at[xo], own("wi"), at_x)
    gather("d", "x", "")
    push("tok", r.tokens, r.tok2, at_x)
    push("cot", r.cot, r.cots.at[rows_mine, :], at_x)
    reshard("fo", r.wo.at[me["z"], me["y"], me["c"]], D)

    rope = r.rope
    mod = lane % HD

    def rope_rows(i, _):
        ch, sh = rope[0, pl.ds(i, 1), :], rope[1, pl.ds(i, 1), :]
        cl, sl = rope[2], rope[3]
        sine = sh * cl + ch * sl
        at = pl.ds(pl.multiple_of(i * 32, 32), 32)
        r.cos[at, :] = ch * cl - sh * sl
        r.sinl[at, :] = jnp.where(mod < 8, -sine, 0.0)
        r.sinh[at, :] = jnp.where(mod < 8, 0.0, sine)
        return 0

    def turn(u, at, sign):
        return (
            u * r.cos[at, :]
            + sign * (pltpu.roll(u, 120, 1) * r.sinl[at, :] + pltpu.roll(u, 8, 1) * r.sinh[at, :])
        )

    relay("v", "x", "z", "")
    wait("sq")
    gather("q", "z", "x", 0)
    gather("q", "z", "x", 1)
    relay("d", "x", "z", "")
    wait("si")
    gather("i", "z", "x", 0)
    gather("i", "z", "x", 1)
    gather("o", "z", "", 0)
    gather("o", "z", "", 1)
    lax.fori_loop(0, S // 32, rope_rows, 0)

    RC = 128

    def norm_rows(src, base, keep):
        def one(i, _):
            v = src[pl.ds(pl.multiple_of(i * RC, RC), RC), :].astype(F32)
            c = v - jnp.mean(v, axis=-1, keepdims=True)
            scale = lax.rsqrt(jnp.mean(c * c, axis=-1, keepdims=True) + EPS)
            r.n[pl.ds(pl.multiple_of(base + i * RC, RC), RC), :] = c * scale
            if keep:
                r.scale[pl.ds(pl.multiple_of(i * RC, RC), RC), :] = jnp.broadcast_to(scale, (RC, 128))
            return 0

        lax.fori_loop(0, T // RC, one, 0)

    norm_rows(r.tokens, x * T, True)

    relay("v", "z", "y", "x")
    relay("q", "z", "y", "x", 0)
    relay("v", "y", "c", "xz")
    relay("q", "z", "y", "x", 1)
    arrived("v")

    widths = [D // N, D // N, D // N, D // N, 3 * D // N, D // N, FF // N, D // N]

    def column(v, n):
        j = iota((1, n), 1)
        if v == 4:
            head_at = x * HC + 2 * (j // 384) + (j % 128) // HD
            return head_at * (3 * HD) + ((j % 384) // 128) * HD + j % HD
        if v == 6:
            return (j // 64) * 128 + x * 64 + j % 64
        return j

    def lengths(v):
        return {4: 3 * HW, 6: FH}.get(v, D)

    vec2 = r.wv.reshape(N * 8, 128)

    def expand(v):
        n = lengths(v)
        j = column(v, n)
        pick = (iota((128, n), 0) == j % widths[v]).astype(F32).astype(BF16)
        rows_v = vec2[pl.ds(v, N, stride=8), :].astype(BF16)
        spread = mm(rows_v, pick)
        r.vrow[v : v + 1, 0:n] = jnp.sum(
            jnp.where(iota((N, n), 0) == j // widths[v], spread, 0.0), axis=0, keepdims=True
        )

    for v in range(8):
        expand(v)

    def row(v, n=D, off=0):
        return r.vrow[v : v + 1, off : off + n]

    def affine_attn(base):
        def one(i, _):
            at = pl.ds(pl.multiple_of(base + i * RC, RC), RC)
            r.ha[at, :] = (r.n[at, :] * row(0) + row(1)).astype(BF16)
            return 0

        lax.fori_loop(0, T // RC, one, 0)

    def affine_mlp(base):
        def one(i, _):
            at = pl.ds(pl.multiple_of(base + i * RC, RC), RC)
            r.hm[at, :] = (r.n[at, :] * row(2) + row(3)).astype(BF16)
            return 0

        lax.fori_loop(0, T // RC, one, 0)

    affine_attn(x * T)
    relay("d", "z", "y", "x")
    relay("q", "y", "c", "xz", 0)
    affine_mlp(x * T)
    relay("q", "y", "c", "xz", 1)
    relay("i", "z", "y", "x", 0)

    wait("tok")
    norm_rows(r.tok2, xo * T, False)
    affine_attn(xo * T)
    affine_mlp(xo * T)
    relay("i", "z", "y", "x", 1)
    relay("d", "y", "c", "xz")

    wq = r.wq.reshape(D, 3 * HW)

    def qkv(b):
        def one(i, _):
            at = pl.ds(pl.multiple_of(i * QB, QB), QB)
            u = mm(r.ha[at, :], wq[:, chunk("q", b)]) + row(4, 384, b * 384)
            for jj, name in enumerate("qkv"):
                w = u[:, jj * 128 : (jj + 1) * 128]
                if jj < 2:
                    w = turn(w, at, 1.0)
                if jj == 0:
                    w = w * HD**-0.5
                w = w.astype(BF16)
                held[name][at, b * 128 : (b + 1) * 128] = w
                if jj >= 1:
                    held[name + "t"][b * 128 : (b + 1) * 128, at] = w.T
            return 0

        arrived("q", b)
        lax.fori_loop(0, S // QB, one, 0)

    qkv(0)
    qkv(1)
    arrived("d")
    wd = r.wd.reshape(D, D)
    mine = pl.ds(pl.multiple_of(x * HW, HW), HW)
    r.do2[rows_mine, :] = mm(r.cot[...], wd[mine, :], NT).astype(BF16)

    r.dk[...] = jnp.zeros_like(r.dk)
    r.dv[...] = jnp.zeros_like(r.dv)
    causal = iota((QB, QB), 0) <= iota((QB, QB), 1)

    def head(blocks, h, _):
        lanes = pl.ds(pl.multiple_of((h // 2) * 128, 128), 128)
        ours = (lane // HD) == h % 2
        head_rows = pl.ds(pl.multiple_of(h * HD, HD), HD)
        for i in blocks:
            here = slice(i * QB, (i + 1) * QB)
            qm = jnp.where(ours, r.q[here, lanes], jnp.zeros((), BF16))
            dom = jnp.where(ours, r.do2[here, lanes], jnp.zeros((), BF16))
            top = None
            for j in range(i + 1):
                st = mm(r.k[j * QB : (j + 1) * QB, lanes], qm, NT)
                if j == i:
                    st = jnp.where(causal, st, NEG)
                r.st[j] = st
                part = jnp.max(st, axis=0, keepdims=True)
                top = part if top is None else jnp.maximum(top, part)
            total = None
            for j in range(i + 1):
                e = jnp.exp(r.st[j] - top)
                r.st[j] = e
                part = jnp.sum(e, axis=0, keepdims=True)
                total = part if total is None else total + part
            scale = 1.0 / total
            delta = None
            for j in range(i + 1):
                p = r.st[j] * scale
                r.st[j] = p
                r.pb[j * QB : (j + 1) * QB, :] = p.astype(BF16)
                dp = mm(r.v[j * QB : (j + 1) * QB, lanes], dom, NT)
                r.dp[j] = dp
                part = jnp.sum(p * dp, axis=0, keepdims=True)
                delta = part if delta is None else delta + part
            for j in range(i + 1):
                ds = r.st[j] * (r.dp[j] - delta)
                r.ds[j * QB : (j + 1) * QB, :] = ds.astype(BF16)
            n = (i + 1) * QB
            pb, ds = r.pb[0:n, :], r.ds[0:n, :]
            r.ot[head_rows, here] = mm(r.vt[head_rows, 0:n], pb).astype(BF16)
            r.dqt[head_rows, here] = mm(r.kt[head_rows, 0:n], ds)
            r.dk[0:n, lanes] += mm(ds, qm)
            r.dv[0:n, lanes] += mm(pb, dom)
        return 0

    per_x = T // QB

    def attend(theirs, first, last):
        for k in range(X):
            at = (1 - k if theirs else k) * per_x
            run = functools.partial(head, range(at, at + per_x))

            @pl.when(x == k)
            def _():
                lax.fori_loop(first, last, run, 0)

    attend(False, 0, 2)
    relay("i", "y", "c", "xz", 0)
    relay("o", "z", "y", "", 0)
    attend(False, 2, 4)
    relay("i", "y", "c", "xz", 1)
    r.hmt[...] = r.hm[...].T

    wi = r.wi.reshape(D, FH)
    wo = r.wo.reshape(FH, D)
    gi = r.gi.reshape(D, FH)
    go = r.go.reshape(FH, D)
    FB = 256

    def ff_cols(b):
        return pl.ds(pl.multiple_of(b * FB, FB), FB)

    def ff_forward(b, _):
        cols = ff_cols(b)
        f = mm(r.hm[...], wi[:, cols]) + r.vrow[6:7, cols]
        phi = 0.5 + 0.5 * lax.erf(f * (0.5**0.5))
        r.act[:, cols] = (f * phi).astype(BF16)
        r.slope[:, cols] = phi + f * (jnp.exp(-0.5 * f * f) * (0.5 / np.pi) ** 0.5)
        return 0

    arrived("i", 0)
    lax.fori_loop(0, FH // FB // 2, ff_forward, 0)
    relay("o", "z", "y", "", 1)
    arrived("i", 1)
    lax.fori_loop(FH // FB // 2, FH // FB, ff_forward, 0)
    relay("o", "y", "c", "z", 0)

    wait("cot")
    r.cots[rows_mine, :] = r.cot[...]
    r.do2[rows_theirs, :] = mm(r.cots[rows_theirs, :], wd[mine, :], NT).astype(BF16)

    def out_grad(b, _):
        at = ff_cols(b)
        go[at, :] = mm(r.act[:, at], r.cots[...], TN).astype(BF16)
        return 0

    lax.fori_loop(0, FH // FB, out_grad, 0)
    scatter("o", "c", "", 0)
    scatter("o", "c", "", 1)
    relay("o", "y", "c", "z", 1)

    def send_o(b):
        own_rows = slice(b * 128, (b + 1) * 128)
        to = pl.ds(pl.multiple_of(x * HW + b * 128, 128), 128)
        push(("o", b), r.ot.at[own_rows, rows_theirs], r.of.at[to, :], at_x)
        r.of[to, :] = r.ot[own_rows, rows_mine]

    r.vg[...] = jnp.zeros_like(r.vg)
    gq = r.gq.reshape(D, 3 * HW)

    def qkv_back(b):
        def one(i, _):
            at = pl.ds(pl.multiple_of(i * QB, QB), QB)
            cols = slice(b * 128, (b + 1) * 128)
            dq = r.dqt[cols, at].T
            out = (
                turn(dq, at, -1.0) * HD**-0.5,
                turn(r.dk[at, cols], at, -1.0),
                r.dv[at, cols],
            )
            for jj in range(3):
                w = out[jj].astype(BF16)
                to = slice(b * 384 + jj * 128, b * 384 + (jj + 1) * 128)
                r.dqkv[at, to] = w
                r.vg[4:5, to] += jnp.sum(w.astype(F32), axis=0, keepdims=True)
            return 0

        lax.fori_loop(0, S // QB, one, 0)
        cols = chunk("q", b)
        for k in range(D // QB):
            gq[k * QB : (k + 1) * QB, cols] = mm(
                r.ha[:, k * QB : (k + 1) * QB], r.dqkv[:, cols], TN
            ).astype(BF16)
        scatter("q", "c", "", b)

    arrived("o", 0)
    arrived("o", 1)
    r.mos[...] = mm(r.act[rows_theirs, :], wo[...]).astype(BF16)
    push("mo", r.mos, r.mor, at_x)
    step("o", "c", "y", "", 0)
    step("o", "c", "y", "", 1)

    def ff_backward(b, _):
        cols = ff_cols(b)
        df = (mm(r.cots[...], wo[cols, :], NT) * r.slope[:, cols]).astype(BF16)
        r.vg[6:7, cols] = jnp.sum(df.astype(F32), axis=0, keepdims=True)
        r.df[:, cols] = df
        gi[:, cols] = mm(r.hmt[...], df).astype(BF16)
        return 0

    lax.fori_loop(0, FH // FB // 2, ff_backward, 0)
    scatter("i", "c", "", 0)
    lax.fori_loop(FH // FB // 2, FH // FB, ff_backward, 0)
    scatter("i", "c", "", 1)
    r.mo[...] = mm(r.act[rows_mine, :], wo[...])

    def dm_rows(i, _):
        at = pl.ds(pl.multiple_of(i * QB, QB), QB)
        dm = mm(r.df[at, :], wi[...], NT)
        r.vg[2:3, 0:D] += jnp.sum(dm * r.n[at, :], axis=0, keepdims=True)
        r.vg[3:4, 0:D] += jnp.sum(dm, axis=0, keepdims=True)
        r.um[at, :] = dm * row(2)
        return 0

    lax.fori_loop(0, S // QB, dm_rows, 0)
    step("i", "c", "y", "", 0)
    step("i", "c", "y", "", 1)
    step("o", "y", "z", "c", 0)
    step("o", "y", "z", "c", 1)

    attend(True, 0, 2)
    send_o(0)
    qkv_back(0)
    step("i", "y", "z", "c", 0)
    step("i", "y", "z", "c", 1)
    attend(True, 2, 4)
    send_o(1)
    half_z = pl.ds(x * (Z // X), Z // X)
    r.gd.reshape(D, D)[mine, :] = mm(r.ot[...], r.cots[...]).astype(BF16)
    gd_part = r.gd.at[half_z, :, :, xo]
    push("gd", gd_part, gd_part, at_x)
    qkv_back(1)

    def dh_rows(base, mine_too):
        def one(i, _):
            at = pl.ds(pl.multiple_of(base + i * QB, QB), QB)
            to = pl.ds(pl.multiple_of(i * QB, QB), QB)
            dh = mm(r.dqkv[at, :], wq[...], NT)
            r.vg[0:1, 0:D] += jnp.sum(dh * r.n[at, :], axis=0, keepdims=True)
            r.vg[1:2, 0:D] += jnp.sum(dh, axis=0, keepdims=True)
            u = dh * row(0) + r.um[at, :]
            if mine_too:
                r.u[to, :] = u
            else:
                r.us[to, :] = u.astype(BF16)
            return 0

        lax.fori_loop(0, T // QB, one, 0)

    dh_rows(xo * T, False)
    push("u", r.us, r.ur, at_x)
    step("q", "c", "y", "", 0)
    step("q", "c", "y", "", 1)
    dh_rows(x * T, True)

    g_sum = jnp.sum(r.cot[...].astype(F32), axis=0, keepdims=True)
    r.vg[5:6, 0:D] = g_sum
    r.vg[7:8, 0:D] = g_sum
    gv2 = r.gv.reshape(N * 8, 128)

    def collapse(v):
        n = lengths(v)
        j = column(v, n)
        pick = (iota((128, n), 0) == j % widths[v]).astype(F32).astype(BF16)
        left = jnp.where(iota((N, n), 0) == j // widths[v], r.vg[v : v + 1, 0:n], 0.0)
        acc = None
        for _ in range(3):
            low = left.astype(BF16)
            part = mm(low, pick, NT)
            acc = part if acc is None else acc + part
            left = left - low.astype(F32)
        gv2[pl.ds(v, N, stride=8), :] = acc

    for v in range(8):
        collapse(v)
    scatter("v", "c", "")
    wait("gd")
    scatter("d", "c", "x")
    step("q", "y", "z", "c", 0)
    step("q", "y", "z", "c", 1)

    def flat(out, width, k=None, part=D):
        per = width // 128
        n = out.shape[0] // per
        lo = 0 if k is None else k * (part // 128)

        def put(acc):
            for j in range(acc.shape[1] // 128):
                out[pl.ds(lo + j, n, stride=per), :] = acc[:, j * 128 : (j + 1) * 128]

        return put

    add_parts("o", "z", "cy", 0, flat(r.oo, D, 0, CH["o"]))
    add_parts("o", "z", "cy", 1, flat(r.oo, D, 1, CH["o"]))
    add_parts("q", "z", "cy", 0)
    add_parts("i", "z", "cy", 0)
    add_parts("i", "z", "cy", 1)
    at_me = (me["z"], me["y"], me["c"])
    push("si", r.gi.at[at_me + (xo,)], r.xi, at_x)
    step("v", "c", "y")
    step("d", "c", "y", "x")

    wait(("o", 0))
    wait(("o", 1))
    wait("mo")
    r.out[...] = (
        r.tokens[...].astype(F32)
        + mm(r.of[...], wd[...], TN)
        + row(5)
        + (r.mo[...] + r.mor[...].astype(F32) + row(7))
    ).astype(BF16)
    step("v", "y", "z", "c")
    step("d", "y", "z", "cx")
    add_parts("q", "z", "cy", 1)
    push("sq", r.gq.at[at_me + (xo,)], r.xq, at_x)
    step("v", "z", "x", "cy")
    add_parts("d", "z", "cyx", None, flat(r.od, D))

    wait("u")

    def final_rows(i, _):
        at = pl.ds(pl.multiple_of(i * RC, RC), RC)
        far = pl.ds(pl.multiple_of(x * T + i * RC, RC), RC)
        u = r.u[at, :] + r.ur[at, :].astype(F32)
        n = r.n[far, :]
        back = u - jnp.mean(u, axis=-1, keepdims=True) - n * jnp.mean(u * n, axis=-1, keepdims=True)
        r.gtok[at, :] = (r.cot[at, :].astype(F32) + back * r.scale[at, 0:1]).astype(BF16)
        return 0

    lax.fori_loop(0, T // RC, final_rows, 0)

    def join(mine_ref, got, out, width, place):
        per = width // 128
        n = out.shape[0] // per
        here = mine_ref[at_me + (x,)].astype(F32)
        there = got[...].astype(F32)
        halves = (jnp.where(x == 0, here, there), jnp.where(x == 0, there, here))

        def piece(b, to_high):
            half, m, odd = place(b)
            v = halves[half][:, m * 128 : (m + 1) * 128]
            return pltpu.roll(v, 64, 1) if odd != to_high else v

        for j in range(per):
            both = jnp.where(lane < 64, piece(2 * j, False), piece(2 * j + 1, True))
            out[pl.ds(j, n, stride=per), :] = both

    def place_q(b):
        h, jj = b // 3, b % 3
        return h // HC, (h % HC) // 2 * 3 + jj, h % 2 == 1

    def place_i(b):
        return b % 2, b // 4, (b // 2) % 2 == 1

    wait("si")
    join(r.gi, r.xi, r.oi, FF, place_i)
    wait("sq")
    join(r.gq, r.xq, r.oq, 3 * D, place_q)

    def put_vec(acc):
        r.ov[...] = acc

    add_parts("v", "x", "cyz", None, put_vec)


def rope_table(length):
    lanes = np.arange(128) % HD
    rot = HD // 4
    inverse = np.where(lanes < rot, 1.0 / ROPE_BASE ** (2.0 * (lanes % (rot // 2)) / rot), 0.0)
    high = 32.0 * np.arange(length // 32)[:, None] * inverse
    low = np.arange(32)[:, None] * inverse
    return np.stack([np.cos(high), np.sin(high), np.cos(low), np.sin(low)]).astype(np.float32)


def hand_over(*refs):
    for src, dst in zip(refs[:6], refs[7:13]):
        dst[...] = src[...]
    for v, dst in enumerate(refs[13:]):
        dst[...] = refs[6][v : v + 1, 0 : dst.shape[1]]


def layer(sizes, tokens, cotangent, *params):
    Z, Y, C, X = (sizes[a] for a in AX)
    N = Z * Y * C * X
    T = tokens.shape[1]
    S = T * X
    HW = HEADS // X * HD
    vectors = [params[i] for i in (0, 1, 2, 3, 5, 7, 9, 11)]
    weights = [params[i] for i in (4, 6, 8, 10)]
    flats = [w.reshape(-1, 128) for w in weights]
    full = dict(z=Z, y=Y, c=C, x=X)

    FH = FF // X

    def parts(name, axis, done, slab, dtype):
        free = [full[a] for a in AX if a not in done and a != axis and (a != "x" or name != "o")]
        return pltpu.VMEM((full[axis] - 1, *free, *slab), dtype)

    slabs = {
        "q": (D // N, 3 * HW),
        "d": (D // N, D),
        "i": (D // N, FH),
        "o": (FF // N, D),
        "v": (8, 128),
    }
    orders = {"q": "cyz", "d": "cyz", "i": "cyz", "o": "cyz", "v": "cyzx"}
    keep = types.SimpleNamespace()
    scratch = vars(keep)
    for k, slab in slabs.items():
        kind = F32 if k == "v" else BF16
        devs = (Z, Y, C) if k == "o" else (Z, Y, C, X)
        scratch["w" + k] = pltpu.VMEM((*devs, *slab), kind)
        scratch["g" + k] = pltpu.VMEM((*devs, *slab), kind)
        for n, axis in enumerate(orders[k]):
            done = orders[k][:n] + ("x" if k == "d" else "")
            scratch["r" + k + axis] = parts(k, axis, done, slab, kind)
    keep.xq = pltpu.VMEM(slabs["q"], BF16)
    keep.xi = pltpu.VMEM(slabs["i"], BF16)
    keep.sq = pltpu.VMEM((X, *slabs["q"]), BF16)
    keep.si = pltpu.VMEM((X, *slabs["i"]), BF16)
    keep.tmp = pltpu.VMEM((max(f.shape[0] for f in flats), 128), F32)
    keep.cos = keep.sinl = keep.sinh = pltpu.VMEM((S, 128), F32)
    keep.tok2 = pltpu.VMEM((T, D), BF16)
    keep.cots = pltpu.VMEM((S, D), BF16)
    keep.n = pltpu.VMEM((S, D), F32)
    keep.scale = pltpu.VMEM((T, 128), F32)
    keep.vrow = pltpu.VMEM((8, FH), F32)
    keep.vg = pltpu.VMEM((8, FH), F32)
    keep.ha = keep.hm = pltpu.VMEM((S, D), BF16)
    keep.hmt = pltpu.VMEM((D, S), BF16)
    keep.q = keep.k = keep.v = keep.do2 = pltpu.VMEM((S, HW), BF16)
    keep.kt = keep.vt = keep.ot = pltpu.VMEM((HW, S), BF16)
    keep.dqt = pltpu.VMEM((HW, S), F32)
    keep.dk = pltpu.VMEM((S, HW), F32)
    keep.dv = pltpu.VMEM((S, HW), F32)
    keep.st = pltpu.VMEM((S // QB, QB, QB), F32)
    keep.dp = pltpu.VMEM((S // QB, QB, QB), F32)
    keep.pb = pltpu.VMEM((S, QB), BF16)
    keep.ds = pltpu.VMEM((S, QB), BF16)
    keep.dqkv = pltpu.VMEM((S, 3 * HW), BF16)
    keep.of = pltpu.VMEM((D, T), BF16)
    keep.act = keep.df = pltpu.VMEM((S, FH), BF16)
    keep.slope = pltpu.VMEM((S, FH), F32)
    keep.um = pltpu.VMEM((S, D), F32)
    keep.u = keep.mo = pltpu.VMEM((T, D), F32)
    keep.us = keep.ur = keep.mos = keep.mor = pltpu.VMEM((T, D), BF16)
    copies = 128
    keep.send = pltpu.SemaphoreType.DMA((copies,))
    keep.recv = pltpu.SemaphoreType.DMA((copies,))
    ins = "tokens cot fq fd".split() + "fi fo rope".split() + ["v%d" % v for v in range(8)]
    outs = dict(
        out=jax.ShapeDtypeStruct((T, D), BF16),
        gtok=jax.ShapeDtypeStruct((T, D), BF16),
        oq=jax.ShapeDtypeStruct(flats[0].shape, F32),
        od=jax.ShapeDtypeStruct(flats[1].shape, F32),
        oi=jax.ShapeDtypeStruct(flats[2].shape, F32),
        oo=jax.ShapeDtypeStruct(flats[3].shape, F32),
        ov=jax.ShapeDtypeStruct((8, 128), F32),
    )
    vmem = pl.BlockSpec(memory_space=pltpu.VMEM)
    names = ins + list(outs) + list(scratch)
    out, gtok, gq, gd, gi, go, gv = pl.pallas_call(
        functools.partial(fused, sizes, names),
        out_shape=list(outs.values()),
        in_specs=[vmem] * len(ins),
        out_specs=[vmem] * len(outs),
        scratch_shapes=list(scratch.values()),
        compiler_params=pltpu.CompilerParams(
            collective_id=0, has_side_effects=True, vmem_limit_bytes=67043328
        ),
        name="layer",
    )(
        tokens.reshape(T, D),
        cotangent.reshape(T, D),
        *flats,
        jnp.asarray(rope_table(S)),
        *[v.reshape(1, -1) for v in vectors],
    )
    shapes = [jax.ShapeDtypeStruct(a.shape, a.dtype) for a in (out, gtok, gq, gd, gi, go)]
    shapes += [jax.ShapeDtypeStruct((1, p.shape[0]), F32) for p in vectors]
    out, gtok, gq, gd, gi, go, *v = pl.pallas_call(
        hand_over,
        out_shape=shapes,
        in_specs=[vmem] * 7,
        out_specs=[vmem] * len(shapes),
        name="results",
    )(out, gtok, gq, gd, gi, go, gv)
    v = [a.reshape(-1) for a in v]
    return (
        out.reshape(tokens.shape),
        gtok.reshape(tokens.shape),
        v[0],
        v[1],
        v[2],
        v[3],
        gq.reshape(-1),
        v[4],
        gd.reshape(-1),
        v[5],
        gi.reshape(-1),
        v[6],
        go.reshape(-1),
        v[7],
    )


def solution(mesh):
    n_seq, n_ctx = mesh.shape["seq"], mesh.shape["ctx"]
    if n_ctx != 2 or n_seq % 8 or (D // (n_seq * n_ctx)) % 16:
        return general(mesh)
    sizes = {"z": n_seq // 4, "y": 2, "c": 2, "x": n_ctx}
    flat = P(("seq", "ctx"))
    rows = P("seq", "ctx", None)
    return jax.shard_map(
        functools.partial(layer, sizes),
        mesh=mesh,
        in_specs=(rows, rows) + (flat,) * 12,
        out_specs=(rows, rows) + (flat,) * 12,
        check_vma=False,
    )
```

```python
import functools
import types

import jax
import jax.numpy as jnp
import numpy as np
from jax import lax
from jax.experimental import pallas as pl
from jax.experimental.pallas import tpu as pltpu
from jax.sharding import PartitionSpec as P

D = 512
HEADS = 8
FF = 2048


EPS = 1e-05
BOTH = ("seq", "ctx")
ROPE_BASE = 10000.0
NEG = -1e30


def layer_normalize(values, gain, bias):
    mean = jnp.mean(values, axis=-1, keepdims=True)
    centered = values - mean
    var = jnp.mean(centered * centered, axis=-1, keepdims=True)
    return centered * lax.rsqrt(var + EPS) * gain + bias


def rotate(values, cosine, sine):
    width = cosine.shape[-1]
    half = width // 2
    part = values[..., :width]
    turned = jnp.concatenate([-part[..., half:], part[..., :half]], axis=-1)
    return jnp.concatenate([part * cosine + turned * sine, values[..., width:]], axis=-1)


def gelu_exact(values):
    return jax.nn.gelu(values, approximate=False)


def matrices(mix_flat, proj_flat, expand_flat, reduce_flat):
    return (
        mix_flat.reshape(D, 3 * D),
        proj_flat.reshape(D, D),
        expand_flat.reshape(D, FF),
        reduce_flat.reshape(FF, D),
    )


def body(
    tokens,
    cotangent,
    attn_norm_gain,
    attn_norm_bias,
    mlp_norm_gain,
    mlp_norm_bias,
    qkv_weight,
    qkv_bias,
    dense_weight,
    dense_bias,
    fc_in_weight,
    fc_in_bias,
    fc_out_weight,
    fc_out_bias,
):
    (
        gain_attn,
        attention_shift,
        gain_mlp,
        shift_mlp,
        mix_flat,
        mix_bias,
        proj_flat,
        proj_bias,
        expand_flat,
        expand_bias,
        reduce_flat,
        reduce_bias,
    ) = (
        lax.all_gather(attn_norm_gain, BOTH, axis=0, tiled=True),
        lax.all_gather(attn_norm_bias, BOTH, axis=0, tiled=True),
        lax.all_gather(mlp_norm_gain, BOTH, axis=0, tiled=True),
        lax.all_gather(mlp_norm_bias, BOTH, axis=0, tiled=True),
        lax.all_gather(qkv_weight, BOTH, axis=0, tiled=True),
        lax.all_gather(qkv_bias, BOTH, axis=0, tiled=True),
        lax.all_gather(dense_weight, BOTH, axis=0, tiled=True),
        lax.all_gather(dense_bias, BOTH, axis=0, tiled=True),
        lax.all_gather(fc_in_weight, BOTH, axis=0, tiled=True),
        lax.all_gather(fc_in_bias, BOTH, axis=0, tiled=True),
        lax.all_gather(fc_out_weight, BOTH, axis=0, tiled=True),
        lax.all_gather(fc_out_bias, BOTH, axis=0, tiled=True),
    )
    mix_weight, proj_weight, expand_weight, reduce_weight = matrices(
        mix_flat, proj_flat, expand_flat, reduce_flat
    )
    shape = tokens.shape
    group = shape[1]
    width = shape[2]
    heads = HEADS
    head_dim = width // heads
    rows = tokens.reshape(group, width).astype(jnp.float32)
    attn_in, attn_norm_back = jax.vjp(
        layer_normalize, rows, gain_attn.astype(jnp.float32), attention_shift.astype(jnp.float32)
    )
    mlp_in, mlp_norm_back = jax.vjp(
        layer_normalize, rows, gain_mlp.astype(jnp.float32), shift_mlp.astype(jnp.float32)
    )
    attn_low = attn_in.astype(jnp.bfloat16)
    mlp_low = mlp_in.astype(jnp.bfloat16)
    mixed = jnp.dot(attn_low, mix_weight, preferred_element_type=jnp.float32) + mix_bias.astype(
        jnp.float32
    )
    mixed = mixed.reshape(group, heads, 3, head_dim)
    place = lax.axis_index("ctx")
    blocks_total = lax.axis_size("ctx")
    local_pos = jnp.arange(group, dtype=jnp.int32)
    query_pos = place * group + local_pos
    rot_dims = head_dim // 4
    inverse = 1.0 / ROPE_BASE ** (
        jnp.arange(0, rot_dims, 2, dtype=jnp.int32).astype(jnp.float32) / rot_dims
    )
    angles = query_pos.astype(jnp.float32)[:, None] * inverse[None, :]
    angles = jnp.concatenate([angles, angles], axis=-1)
    cosine = jnp.cos(angles)[:, None, :]
    sine = jnp.sin(angles)[:, None, :]
    scale = head_dim ** (-0.5)

    def turn(query_unrotated, key_raw):
        return (rotate(query_unrotated, cosine, sine) * scale, rotate(key_raw, cosine, sine))

    (query_f, key_f), turn_back = jax.vjp(turn, mixed[:, :, 0], mixed[:, :, 1])
    query = query_f.astype(jnp.bfloat16)
    key_own = key_f.astype(jnp.bfloat16).reshape(group, width)
    value_own = mixed[:, :, 2].astype(jnp.bfloat16).reshape(group, width)
    all_keys, all_values = (
        lax.all_gather(key_own, "ctx", axis=0, tiled=True),
        lax.all_gather(value_own, "ctx", axis=0, tiled=True),
    )
    count = place + 1

    def block(index):
        keys = lax.dynamic_slice_in_dim(all_keys, index * group, group, 0).reshape(
            group, heads, head_dim
        )
        values = lax.dynamic_slice_in_dim(all_values, index * group, group, 0).reshape(
            group, heads, head_dim
        )
        scores = jnp.einsum("qhd,khd->hqk", query, keys, preferred_element_type=jnp.float32)
        allowed = (index * group + local_pos)[None, :] <= query_pos[:, None]
        return (keys, values, scores, allowed[None])

    def max_step(index, carry):
        top, total = carry
        _, _, scores, allowed = block(index)
        new_top = jnp.maximum(top, jnp.max(jnp.where(allowed, scores, NEG), axis=-1))
        terms = jnp.where(allowed, jnp.exp(scores - new_top[:, :, None]), 0.0)
        return (new_top, total * jnp.exp(top - new_top) + jnp.sum(terms, axis=-1))

    start = (jnp.full((heads, group), NEG, jnp.float32), jnp.zeros((heads, group), jnp.float32))
    top, total = lax.fori_loop(0, count, max_step, start)
    log_total = top + jnp.log(total)

    def probs_of(scores, allowed):
        return jnp.where(allowed, jnp.exp(scores - log_total[:, :, None]), 0.0)

    def out_step(index, acc):
        _, values, scores, allowed = block(index)
        probs = probs_of(scores, allowed).astype(jnp.bfloat16)
        return acc + jnp.einsum("hqk,khd->qhd", probs, values, preferred_element_type=jnp.float32)

    heads_out = lax.fori_loop(0, count, out_step, jnp.zeros((group, heads, head_dim), jnp.float32))
    attn_out = heads_out.reshape(group, width).astype(jnp.bfloat16)
    branch_attn = jnp.dot(
        attn_out, proj_weight, preferred_element_type=jnp.float32
    ) + proj_bias.astype(jnp.float32)
    expand = jnp.dot(
        mlp_low, expand_weight, preferred_element_type=jnp.float32
    ) + expand_bias.astype(jnp.float32)
    active_rows, active_back = jax.vjp(gelu_exact, expand)
    active_low = active_rows.astype(jnp.bfloat16)
    branch_mlp = jnp.dot(
        active_low, reduce_weight, preferred_element_type=jnp.float32
    ) + reduce_bias.astype(jnp.float32)
    layer_out = (rows + branch_attn + branch_mlp).astype(jnp.bfloat16).reshape(shape)
    back_mix, back_proj, back_expand, back_reduce = (
        lax.all_gather(qkv_weight, BOTH, axis=0, tiled=True),
        lax.all_gather(dense_weight, BOTH, axis=0, tiled=True),
        lax.all_gather(fc_in_weight, BOTH, axis=0, tiled=True),
        lax.all_gather(fc_out_weight, BOTH, axis=0, tiled=True),
    )
    back_mix, back_proj, back_expand, back_reduce = matrices(
        back_mix, back_proj, back_expand, back_reduce
    )
    grad_rows = cotangent.reshape(group, width)
    grad_float = grad_rows.astype(jnp.float32)
    grad_reduce = jnp.einsum("tf,td->fd", active_low, grad_rows, preferred_element_type=jnp.float32)
    grad_out_bias = jnp.sum(grad_float, axis=0)
    grad_proj = jnp.einsum("te,td->ed", attn_out, grad_rows, preferred_element_type=jnp.float32)
    grad_active = jnp.einsum(
        "td,fd->tf", grad_rows, back_reduce, preferred_element_type=jnp.float32
    )
    grad_expand = active_back(grad_active)[0].astype(jnp.bfloat16)
    grad_expand_w = jnp.einsum(
        "td,tf->df", mlp_low, grad_expand, preferred_element_type=jnp.float32
    )
    grad_expand_b = jnp.sum(grad_expand.astype(jnp.float32), axis=0)
    grad_mlp_in = jnp.einsum(
        "tf,df->td", grad_expand, back_expand, preferred_element_type=jnp.float32
    )
    grad_heads = jnp.einsum("td,ed->te", grad_rows, back_proj, preferred_element_type=jnp.float32)
    grad_heads = grad_heads.astype(jnp.bfloat16).reshape(group, heads, head_dim)

    def delta_step(index, acc):
        _, values, scores, allowed = block(index)
        probs = probs_of(scores, allowed)
        grad_probs = jnp.einsum(
            "qhd,khd->hqk", grad_heads, values, preferred_element_type=jnp.float32
        )
        return acc + jnp.sum(probs * grad_probs, axis=-1)

    delta = lax.fori_loop(0, count, delta_step, jnp.zeros((heads, group), jnp.float32))

    def query_step(index, grad_query):
        keys, values, scores, allowed = block(index)
        probs = probs_of(scores, allowed)
        grad_probs = jnp.einsum(
            "qhd,khd->hqk", grad_heads, values, preferred_element_type=jnp.float32
        )
        grad_scores = (probs * (grad_probs - delta[:, :, None])).astype(jnp.bfloat16)
        return grad_query + jnp.einsum(
            "hqk,khd->qhd", grad_scores, keys, preferred_element_type=jnp.float32
        )

    grad_query = lax.fori_loop(
        0, count, query_step, jnp.zeros((group, heads, head_dim), jnp.float32)
    )
    all_queries, all_grad_heads = (
        lax.all_gather(query.reshape(group, width), "ctx", axis=0, tiled=True),
        lax.all_gather(grad_heads.reshape(group, width), "ctx", axis=0, tiled=True),
    )
    gathered_log_sums, all_delta = (
        lax.all_gather(jnp.transpose(log_total), "ctx", axis=0, tiled=True),
        lax.all_gather(jnp.transpose(delta), "ctx", axis=0, tiled=True),
    )
    keys_mine = key_own.reshape(group, heads, head_dim)
    values_mine = value_own.reshape(group, heads, head_dim)

    def owner_step(index, carry):
        key_acc, value_accumulator = carry
        queries = lax.dynamic_slice_in_dim(all_queries, index * group, group, 0).reshape(
            group, heads, head_dim
        )
        outer_grads = lax.dynamic_slice_in_dim(all_grad_heads, index * group, group, 0).reshape(
            group, heads, head_dim
        )
        lse_rows = jnp.transpose(
            lax.dynamic_slice_in_dim(gathered_log_sums, index * group, group, 0)
        )
        delta_rows = jnp.transpose(lax.dynamic_slice_in_dim(all_delta, index * group, group, 0))
        scores = jnp.einsum("qhd,khd->hqk", queries, keys_mine, preferred_element_type=jnp.float32)
        allowed = (query_pos[None, :] <= (index * group + local_pos)[:, None])[None]
        probs = jnp.where(allowed, jnp.exp(scores - lse_rows[:, :, None]), 0.0)
        grad_probs = jnp.einsum(
            "qhd,khd->hqk", outer_grads, values_mine, preferred_element_type=jnp.float32
        )
        grad_scores = (probs * (grad_probs - delta_rows[:, :, None])).astype(jnp.bfloat16)
        key_acc = key_acc + jnp.einsum(
            "hqk,qhd->khd", grad_scores, queries, preferred_element_type=jnp.float32
        )
        value_accumulator = value_accumulator + jnp.einsum(
            "hqk,qhd->khd",
            probs.astype(jnp.bfloat16),
            outer_grads,
            preferred_element_type=jnp.float32,
        )
        return (key_acc, value_accumulator)

    empty_heads = jnp.zeros((group, heads, head_dim), jnp.float32)
    own_key_grad, own_value_grad = lax.fori_loop(
        place, blocks_total, owner_step, (empty_heads, empty_heads)
    )
    grad_query_raw, grad_key_raw = turn_back((grad_query, own_key_grad))
    grad_mixed = jnp.stack([grad_query_raw, grad_key_raw, own_value_grad], axis=2)
    grad_mixed = grad_mixed.reshape(group, 3 * width).astype(jnp.bfloat16)
    grad_mix_w = jnp.einsum("td,te->de", attn_low, grad_mixed, preferred_element_type=jnp.float32)
    grad_mix_b = jnp.sum(grad_mixed.astype(jnp.float32), axis=0)
    grad_attn_in = jnp.einsum("te,de->td", grad_mixed, back_mix, preferred_element_type=jnp.float32)
    input_attn, gain_attn_grad, shift_attn_grad = attn_norm_back(grad_attn_in)
    input_mlp, gain_mlp_grad, shift_mlp_grad = mlp_norm_back(grad_mlp_in)
    grad_tokens = (grad_float + input_attn + input_mlp).astype(jnp.bfloat16).reshape(shape)
    sums = (
        lax.psum_scatter(gain_attn_grad, BOTH, scatter_dimension=0, tiled=True),
        lax.psum_scatter(shift_attn_grad, BOTH, scatter_dimension=0, tiled=True),
        lax.psum_scatter(gain_mlp_grad, BOTH, scatter_dimension=0, tiled=True),
        lax.psum_scatter(shift_mlp_grad, BOTH, scatter_dimension=0, tiled=True),
        lax.psum_scatter(grad_mix_w.reshape(-1), BOTH, scatter_dimension=0, tiled=True),
        lax.psum_scatter(grad_mix_b, BOTH, scatter_dimension=0, tiled=True),
        lax.psum_scatter(grad_proj.reshape(-1), BOTH, scatter_dimension=0, tiled=True),
        lax.psum_scatter(grad_out_bias, BOTH, scatter_dimension=0, tiled=True),
        lax.psum_scatter(
            grad_expand_w.reshape(-1), BOTH, scatter_dimension=0, tiled=True
        ),
        lax.psum_scatter(grad_expand_b, BOTH, scatter_dimension=0, tiled=True),
        lax.psum_scatter(grad_reduce.reshape(-1), BOTH, scatter_dimension=0, tiled=True),
        lax.psum_scatter(grad_out_bias, BOTH, scatter_dimension=0, tiled=True),
    )
    return (
        layer_out,
        grad_tokens,
        sums[0],
        sums[1],
        sums[2],
        sums[3],
        sums[4],
        sums[5],
        sums[6],
        sums[7],
        sums[8],
        sums[9],
        sums[10],
        sums[11],
    )


def general(mesh):
    return jax.shard_map(
        body,
        mesh=mesh,
        in_specs=(
            P("seq", "ctx", None),
            P("seq", "ctx", None),
            P(BOTH),
            P(BOTH),
            P(BOTH),
            P(BOTH),
            P(BOTH),
            P(BOTH),
            P(BOTH),
            P(BOTH),
            P(BOTH),
            P(BOTH),
            P(BOTH),
            P(BOTH),
        ),
        out_specs=(
            P("seq", "ctx", None),
            P("seq", "ctx", None),
            P(BOTH),
            P(BOTH),
            P(BOTH),
            P(BOTH),
            P(BOTH),
            P(BOTH),
            P(BOTH),
            P(BOTH),
            P(BOTH),
            P(BOTH),
            P(BOTH),
            P(BOTH),
        ),
        check_vma=False,
    )


MESH = pl.DeviceIdType.MESH
F32, BF16 = jnp.float32, jnp.bfloat16
HD = D // HEADS
AX = "zycx"
NN = (((1,), (0,)), ((), ()))
NT = (((1,), (1,)), ((), ()))
TN = (((0,), (0,)), ((), ()))
QB = 256


def mm(a, b, dims=NN):
    return lax.dot_general(a, b, dims, preferred_element_type=F32)


def iota(shape, dim):
    return lax.broadcasted_iota(jnp.int32, shape, dim)


def fused(sizes, names, *refs):
    held = dict(zip(names, refs))
    r = types.SimpleNamespace(**held)
    X = sizes["x"]
    C = sizes["c"]
    Y = sizes["y"]
    Z = sizes["z"]
    N = Z * Y * C * X
    T = r.tokens.shape[0]
    S = T * X
    HC = HEADS // X
    HW = HC * HD
    FH = FF // X
    CH = dict(q=384, i=FH // 2, o=D // 2)
    s = lax.axis_index("seq")
    me = {"x": lax.axis_index("ctx"), "c": s % C, "y": (s // C) % Y, "z": s // (C * Y)}
    x = me["x"]
    xo = 1 - x

    def device(at):
        return ((at["z"] * Y + at["y"]) * C + at["c"], at["x"])

    def others(axis):
        n = sizes[axis]
        return [dict(me, **{axis: (me[axis] + d) % n}) for d in range(1, n)]

    flight = {}
    count = [0]

    def push(key, src, dst, at):
        k = count[0]
        count[0] += 1
        cp = pltpu.make_async_remote_copy(
            src_ref=src,
            dst_ref=dst,
            send_sem=r.send.at[k],
            recv_sem=r.recv.at[k],
            device_id=device(at),
            device_id_type=MESH,
        )
        cp.start()
        flight.setdefault(key, []).append(cp)

    def wait(key):
        for cp in flight.pop(key):
            cp.wait()

    def axes(name):
        return AX[: 3 if name == "o" else 4]

    def chunk(name, k):
        if k is None:
            return slice(None)
        w = CH[name]
        return slice(k * w, (k + 1) * w)

    def gather(name, axis, known, k=None):
        ref = held["w" + name]
        spot = tuple(slice(None) if a in known else me[a] for a in axes(name))
        part = ref.at[spot + (slice(None), chunk(name, k))]
        for at in others(axis):
            push(("w", name, axis, k), part, part, at)

    def relay(name, axis, nxt, known, k=None):
        wait(("w", name, axis, k))
        gather(name, nxt, known + axis, k)

    def arrived(name, k=None):
        wait(("w", name, "c", k))

    def scatter(name, axis, done, k=None):
        ref, got = held["g" + name], held["r" + name + axis]
        free = [a for a in axes(name) if a not in done and a != axis]
        cols = (slice(None), chunk(name, k))
        for n, at in enumerate(others(axis)):
            spot = tuple(slice(None) if a in free else at[a] for a in axes(name))
            to = (n,) + (slice(None),) * len(free)
            push(("g", name, axis, k), ref.at[spot + cols], got.at[to + cols], at)

    def add_parts(name, axis, done, k=None, finish=None):
        wait(("g", name, axis, k))
        ref, got = held["g" + name], held["r" + name + axis]
        free = [a for a in axes(name) if a not in done and a != axis]
        cols = (slice(None), chunk(name, k))
        total = 1
        for a in free:
            total *= sizes[a]

        def one(i, _):
            at, rest = dict(me), i
            for a in reversed(free):
                at[a] = rest % sizes[a]
                rest = rest // sizes[a]
            spot = tuple(at[a] for a in axes(name))
            inner = tuple(at[a] for a in free)
            acc = ref[spot + cols].astype(F32)
            for n in range(sizes[axis] - 1):
                acc = acc + got[(n,) + inner + cols].astype(F32)
            if finish is None:
                ref[spot + cols] = acc.astype(ref.dtype)
            else:
                finish(acc)
            return 0

        if total == 1:
            one(0, 0)
        else:
            lax.fori_loop(0, total, one, 0)

    def step(name, axis, nxt, done="", k=None):
        add_parts(name, axis, done, k)
        scatter(name, nxt, done + axis, k)

    barrier = pltpu.get_barrier_semaphore()
    greet = [at for a in AX for at in others(a)]
    for at in greet:
        pl.semaphore_signal(barrier, inc=1, device_id=device(at), device_id_type=MESH)

    tmp = r.tmp
    lane = iota((1, 128), 1)

    def own(name):
        return held[name].at[me["z"], me["y"], me["c"], x]

    def block64(b, per, rows, to_high):
        v = tmp[pl.ds(b // 2, rows, stride=per), :]
        return pltpu.roll(v, 64, 1) if (b % 2 == 1) != to_high else v

    def split(src, dst, width, table):
        n = held[src].shape[0]
        per = width // 128
        tmp[0:n, :] = held[src][...].astype(F32)
        for half in range(X):
            for m in range(per // X):
                low, high = table(half, m)
                low = block64(low, per, n // per, False)
                high = block64(high, per, n // per, True)
                dst[half, :, m * 128 : (m + 1) * 128] = jnp.where(lane < 64, low, high).astype(BF16)

    def table_q(half, m):
        h0 = half * HC + 2 * (m // 3)
        return 3 * h0 + m % 3, 3 * (h0 + 1) + m % 3

    def table_i(half, m):
        return 4 * m + half, 4 * m + 2 + half

    def reshard(src, dst, width):
        n = held[src].shape[0]
        k = width // 128
        tmp[0:n, :] = held[src][...].astype(F32)
        for j in range(k):
            dst[:, j * 128 : (j + 1) * 128] = tmp[pl.ds(j, n // k, stride=k), :].astype(BF16)

    split("fq", r.sq, 3 * D, table_q)
    split("fi", r.si, FF, table_i)
    reshard("fd", own("wd"), D)
    vecs = own("wv")
    vecs[...] = jnp.zeros_like(vecs)
    for v in range(8):
        vin = held["v%d" % v]
        vecs[v : v + 1, 0 : vin.shape[1]] = vin[...].astype(F32)
    own("wq")[...] = r.sq[x]
    own("wi")[...] = r.si[x]

    pl.semaphore_wait(barrier, len(greet))

    rows_mine = pl.ds(pl.multiple_of(x * T, T), T)
    rows_theirs = pl.ds(pl.multiple_of(xo * T, T), T)
    at_x = others("x")[0]
    gather("v", "x", "")
    push("sq", r.sq.at[xo], own("wq"), at_x)
    push("si", r.si.at[xo], own("wi"), at_x)
    gather("d", "x", "")
    push("tok", r.tokens, r.tok2, at_x)
    push("cot", r.cot, r.cots.at[rows_mine, :], at_x)
    reshard("fo", r.wo.at[me["z"], me["y"], me["c"]], D)

    rope = r.rope
    mod = lane % HD

    def rope_rows(i, _):
        ch, sh = rope[0, pl.ds(i, 1), :], rope[1, pl.ds(i, 1), :]
        cl, sl = rope[2], rope[3]
        sine = sh * cl + ch * sl
        at = pl.ds(pl.multiple_of(i * 32, 32), 32)
        r.cos[at, :] = ch * cl - sh * sl
        r.sinl[at, :] = jnp.where(mod < 8, -sine, 0.0)
        r.sinh[at, :] = jnp.where(mod < 8, 0.0, sine)
        return 0

    def turn(u, at, sign):
        return (
            u * r.cos[at, :]
            + sign * (pltpu.roll(u, 120, 1) * r.sinl[at, :] + pltpu.roll(u, 8, 1) * r.sinh[at, :])
        )

    relay("v", "x", "z", "")
    wait("sq")
    gather("q", "z", "x", 0)
    gather("q", "z", "x", 1)
    relay("d", "x", "z", "")
    wait("si")
    gather("i", "z", "x", 0)
    gather("i", "z", "x", 1)
    gather("o", "z", "", 0)
    gather("o", "z", "", 1)
    lax.fori_loop(0, S // 32, rope_rows, 0)

    RC = 128

    def norm_rows(src, base, keep):
        def one(i, _):
            v = src[pl.ds(pl.multiple_of(i * RC, RC), RC), :].astype(F32)
            c = v - jnp.mean(v, axis=-1, keepdims=True)
            scale = lax.rsqrt(jnp.mean(c * c, axis=-1, keepdims=True) + EPS)
            r.n[pl.ds(pl.multiple_of(base + i * RC, RC), RC), :] = c * scale
            if keep:
                r.scale[pl.ds(pl.multiple_of(i * RC, RC), RC), :] = jnp.broadcast_to(scale, (RC, 128))
            return 0

        lax.fori_loop(0, T // RC, one, 0)

    norm_rows(r.tokens, x * T, True)

    relay("v", "z", "y", "x")
    relay("q", "z", "y", "x", 0)
    relay("v", "y", "c", "xz")
    relay("q", "z", "y", "x", 1)
    arrived("v")

    widths = [D // N, D // N, D // N, D // N, 3 * D // N, D // N, FF // N, D // N]

    def column(v, n):
        j = iota((1, n), 1)
        if v == 4:
            head_at = x * HC + 2 * (j // 384) + (j % 128) // HD
            return head_at * (3 * HD) + ((j % 384) // 128) * HD + j % HD
        if v == 6:
            return (j // 64) * 128 + x * 64 + j % 64
        return j

    def lengths(v):
        return {4: 3 * HW, 6: FH}.get(v, D)

    vec2 = r.wv.reshape(N * 8, 128)

    def expand(v):
        n = lengths(v)
        j = column(v, n)
        pick = (iota((128, n), 0) == j % widths[v]).astype(F32).astype(BF16)
        rows_v = vec2[pl.ds(v, N, stride=8), :].astype(BF16)
        spread = mm(rows_v, pick)
        r.vrow[v : v + 1, 0:n] = jnp.sum(
            jnp.where(iota((N, n), 0) == j // widths[v], spread, 0.0), axis=0, keepdims=True
        )

    for v in range(8):
        expand(v)

    def row(v, n=D, off=0):
        return r.vrow[v : v + 1, off : off + n]

    def affine_attn(base):
        def one(i, _):
            at = pl.ds(pl.multiple_of(base + i * RC, RC), RC)
            r.ha[at, :] = (r.n[at, :] * row(0) + row(1)).astype(BF16)
            return 0

        lax.fori_loop(0, T // RC, one, 0)

    def affine_mlp(base):
        def one(i, _):
            at = pl.ds(pl.multiple_of(base + i * RC, RC), RC)
            r.hm[at, :] = (r.n[at, :] * row(2) + row(3)).astype(BF16)
            return 0

        lax.fori_loop(0, T // RC, one, 0)

    affine_attn(x * T)
    relay("d", "z", "y", "x")
    relay("q", "y", "c", "xz", 0)
    affine_mlp(x * T)
    relay("q", "y", "c", "xz", 1)

    wait("tok")
    norm_rows(r.tok2, xo * T, False)
    affine_attn(xo * T)
    affine_mlp(xo * T)
    relay("i", "z", "y", "x", 0)
    relay("d", "y", "c", "xz")

    wq = r.wq.reshape(D, 3 * HW)

    def qkv(b):
        def one(i, _):
            at = pl.ds(pl.multiple_of(i * QB, QB), QB)
            u = mm(r.ha[at, :], wq[:, chunk("q", b)]) + row(4, 384, b * 384)
            for jj, name in enumerate("qkv"):
                w = u[:, jj * 128 : (jj + 1) * 128]
                if jj < 2:
                    w = turn(w, at, 1.0)
                if jj == 0:
                    w = w * HD**-0.5
                w = w.astype(BF16)
                held[name][at, b * 128 : (b + 1) * 128] = w
                if jj >= 1:
                    held[name + "t"][b * 128 : (b + 1) * 128, at] = w.T
            return 0

        arrived("q", b)
        lax.fori_loop(0, S // QB, one, 0)

    qkv(0)
    relay("i", "z", "y", "x", 1)
    qkv(1)
    arrived("d")
    wd = r.wd.reshape(D, D)
    mine = pl.ds(pl.multiple_of(x * HW, HW), HW)
    r.do2[rows_mine, :] = mm(r.cot[...], wd[mine, :], NT).astype(BF16)

    r.dk[...] = jnp.zeros_like(r.dk)
    r.dv[...] = jnp.zeros_like(r.dv)
    causal = iota((QB, QB), 0) <= iota((QB, QB), 1)

    def head(blocks, h, _):
        lanes = pl.ds(pl.multiple_of((h // 2) * 128, 128), 128)
        ours = (lane // HD) == h % 2
        head_rows = pl.ds(pl.multiple_of(h * HD, HD), HD)
        for i in blocks:
            here = slice(i * QB, (i + 1) * QB)
            qm = jnp.where(ours, r.q[here, lanes], jnp.zeros((), BF16))
            dom = jnp.where(ours, r.do2[here, lanes], jnp.zeros((), BF16))
            top = None
            for j in range(i + 1):
                st = mm(r.k[j * QB : (j + 1) * QB, lanes], qm, NT)
                if j == i:
                    st = jnp.where(causal, st, NEG)
                r.st[j] = st
                part = jnp.max(st, axis=0, keepdims=True)
                top = part if top is None else jnp.maximum(top, part)
            total = du = None
            for j in range(i + 1):
                e = jnp.exp(r.st[j] - top)
                r.st[j] = e
                dp = mm(r.v[j * QB : (j + 1) * QB, lanes], dom, NT)
                r.dp[j] = dp
                part, both = (jnp.sum(w, axis=0, keepdims=True) for w in (e, e * dp))
                total = part if total is None else total + part
                du = both if du is None else du + both
            scale = 1.0 / total
            delta = du * scale
            for j in range(i + 1):
                p = r.st[j] * scale
                r.pb[j * QB : (j + 1) * QB, :] = p.astype(BF16)
                ds = p * (r.dp[j] - delta)
                r.ds[j * QB : (j + 1) * QB, :] = ds.astype(BF16)
            n = (i + 1) * QB
            pb, ds = r.pb[0:n, :], r.ds[0:n, :]
            r.ot[head_rows, here] = mm(r.vt[head_rows, 0:n], pb).astype(BF16)
            r.dqt[head_rows, here] = mm(r.kt[head_rows, 0:n], ds)
            r.dk[0:n, lanes] += mm(ds, qm)
            r.dv[0:n, lanes] += mm(pb, dom)
        return 0

    per_x = T // QB

    def attend(theirs, first, last):
        for k in range(X):
            at = (1 - k if theirs else k) * per_x
            run = functools.partial(head, range(at, at + per_x))

            @pl.when(x == k)
            def _():
                lax.fori_loop(first, last, run, 0)

    attend(False, 0, 2)
    relay("i", "y", "c", "xz", 0)
    relay("o", "z", "y", "", 0)
    attend(False, 2, 4)
    relay("i", "y", "c", "xz", 1)
    r.hmt[...] = r.hm[...].T

    wi = r.wi.reshape(D, FH)
    wo = r.wo.reshape(FH, D)
    gi = r.gi.reshape(D, FH)
    go = r.go.reshape(FH, D)
    FB = 256

    def ff_cols(b):
        return pl.ds(pl.multiple_of(b * FB, FB), FB)

    def ff_forward(b, _):
        cols = ff_cols(b)
        f = mm(r.hm[...], wi[:, cols]) + r.vrow[6:7, cols]
        phi = 0.5 + 0.5 * lax.erf(f * (0.5**0.5))
        r.act[:, cols] = (f * phi).astype(BF16)
        r.slope[:, cols] = phi + f * (jnp.exp(-0.5 * f * f) * (0.5 / np.pi) ** 0.5)
        return 0

    arrived("i", 0)
    lax.fori_loop(0, FH // FB // 2, ff_forward, 0)
    relay("o", "z", "y", "", 1)
    arrived("i", 1)
    lax.fori_loop(FH // FB // 2, FH // FB, ff_forward, 0)

    wait("cot")
    r.cots[rows_mine, :] = r.cot[...]
    r.do2[rows_theirs, :] = mm(r.cots[rows_theirs, :], wd[mine, :], NT).astype(BF16)

    def out_grad(b, _):
        at = ff_cols(b)
        go[at, :] = mm(r.act[:, at], r.cots[...], TN).astype(BF16)
        return 0

    lax.fori_loop(0, FH // FB, out_grad, 0)
    scatter("o", "c", "", 0)
    scatter("o", "c", "", 1)
    relay("o", "y", "c", "z", 0)

    def send_o(b):
        own_rows = slice(b * 128, (b + 1) * 128)
        to = pl.ds(pl.multiple_of(x * HW + b * 128, 128), 128)
        push(("o", b), r.ot.at[own_rows, rows_theirs], r.of.at[to, :], at_x)
        r.of[to, :] = r.ot[own_rows, rows_mine]

    r.vg[...] = jnp.zeros_like(r.vg)
    gq = r.gq.reshape(D, 3 * HW)

    def qkv_back(b):
        def one(i, _):
            at = pl.ds(pl.multiple_of(i * QB, QB), QB)
            cols = slice(b * 128, (b + 1) * 128)
            dq = r.dqt[cols, at].T
            out = (
                turn(dq, at, -1.0) * HD**-0.5,
                turn(r.dk[at, cols], at, -1.0),
                r.dv[at, cols],
            )
            for jj in range(3):
                w = out[jj].astype(BF16)
                to = slice(b * 384 + jj * 128, b * 384 + (jj + 1) * 128)
                r.dqkv[at, to] = w
                r.vg[4:5, to] += jnp.sum(w.astype(F32), axis=0, keepdims=True)
            return 0

        lax.fori_loop(0, S // QB, one, 0)
        cols = chunk("q", b)
        for k in range(D // QB):
            gq[k * QB : (k + 1) * QB, cols] = mm(
                r.ha[:, k * QB : (k + 1) * QB], r.dqkv[:, cols], TN
            ).astype(BF16)
        scatter("q", "c", "", b)

    attend(True, 0, 2)
    relay("o", "y", "c", "z", 1)
    step("o", "c", "y", "", 0)
    step("o", "c", "y", "", 1)
    send_o(0)
    qkv_back(0)

    arrived("o", 0)
    arrived("o", 1)
    r.mos[...] = mm(r.act[rows_theirs, :], wo[...]).astype(BF16)
    push("mo", r.mos, r.mor, at_x)
    attend(True, 2, 4)
    send_o(1)
    half_z = pl.ds(x * (Z // X), Z // X)
    r.gd.reshape(D, D)[mine, :] = mm(r.ot[...], r.cots[...]).astype(BF16)
    gd_part = r.gd.at[half_z, :, :, xo]
    push("gd", gd_part, gd_part, at_x)
    step("q", "c", "y", "", 0)
    step("o", "y", "z", "c", 0)
    step("o", "y", "z", "c", 1)
    qkv_back(1)

    def ff_backward(b, _):
        cols = ff_cols(b)
        df = (mm(r.cots[...], wo[cols, :], NT) * r.slope[:, cols]).astype(BF16)
        r.vg[6:7, cols] = jnp.sum(df.astype(F32), axis=0, keepdims=True)
        r.df[:, cols] = df
        gi[:, cols] = mm(r.hmt[...], df).astype(BF16)
        return 0

    lax.fori_loop(0, FH // FB // 2, ff_backward, 0)
    scatter("i", "c", "", 0)
    step("q", "c", "y", "", 1)
    lax.fori_loop(FH // FB // 2, FH // FB, ff_backward, 0)
    scatter("i", "c", "", 1)
    step("i", "c", "y", "", 0)

    def input_grads(base, mine_too):
        def one(i, _):
            at = pl.ds(pl.multiple_of(base + i * QB, QB), QB)
            to = pl.ds(pl.multiple_of(i * QB, QB), QB)
            n = r.n[at, :]
            dm = mm(r.df[at, :], wi[...], NT)
            r.vg[2:3, 0:D] += jnp.sum(dm * n, axis=0, keepdims=True)
            r.vg[3:4, 0:D] += jnp.sum(dm, axis=0, keepdims=True)
            dh = mm(r.dqkv[at, :], wq[...], NT)
            r.vg[0:1, 0:D] += jnp.sum(dh * n, axis=0, keepdims=True)
            r.vg[1:2, 0:D] += jnp.sum(dh, axis=0, keepdims=True)
            u = dh * row(0) + dm * row(2)
            if mine_too:
                r.u[to, :] = u
            else:
                r.us[to, :] = u.astype(BF16)
            return 0

        lax.fori_loop(0, T // QB, one, 0)

    input_grads(xo * T, False)
    push("u", r.us, r.ur, at_x)
    step("i", "c", "y", "", 1)
    step("q", "y", "z", "c", 0)
    step("q", "y", "z", "c", 1)
    input_grads(x * T, True)

    g_sum = jnp.sum(r.cot[...].astype(F32), axis=0, keepdims=True)
    r.vg[5:6, 0:D] = g_sum
    r.vg[7:8, 0:D] = g_sum
    gv2 = r.gv.reshape(N * 8, 128)

    def collapse(v):
        n = lengths(v)
        j = column(v, n)
        pick = (iota((128, n), 0) == j % widths[v]).astype(F32).astype(BF16)
        left = jnp.where(iota((N, n), 0) == j // widths[v], r.vg[v : v + 1, 0:n], 0.0)
        acc = None
        for _ in range(3):
            low = left.astype(BF16)
            part = mm(low, pick, NT)
            acc = part if acc is None else acc + part
            left = left - low.astype(F32)
        gv2[pl.ds(v, N, stride=8), :] = acc

    for v in range(8):
        collapse(v)
    scatter("v", "c", "")
    wait("gd")
    scatter("d", "c", "x")
    step("i", "y", "z", "c", 0)
    r.mo[...] = mm(r.act[rows_mine, :], wo[...])
    step("i", "y", "z", "c", 1)

    def flat(out, width, k=None, part=D):
        per = width // 128
        n = out.shape[0] // per
        lo = 0 if k is None else k * (part // 128)

        def put(acc):
            for j in range(acc.shape[1] // 128):
                out[pl.ds(lo + j, n, stride=per), :] = acc[:, j * 128 : (j + 1) * 128]

        return put

    step("v", "c", "y")
    step("d", "c", "y", "x")
    add_parts("o", "z", "cy", 0, flat(r.oo, D, 0, CH["o"]))
    add_parts("o", "z", "cy", 1, flat(r.oo, D, 1, CH["o"]))
    at_me = (me["z"], me["y"], me["c"])
    step("v", "y", "z", "c")
    step("d", "y", "z", "cx")
    add_parts("q", "z", "cy", 0)
    add_parts("q", "z", "cy", 1)
    push("sq", r.gq.at[at_me + (xo,)], r.xq, at_x)

    wait(("o", 0))
    wait(("o", 1))
    wait("mo")
    r.out[...] = (
        r.tokens[...].astype(F32)
        + mm(r.of[...], wd[...], TN)
        + row(5)
        + (r.mo[...] + r.mor[...].astype(F32) + row(7))
    ).astype(BF16)
    step("v", "z", "x", "cy")
    add_parts("d", "z", "cyx", None, flat(r.od, D))
    add_parts("i", "z", "cy", 0)
    add_parts("i", "z", "cy", 1)
    push("si", r.gi.at[at_me + (xo,)], r.xi, at_x)

    wait("u")

    def final_rows(i, _):
        at = pl.ds(pl.multiple_of(i * RC, RC), RC)
        far = pl.ds(pl.multiple_of(x * T + i * RC, RC), RC)
        u = r.u[at, :] + r.ur[at, :].astype(F32)
        n = r.n[far, :]
        back = u - jnp.mean(u, axis=-1, keepdims=True) - n * jnp.mean(u * n, axis=-1, keepdims=True)
        r.gtok[at, :] = (r.cot[at, :].astype(F32) + back * r.scale[at, 0:1]).astype(BF16)
        return 0

    lax.fori_loop(0, T // RC, final_rows, 0)

    def join(mine_ref, got, out, width, place):
        per = width // 128
        n = out.shape[0] // per
        here = mine_ref[at_me + (x,)].astype(F32)
        there = got[...].astype(F32)
        halves = (jnp.where(x == 0, here, there), jnp.where(x == 0, there, here))

        def piece(b, to_high):
            half, m, odd = place(b)
            v = halves[half][:, m * 128 : (m + 1) * 128]
            return pltpu.roll(v, 64, 1) if odd != to_high else v

        for j in range(per):
            both = jnp.where(lane < 64, piece(2 * j, False), piece(2 * j + 1, True))
            out[pl.ds(j, n, stride=per), :] = both

    def place_q(b):
        h, jj = b // 3, b % 3
        return h // HC, (h % HC) // 2 * 3 + jj, h % 2 == 1

    def place_i(b):
        return b % 2, b // 4, (b // 2) % 2 == 1

    wait("sq")
    join(r.gq, r.xq, r.oq, 3 * D, place_q)
    wait("si")
    join(r.gi, r.xi, r.oi, FF, place_i)

    def put_vec(acc):
        r.ov[...] = acc

    add_parts("v", "x", "cyz", None, put_vec)


def rope_table(length):
    lanes = np.arange(128) % HD
    rot = HD // 4
    inverse = np.where(lanes < rot, 1.0 / ROPE_BASE ** (2.0 * (lanes % (rot // 2)) / rot), 0.0)
    high = 32.0 * np.arange(length // 32)[:, None] * inverse
    low = np.arange(32)[:, None] * inverse
    return np.stack([np.cos(high), np.sin(high), np.cos(low), np.sin(low)]).astype(np.float32)


def hand_over(*refs):
    for src, dst in zip(refs[:6], refs[7:13]):
        dst[...] = src[...]
    for v, dst in enumerate(refs[13:]):
        dst[...] = refs[6][v : v + 1, 0 : dst.shape[1]]


def layer(sizes, tokens, cotangent, *params):
    Z, Y, C, X = (sizes[a] for a in AX)
    N = Z * Y * C * X
    T = tokens.shape[1]
    S = T * X
    HW = HEADS // X * HD
    vectors = [params[i] for i in (0, 1, 2, 3, 5, 7, 9, 11)]
    weights = [params[i] for i in (4, 6, 8, 10)]
    flats = [w.reshape(-1, 128) for w in weights]
    full = dict(z=Z, y=Y, c=C, x=X)

    FH = FF // X

    def parts(name, axis, done, slab, dtype):
        free = [full[a] for a in AX if a not in done and a != axis and (a != "x" or name != "o")]
        return pltpu.VMEM((full[axis] - 1, *free, *slab), dtype)

    slabs = {
        "q": (D // N, 3 * HW),
        "d": (D // N, D),
        "i": (D // N, FH),
        "o": (FF // N, D),
        "v": (8, 128),
    }
    orders = {"q": "cyz", "d": "cyz", "i": "cyz", "o": "cyz", "v": "cyzx"}
    keep = types.SimpleNamespace()
    scratch = vars(keep)
    for k, slab in slabs.items():
        kind = F32 if k == "v" else BF16
        devs = (Z, Y, C) if k == "o" else (Z, Y, C, X)
        scratch["w" + k] = pltpu.VMEM((*devs, *slab), kind)
        scratch["g" + k] = pltpu.VMEM((*devs, *slab), kind)
        for n, axis in enumerate(orders[k]):
            done = orders[k][:n] + ("x" if k == "d" else "")
            scratch["r" + k + axis] = parts(k, axis, done, slab, kind)
    keep.xq = pltpu.VMEM(slabs["q"], BF16)
    keep.xi = pltpu.VMEM(slabs["i"], BF16)
    keep.sq = pltpu.VMEM((X, *slabs["q"]), BF16)
    keep.si = pltpu.VMEM((X, *slabs["i"]), BF16)
    keep.tmp = pltpu.VMEM((max(f.shape[0] for f in flats), 128), F32)
    keep.cos = keep.sinl = keep.sinh = pltpu.VMEM((S, 128), F32)
    keep.tok2 = pltpu.VMEM((T, D), BF16)
    keep.cots = pltpu.VMEM((S, D), BF16)
    keep.n = pltpu.VMEM((S, D), F32)
    keep.scale = pltpu.VMEM((T, 128), F32)
    keep.vrow = pltpu.VMEM((8, FH), F32)
    keep.vg = pltpu.VMEM((8, FH), F32)
    keep.ha = keep.hm = pltpu.VMEM((S, D), BF16)
    keep.hmt = pltpu.VMEM((D, S), BF16)
    keep.q = keep.k = keep.v = keep.do2 = pltpu.VMEM((S, HW), BF16)
    keep.kt = keep.vt = keep.ot = pltpu.VMEM((HW, S), BF16)
    keep.dqt = pltpu.VMEM((HW, S), F32)
    keep.dk = pltpu.VMEM((S, HW), F32)
    keep.dv = pltpu.VMEM((S, HW), F32)
    keep.st = pltpu.VMEM((S // QB, QB, QB), F32)
    keep.dp = pltpu.VMEM((S // QB, QB, QB), F32)
    keep.pb = pltpu.VMEM((S, QB), BF16)
    keep.ds = pltpu.VMEM((S, QB), BF16)
    keep.dqkv = pltpu.VMEM((S, 3 * HW), BF16)
    keep.of = pltpu.VMEM((D, T), BF16)
    keep.act = keep.df = pltpu.VMEM((S, FH), BF16)
    keep.slope = pltpu.VMEM((S, FH), F32)
    keep.u = keep.mo = pltpu.VMEM((T, D), F32)
    keep.us = keep.ur = keep.mos = keep.mor = pltpu.VMEM((T, D), BF16)
    copies = 128
    keep.send = pltpu.SemaphoreType.DMA((copies,))
    keep.recv = pltpu.SemaphoreType.DMA((copies,))
    ins = "tokens cot fq fd".split() + "fi fo rope".split() + ["v%d" % v for v in range(8)]
    outs = dict(
        out=jax.ShapeDtypeStruct((T, D), BF16),
        gtok=jax.ShapeDtypeStruct((T, D), BF16),
        oq=jax.ShapeDtypeStruct(flats[0].shape, F32),
        od=jax.ShapeDtypeStruct(flats[1].shape, F32),
        oi=jax.ShapeDtypeStruct(flats[2].shape, F32),
        oo=jax.ShapeDtypeStruct(flats[3].shape, F32),
        ov=jax.ShapeDtypeStruct((8, 128), F32),
    )
    vmem = pl.BlockSpec(memory_space=pltpu.VMEM)
    names = ins + list(outs) + list(scratch)
    out, gtok, gq, gd, gi, go, gv = pl.pallas_call(
        functools.partial(fused, sizes, names),
        out_shape=list(outs.values()),
        in_specs=[vmem] * len(ins),
        out_specs=[vmem] * len(outs),
        scratch_shapes=list(scratch.values()),
        compiler_params=pltpu.CompilerParams(
            collective_id=0, has_side_effects=True, vmem_limit_bytes=67043328
        ),
        name="layer",
    )(
        tokens.reshape(T, D),
        cotangent.reshape(T, D),
        *flats,
        jnp.asarray(rope_table(S)),
        *[v.reshape(1, -1) for v in vectors],
    )
    shapes = [jax.ShapeDtypeStruct(a.shape, a.dtype) for a in (out, gtok, gq, gd, gi, go)]
    shapes += [jax.ShapeDtypeStruct((1, p.shape[0]), F32) for p in vectors]
    out, gtok, gq, gd, gi, go, *v = pl.pallas_call(
        hand_over,
        out_shape=shapes,
        in_specs=[vmem] * 7,
        out_specs=[vmem] * len(shapes),
        name="results",
    )(out, gtok, gq, gd, gi, go, gv)
    v = [a.reshape(-1) for a in v]
    return (
        out.reshape(tokens.shape),
        gtok.reshape(tokens.shape),
        v[0],
        v[1],
        v[2],
        v[3],
        gq.reshape(-1),
        v[4],
        gd.reshape(-1),
        v[5],
        gi.reshape(-1),
        v[6],
        go.reshape(-1),
        v[7],
    )


def solution(mesh):
    n_seq, n_ctx = mesh.shape["seq"], mesh.shape["ctx"]
    if n_ctx != 2 or n_seq % 8 or (D // (n_seq * n_ctx)) % 16:
        return general(mesh)
    sizes = {"z": n_seq // 4, "y": 2, "c": 2, "x": n_ctx}
    flat = P(("seq", "ctx"))
    rows = P("seq", "ctx", None)
    return jax.shard_map(
        functools.partial(layer, sizes),
        mesh=mesh,
        in_specs=(rows, rows) + (flat,) * 12,
        out_specs=(rows, rows) + (flat,) * 12,
        check_vma=False,
    )
```

```python
import functools
import types

import jax
import jax.numpy as jnp
import numpy as np
from jax import lax
from jax.experimental import pallas as pl
from jax.experimental.pallas import tpu as pltpu
from jax.sharding import PartitionSpec as P

D = 512
HEADS = 8
FF = 2048


EPS = 1e-05
BOTH = ("seq", "ctx")
ROPE_BASE = 10000.0
NEG = -1e30


def layer_normalize(values, gain, bias):
    mean = jnp.mean(values, axis=-1, keepdims=True)
    centered = values - mean
    var = jnp.mean(centered * centered, axis=-1, keepdims=True)
    return centered * lax.rsqrt(var + EPS) * gain + bias


def rotate(values, cosine, sine):
    width = cosine.shape[-1]
    half = width // 2
    part = values[..., :width]
    turned = jnp.concatenate([-part[..., half:], part[..., :half]], axis=-1)
    return jnp.concatenate([part * cosine + turned * sine, values[..., width:]], axis=-1)


def gelu_exact(values):
    return jax.nn.gelu(values, approximate=False)


def matrices(mix_flat, proj_flat, expand_flat, reduce_flat):
    return (
        mix_flat.reshape(D, 3 * D),
        proj_flat.reshape(D, D),
        expand_flat.reshape(D, FF),
        reduce_flat.reshape(FF, D),
    )


def body(
    tokens,
    cotangent,
    attn_norm_gain,
    attn_norm_bias,
    mlp_norm_gain,
    mlp_norm_bias,
    qkv_weight,
    qkv_bias,
    dense_weight,
    dense_bias,
    fc_in_weight,
    fc_in_bias,
    fc_out_weight,
    fc_out_bias,
):
    (
        gain_attn,
        attention_shift,
        gain_mlp,
        shift_mlp,
        mix_flat,
        mix_bias,
        proj_flat,
        proj_bias,
        expand_flat,
        expand_bias,
        reduce_flat,
        reduce_bias,
    ) = (
        lax.all_gather(attn_norm_gain, BOTH, axis=0, tiled=True),
        lax.all_gather(attn_norm_bias, BOTH, axis=0, tiled=True),
        lax.all_gather(mlp_norm_gain, BOTH, axis=0, tiled=True),
        lax.all_gather(mlp_norm_bias, BOTH, axis=0, tiled=True),
        lax.all_gather(qkv_weight, BOTH, axis=0, tiled=True),
        lax.all_gather(qkv_bias, BOTH, axis=0, tiled=True),
        lax.all_gather(dense_weight, BOTH, axis=0, tiled=True),
        lax.all_gather(dense_bias, BOTH, axis=0, tiled=True),
        lax.all_gather(fc_in_weight, BOTH, axis=0, tiled=True),
        lax.all_gather(fc_in_bias, BOTH, axis=0, tiled=True),
        lax.all_gather(fc_out_weight, BOTH, axis=0, tiled=True),
        lax.all_gather(fc_out_bias, BOTH, axis=0, tiled=True),
    )
    mix_weight, proj_weight, expand_weight, reduce_weight = matrices(
        mix_flat, proj_flat, expand_flat, reduce_flat
    )
    shape = tokens.shape
    group = shape[1]
    width = shape[2]
    heads = HEADS
    head_dim = width // heads
    rows = tokens.reshape(group, width).astype(jnp.float32)
    attn_in, attn_norm_back = jax.vjp(
        layer_normalize, rows, gain_attn.astype(jnp.float32), attention_shift.astype(jnp.float32)
    )
    mlp_in, mlp_norm_back = jax.vjp(
        layer_normalize, rows, gain_mlp.astype(jnp.float32), shift_mlp.astype(jnp.float32)
    )
    attn_low = attn_in.astype(jnp.bfloat16)
    mlp_low = mlp_in.astype(jnp.bfloat16)
    mixed = jnp.dot(attn_low, mix_weight, preferred_element_type=jnp.float32) + mix_bias.astype(
        jnp.float32
    )
    mixed = mixed.reshape(group, heads, 3, head_dim)
    place = lax.axis_index("ctx")
    blocks_total = lax.axis_size("ctx")
    local_pos = jnp.arange(group, dtype=jnp.int32)
    query_pos = place * group + local_pos
    rot_dims = head_dim // 4
    inverse = 1.0 / ROPE_BASE ** (
        jnp.arange(0, rot_dims, 2, dtype=jnp.int32).astype(jnp.float32) / rot_dims
    )
    angles = query_pos.astype(jnp.float32)[:, None] * inverse[None, :]
    angles = jnp.concatenate([angles, angles], axis=-1)
    cosine = jnp.cos(angles)[:, None, :]
    sine = jnp.sin(angles)[:, None, :]
    scale = head_dim ** (-0.5)

    def turn(query_unrotated, key_raw):
        return (rotate(query_unrotated, cosine, sine) * scale, rotate(key_raw, cosine, sine))

    (query_f, key_f), turn_back = jax.vjp(turn, mixed[:, :, 0], mixed[:, :, 1])
    query = query_f.astype(jnp.bfloat16)
    key_own = key_f.astype(jnp.bfloat16).reshape(group, width)
    value_own = mixed[:, :, 2].astype(jnp.bfloat16).reshape(group, width)
    all_keys, all_values = (
        lax.all_gather(key_own, "ctx", axis=0, tiled=True),
        lax.all_gather(value_own, "ctx", axis=0, tiled=True),
    )
    count = place + 1

    def block(index):
        keys = lax.dynamic_slice_in_dim(all_keys, index * group, group, 0).reshape(
            group, heads, head_dim
        )
        values = lax.dynamic_slice_in_dim(all_values, index * group, group, 0).reshape(
            group, heads, head_dim
        )
        scores = jnp.einsum("qhd,khd->hqk", query, keys, preferred_element_type=jnp.float32)
        allowed = (index * group + local_pos)[None, :] <= query_pos[:, None]
        return (keys, values, scores, allowed[None])

    def max_step(index, carry):
        top, total = carry
        _, _, scores, allowed = block(index)
        new_top = jnp.maximum(top, jnp.max(jnp.where(allowed, scores, NEG), axis=-1))
        terms = jnp.where(allowed, jnp.exp(scores - new_top[:, :, None]), 0.0)
        return (new_top, total * jnp.exp(top - new_top) + jnp.sum(terms, axis=-1))

    start = (jnp.full((heads, group), NEG, jnp.float32), jnp.zeros((heads, group), jnp.float32))
    top, total = lax.fori_loop(0, count, max_step, start)
    log_total = top + jnp.log(total)

    def probs_of(scores, allowed):
        return jnp.where(allowed, jnp.exp(scores - log_total[:, :, None]), 0.0)

    def out_step(index, acc):
        _, values, scores, allowed = block(index)
        probs = probs_of(scores, allowed).astype(jnp.bfloat16)
        return acc + jnp.einsum("hqk,khd->qhd", probs, values, preferred_element_type=jnp.float32)

    heads_out = lax.fori_loop(0, count, out_step, jnp.zeros((group, heads, head_dim), jnp.float32))
    attn_out = heads_out.reshape(group, width).astype(jnp.bfloat16)
    branch_attn = jnp.dot(
        attn_out, proj_weight, preferred_element_type=jnp.float32
    ) + proj_bias.astype(jnp.float32)
    expand = jnp.dot(
        mlp_low, expand_weight, preferred_element_type=jnp.float32
    ) + expand_bias.astype(jnp.float32)
    active_rows, active_back = jax.vjp(gelu_exact, expand)
    active_low = active_rows.astype(jnp.bfloat16)
    branch_mlp = jnp.dot(
        active_low, reduce_weight, preferred_element_type=jnp.float32
    ) + reduce_bias.astype(jnp.float32)
    layer_out = (rows + branch_attn + branch_mlp).astype(jnp.bfloat16).reshape(shape)
    back_mix, back_proj, back_expand, back_reduce = (
        lax.all_gather(qkv_weight, BOTH, axis=0, tiled=True),
        lax.all_gather(dense_weight, BOTH, axis=0, tiled=True),
        lax.all_gather(fc_in_weight, BOTH, axis=0, tiled=True),
        lax.all_gather(fc_out_weight, BOTH, axis=0, tiled=True),
    )
    back_mix, back_proj, back_expand, back_reduce = matrices(
        back_mix, back_proj, back_expand, back_reduce
    )
    grad_rows = cotangent.reshape(group, width)
    grad_float = grad_rows.astype(jnp.float32)
    grad_reduce = jnp.einsum("tf,td->fd", active_low, grad_rows, preferred_element_type=jnp.float32)
    grad_out_bias = jnp.sum(grad_float, axis=0)
    grad_proj = jnp.einsum("te,td->ed", attn_out, grad_rows, preferred_element_type=jnp.float32)
    grad_active = jnp.einsum(
        "td,fd->tf", grad_rows, back_reduce, preferred_element_type=jnp.float32
    )
    grad_expand = active_back(grad_active)[0].astype(jnp.bfloat16)
    grad_expand_w = jnp.einsum(
        "td,tf->df", mlp_low, grad_expand, preferred_element_type=jnp.float32
    )
    grad_expand_b = jnp.sum(grad_expand.astype(jnp.float32), axis=0)
    grad_mlp_in = jnp.einsum(
        "tf,df->td", grad_expand, back_expand, preferred_element_type=jnp.float32
    )
    grad_heads = jnp.einsum("td,ed->te", grad_rows, back_proj, preferred_element_type=jnp.float32)
    grad_heads = grad_heads.astype(jnp.bfloat16).reshape(group, heads, head_dim)

    def delta_step(index, acc):
        _, values, scores, allowed = block(index)
        probs = probs_of(scores, allowed)
        grad_probs = jnp.einsum(
            "qhd,khd->hqk", grad_heads, values, preferred_element_type=jnp.float32
        )
        return acc + jnp.sum(probs * grad_probs, axis=-1)

    delta = lax.fori_loop(0, count, delta_step, jnp.zeros((heads, group), jnp.float32))

    def query_step(index, grad_query):
        keys, values, scores, allowed = block(index)
        probs = probs_of(scores, allowed)
        grad_probs = jnp.einsum(
            "qhd,khd->hqk", grad_heads, values, preferred_element_type=jnp.float32
        )
        grad_scores = (probs * (grad_probs - delta[:, :, None])).astype(jnp.bfloat16)
        return grad_query + jnp.einsum(
            "hqk,khd->qhd", grad_scores, keys, preferred_element_type=jnp.float32
        )

    grad_query = lax.fori_loop(
        0, count, query_step, jnp.zeros((group, heads, head_dim), jnp.float32)
    )
    all_queries, all_grad_heads = (
        lax.all_gather(query.reshape(group, width), "ctx", axis=0, tiled=True),
        lax.all_gather(grad_heads.reshape(group, width), "ctx", axis=0, tiled=True),
    )
    gathered_log_sums, all_delta = (
        lax.all_gather(jnp.transpose(log_total), "ctx", axis=0, tiled=True),
        lax.all_gather(jnp.transpose(delta), "ctx", axis=0, tiled=True),
    )
    keys_mine = key_own.reshape(group, heads, head_dim)
    values_mine = value_own.reshape(group, heads, head_dim)

    def owner_step(index, carry):
        key_acc, value_accumulator = carry
        queries = lax.dynamic_slice_in_dim(all_queries, index * group, group, 0).reshape(
            group, heads, head_dim
        )
        outer_grads = lax.dynamic_slice_in_dim(all_grad_heads, index * group, group, 0).reshape(
            group, heads, head_dim
        )
        lse_rows = jnp.transpose(
            lax.dynamic_slice_in_dim(gathered_log_sums, index * group, group, 0)
        )
        delta_rows = jnp.transpose(lax.dynamic_slice_in_dim(all_delta, index * group, group, 0))
        scores = jnp.einsum("qhd,khd->hqk", queries, keys_mine, preferred_element_type=jnp.float32)
        allowed = (query_pos[None, :] <= (index * group + local_pos)[:, None])[None]
        probs = jnp.where(allowed, jnp.exp(scores - lse_rows[:, :, None]), 0.0)
        grad_probs = jnp.einsum(
            "qhd,khd->hqk", outer_grads, values_mine, preferred_element_type=jnp.float32
        )
        grad_scores = (probs * (grad_probs - delta_rows[:, :, None])).astype(jnp.bfloat16)
        key_acc = key_acc + jnp.einsum(
            "hqk,qhd->khd", grad_scores, queries, preferred_element_type=jnp.float32
        )
        value_accumulator = value_accumulator + jnp.einsum(
            "hqk,qhd->khd",
            probs.astype(jnp.bfloat16),
            outer_grads,
            preferred_element_type=jnp.float32,
        )
        return (key_acc, value_accumulator)

    empty_heads = jnp.zeros((group, heads, head_dim), jnp.float32)
    own_key_grad, own_value_grad = lax.fori_loop(
        place, blocks_total, owner_step, (empty_heads, empty_heads)
    )
    grad_query_raw, grad_key_raw = turn_back((grad_query, own_key_grad))
    grad_mixed = jnp.stack([grad_query_raw, grad_key_raw, own_value_grad], axis=2)
    grad_mixed = grad_mixed.reshape(group, 3 * width).astype(jnp.bfloat16)
    grad_mix_w = jnp.einsum("td,te->de", attn_low, grad_mixed, preferred_element_type=jnp.float32)
    grad_mix_b = jnp.sum(grad_mixed.astype(jnp.float32), axis=0)
    grad_attn_in = jnp.einsum("te,de->td", grad_mixed, back_mix, preferred_element_type=jnp.float32)
    input_attn, gain_attn_grad, shift_attn_grad = attn_norm_back(grad_attn_in)
    input_mlp, gain_mlp_grad, shift_mlp_grad = mlp_norm_back(grad_mlp_in)
    grad_tokens = (grad_float + input_attn + input_mlp).astype(jnp.bfloat16).reshape(shape)
    sums = (
        lax.psum_scatter(gain_attn_grad, BOTH, scatter_dimension=0, tiled=True),
        lax.psum_scatter(shift_attn_grad, BOTH, scatter_dimension=0, tiled=True),
        lax.psum_scatter(gain_mlp_grad, BOTH, scatter_dimension=0, tiled=True),
        lax.psum_scatter(shift_mlp_grad, BOTH, scatter_dimension=0, tiled=True),
        lax.psum_scatter(grad_mix_w.reshape(-1), BOTH, scatter_dimension=0, tiled=True),
        lax.psum_scatter(grad_mix_b, BOTH, scatter_dimension=0, tiled=True),
        lax.psum_scatter(grad_proj.reshape(-1), BOTH, scatter_dimension=0, tiled=True),
        lax.psum_scatter(grad_out_bias, BOTH, scatter_dimension=0, tiled=True),
        lax.psum_scatter(
            grad_expand_w.reshape(-1), BOTH, scatter_dimension=0, tiled=True
        ),
        lax.psum_scatter(grad_expand_b, BOTH, scatter_dimension=0, tiled=True),
        lax.psum_scatter(grad_reduce.reshape(-1), BOTH, scatter_dimension=0, tiled=True),
        lax.psum_scatter(grad_out_bias, BOTH, scatter_dimension=0, tiled=True),
    )
    return (
        layer_out,
        grad_tokens,
        sums[0],
        sums[1],
        sums[2],
        sums[3],
        sums[4],
        sums[5],
        sums[6],
        sums[7],
        sums[8],
        sums[9],
        sums[10],
        sums[11],
    )


def general(mesh):
    return jax.shard_map(
        body,
        mesh=mesh,
        in_specs=(
            P("seq", "ctx", None),
            P("seq", "ctx", None),
            P(BOTH),
            P(BOTH),
            P(BOTH),
            P(BOTH),
            P(BOTH),
            P(BOTH),
            P(BOTH),
            P(BOTH),
            P(BOTH),
            P(BOTH),
            P(BOTH),
            P(BOTH),
        ),
        out_specs=(
            P("seq", "ctx", None),
            P("seq", "ctx", None),
            P(BOTH),
            P(BOTH),
            P(BOTH),
            P(BOTH),
            P(BOTH),
            P(BOTH),
            P(BOTH),
            P(BOTH),
            P(BOTH),
            P(BOTH),
            P(BOTH),
            P(BOTH),
        ),
        check_vma=False,
    )


MESH = pl.DeviceIdType.MESH
F32, BF16 = jnp.float32, jnp.bfloat16
HD = D // HEADS
AX = "zycx"
NN = (((1,), (0,)), ((), ()))
NT = (((1,), (1,)), ((), ()))
TN = (((0,), (0,)), ((), ()))
QB = 256


def mm(a, b, dims=NN):
    return lax.dot_general(a, b, dims, preferred_element_type=F32)


def iota(shape, dim):
    return lax.broadcasted_iota(jnp.int32, shape, dim)


def fused(sizes, names, *refs):
    held = dict(zip(names, refs))
    r = types.SimpleNamespace(**held)
    X = sizes["x"]
    C = sizes["c"]
    Y = sizes["y"]
    Z = sizes["z"]
    N = Z * Y * C * X
    T = held["tokens"].shape[0]
    S = T * X
    HC = HEADS // X
    HW = HC * HD
    FH = FF // X
    CH = dict(q=384, i=FH // 2, o=D // 2, d=D // 2)
    s = lax.axis_index("seq")
    me = {"x": lax.axis_index("ctx"), "c": s % C, "y": (s // C) % Y, "z": s // (C * Y)}
    x = me["x"]
    xo = 1 - x

    def device(at):
        return ((at["z"] * Y + at["y"]) * C + at["c"], at["x"])

    def others(axis):
        n = sizes[axis]
        return [dict(me, **{axis: (me[axis] + d) % n}) for d in range(1, n)]

    flight = {}
    count = [0]

    def push(key, src, dst, at):
        k = count[0]
        count[0] += 1
        cp = pltpu.make_async_remote_copy(
            src_ref=src,
            dst_ref=dst,
            send_sem=r.send.at[k],
            recv_sem=r.recv.at[k],
            device_id=device(at),
            device_id_type=MESH,
        )
        cp.start()
        flight.setdefault(key, []).append(cp)

    def wait(key):
        for cp in flight.pop(key):
            cp.wait()

    def axes(name):
        return AX[: 3 if name == "o" else 4]

    def chunk(name, k):
        if k is None:
            return slice(None)
        w = CH[name]
        return slice(k * w, (k + 1) * w)

    def gather(name, axis, known, k=None):
        ref = held["w" + name]
        spot = tuple(slice(None) if a in known else me[a] for a in axes(name))
        part = ref.at[spot + (slice(None), chunk(name, k))]
        for at in others(axis):
            push(("w", name, axis, k), part, part, at)

    def relay(name, axis, nxt, known, k=None):
        wait(("w", name, axis, k))
        gather(name, nxt, known + axis, k)

    def arrived(name, k=None):
        wait(("w", name, "c", k))

    def scatter(name, axis, done, k=None):
        ref, got = held["g" + name], held["r" + name + axis]
        free = [a for a in axes(name) if a not in done and a != axis]
        cols = (slice(None), chunk(name, k))
        for n, at in enumerate(others(axis)):
            spot = tuple(slice(None) if a in free else at[a] for a in axes(name))
            to = (n,) + (slice(None),) * len(free)
            push(("g", name, axis, k), ref.at[spot + cols], got.at[to + cols], at)

    def add_parts(name, axis, done, k=None, finish=None):
        wait(("g", name, axis, k))
        ref, got = held["g" + name], held["r" + name + axis]
        free = [a for a in axes(name) if a not in done and a != axis]
        cols = (slice(None), chunk(name, k))
        total = 1
        for a in free:
            total *= sizes[a]

        def one(i, _):
            at, rest = dict(me), i
            for a in reversed(free):
                at[a] = rest % sizes[a]
                rest = rest // sizes[a]
            spot = tuple(at[a] for a in axes(name))
            inner = tuple(at[a] for a in free)
            acc = ref[spot + cols].astype(F32)
            for n in range(sizes[axis] - 1):
                acc = acc + got[(n,) + inner + cols].astype(F32)
            if finish is None:
                ref[spot + cols] = acc.astype(ref.dtype)
            else:
                finish(acc)
            return 0

        if total == 1:
            one(0, 0)
        else:
            lax.fori_loop(0, total, one, 0)

    def step(name, axis, nxt, done="", k=None):
        add_parts(name, axis, done, k)
        scatter(name, nxt, done + axis, k)

    barrier = pltpu.get_barrier_semaphore()
    greet = [at for a in AX for at in others(a)]
    for at in greet:
        pl.semaphore_signal(barrier, inc=1, device_id=device(at), device_id_type=MESH)
    loads = {}
    for k, name in enumerate(n for n in names if ("h" + n) in held):
        loads[name] = pltpu.make_async_copy(held["h" + name], held[name], r.load.at[k])
        loads[name].start()

    def loaded(*which):
        for name in which:
            loads[name].wait()

    loaded("fq", "fi", "fd", *["v%d" % v for v in range(8)])

    tmp = r.tmp
    lane = iota((1, 128), 1)

    def own(name):
        return held[name].at[me["z"], me["y"], me["c"], x]

    def block64(b, per, rows, to_high):
        v = tmp[pl.ds(b // 2, rows, stride=per), :]
        return pltpu.roll(v, 64, 1) if (b % 2 == 1) != to_high else v

    def split(src, dst, width, table):
        n = held[src].shape[0]
        per = width // 128
        tmp[0:n, :] = held[src][...].astype(F32)
        for half in range(X):
            for m in range(per // X):
                low, high = table(half, m)
                low = block64(low, per, n // per, False)
                high = block64(high, per, n // per, True)
                dst[half, :, m * 128 : (m + 1) * 128] = jnp.where(lane < 64, low, high).astype(BF16)

    def table_q(half, m):
        h0 = half * HC + 2 * (m // 3)
        return 3 * h0 + m % 3, 3 * (h0 + 1) + m % 3

    def table_i(half, m):
        return 4 * m + half, 4 * m + 2 + half

    def reshard(src, dst, width):
        n = held[src].shape[0]
        k = width // 128
        tmp[0:n, :] = held[src][...].astype(F32)
        for j in range(k):
            dst[:, j * 128 : (j + 1) * 128] = tmp[pl.ds(j, n // k, stride=k), :].astype(BF16)

    split("fq", r.sq, 3 * D, table_q)
    split("fi", r.si, FF, table_i)
    reshard("fd", own("wd"), D)
    vecs = own("wv")
    vecs[...] = jnp.zeros_like(vecs)
    for v in range(8):
        vin = held["v%d" % v]
        vecs[v : v + 1, 0 : vin.shape[1]] = vin[...].astype(F32)
    own("wq")[...] = r.sq[x]
    own("wi")[...] = r.si[x]

    loaded("tokens", "cot", "fo", "rope")
    pl.semaphore_wait(barrier, len(greet))

    rows_mine = pl.ds(pl.multiple_of(x * T, T), T)
    rows_theirs = pl.ds(pl.multiple_of(xo * T, T), T)
    at_x = others("x")[0]
    gather("v", "x", "")
    push("sq", r.sq.at[xo], own("wq"), at_x)
    push("si", r.si.at[xo], own("wi"), at_x)
    gather("d", "x", "")
    push("tok", r.tokens, r.tok2, at_x)
    push("cot", r.cot, r.cots.at[rows_mine, :], at_x)
    reshard("fo", r.wo.at[me["z"], me["y"], me["c"]], D)

    rope = r.rope
    mod = lane % HD

    def rope_rows(i, _):
        ch, sh = rope[0, pl.ds(i, 1), :], rope[1, pl.ds(i, 1), :]
        cl, sl = rope[2], rope[3]
        sine = sh * cl + ch * sl
        at = pl.ds(pl.multiple_of(i * 32, 32), 32)
        r.cos[at, :] = ch * cl - sh * sl
        r.sinl[at, :] = jnp.where(mod < 8, -sine, 0.0)
        r.sinh[at, :] = jnp.where(mod < 8, 0.0, sine)
        return 0

    def turn(u, at, sign):
        return (
            u * r.cos[at, :]
            + sign * (pltpu.roll(u, 120, 1) * r.sinl[at, :] + pltpu.roll(u, 8, 1) * r.sinh[at, :])
        )

    relay("v", "x", "z", "")
    wait("sq")
    gather("q", "z", "x", 0)
    gather("q", "z", "x", 1)
    wait(("w", "d", "x", None))
    gather("d", "z", "x", 0)
    gather("d", "z", "x", 1)
    wait("si")
    gather("i", "z", "x", 0)
    gather("i", "z", "x", 1)
    gather("o", "z", "", 0)
    gather("o", "z", "", 1)
    lax.fori_loop(0, S // 32, rope_rows, 0)

    RC = 128

    def norm_rows(src, base, keep):
        def one(i, _):
            v = src[pl.ds(pl.multiple_of(i * RC, RC), RC), :].astype(F32)
            c = v - jnp.mean(v, axis=-1, keepdims=True)
            scale = lax.rsqrt(jnp.mean(c * c, axis=-1, keepdims=True) + EPS)
            r.n[pl.ds(pl.multiple_of(base + i * RC, RC), RC), :] = c * scale
            if keep:
                r.scale[pl.ds(pl.multiple_of(i * RC, RC), RC), :] = jnp.broadcast_to(scale, (RC, 128))
            return 0

        lax.fori_loop(0, T // RC, one, 0)

    norm_rows(r.tokens, x * T, True)

    relay("v", "z", "y", "x")
    relay("q", "z", "y", "x", 0)
    relay("v", "y", "c", "xz")
    relay("q", "z", "y", "x", 1)
    arrived("v")

    widths = [D // N, D // N, D // N, D // N, 3 * D // N, D // N, FF // N, D // N]

    def column(v, n):
        j = iota((1, n), 1)
        if v == 4:
            head_at = x * HC + 2 * (j // 384) + (j % 128) // HD
            return head_at * (3 * HD) + ((j % 384) // 128) * HD + j % HD
        if v == 6:
            return (j // 64) * 128 + x * 64 + j % 64
        return j

    def lengths(v):
        return {4: 3 * HW, 6: FH}.get(v, D)

    vec2 = r.wv.reshape(N * 8, 128)

    def expand(v):
        n = lengths(v)
        j = column(v, n)
        pick = (iota((128, n), 0) == j % widths[v]).astype(F32).astype(BF16)
        rows_v = vec2[pl.ds(v, N, stride=8), :].astype(BF16)
        spread = mm(rows_v, pick)
        r.vrow[v : v + 1, 0:n] = jnp.sum(
            jnp.where(iota((N, n), 0) == j // widths[v], spread, 0.0), axis=0, keepdims=True
        )

    for v in range(8):
        expand(v)

    def row(v, n=D, off=0):
        return r.vrow[v : v + 1, off : off + n]

    def affine_attn(base):
        def one(i, _):
            at = pl.ds(pl.multiple_of(base + i * RC, RC), RC)
            r.ha[at, :] = (r.n[at, :] * row(0) + row(1)).astype(BF16)
            return 0

        lax.fori_loop(0, T // RC, one, 0)

    def affine_mlp(base):
        def one(i, _):
            at = pl.ds(pl.multiple_of(base + i * RC, RC), RC)
            r.hm[at, :] = (r.n[at, :] * row(2) + row(3)).astype(BF16)
            return 0

        lax.fori_loop(0, T // RC, one, 0)

    affine_attn(x * T)
    relay("d", "z", "y", "x", 0)
    relay("q", "y", "c", "xz", 0)
    affine_mlp(x * T)
    relay("q", "y", "c", "xz", 1)
    relay("d", "z", "y", "x", 1)

    wait("tok")
    norm_rows(r.tok2, xo * T, False)
    affine_attn(xo * T)
    affine_mlp(xo * T)
    relay("i", "z", "y", "x", 0)
    relay("d", "y", "c", "xz", 0)

    wq = r.wq.reshape(D, 3 * HW)

    def qkv(b):
        def one(i, _):
            at = pl.ds(pl.multiple_of(i * QB, QB), QB)
            u = mm(r.ha[at, :], wq[:, chunk("q", b)]) + row(4, 384, b * 384)
            for jj, name in enumerate("qkv"):
                w = u[:, jj * 128 : (jj + 1) * 128]
                if jj < 2:
                    w = turn(w, at, 1.0)
                if jj == 0:
                    w = w * HD**-0.5
                w = w.astype(BF16)
                held[name][at, b * 128 : (b + 1) * 128] = w
                if jj >= 1:
                    held[name + "t"][b * 128 : (b + 1) * 128, at] = w.T
            return 0

        arrived("q", b)
        lax.fori_loop(0, S // QB, one, 0)

    qkv(0)
    relay("i", "z", "y", "x", 1)
    relay("d", "y", "c", "xz", 1)
    qkv(1)
    arrived("d", 0)
    arrived("d", 1)
    wd = r.wd.reshape(D, D)
    mine = pl.ds(pl.multiple_of(x * HW, HW), HW)
    r.do2[rows_mine, :] = mm(r.cot[...], wd[mine, :], NT).astype(BF16)

    r.dk[...] = jnp.zeros_like(r.dk)
    r.dv[...] = jnp.zeros_like(r.dv)
    causal = iota((QB, QB), 0) <= iota((QB, QB), 1)

    def head(blocks, h, _):
        lanes = pl.ds(pl.multiple_of((h // 2) * 128, 128), 128)
        ours = (lane // HD) == h % 2
        head_rows = pl.ds(pl.multiple_of(h * HD, HD), HD)
        for i in blocks:
            here = slice(i * QB, (i + 1) * QB)
            qm = jnp.where(ours, r.q[here, lanes], jnp.zeros((), BF16))
            dom = jnp.where(ours, r.do2[here, lanes], jnp.zeros((), BF16))
            top = None
            for j in range(i + 1):
                st = mm(r.k[j * QB : (j + 1) * QB, lanes], qm, NT)
                if j == i:
                    st = jnp.where(causal, st, NEG)
                r.st[j] = st
                part = jnp.max(st, axis=0, keepdims=True)
                top = part if top is None else jnp.maximum(top, part)
            total = du = None
            for j in range(i + 1):
                e = jnp.exp(r.st[j] - top)
                r.st[j] = e
                dp = mm(r.v[j * QB : (j + 1) * QB, lanes], dom, NT)
                r.dp[j] = dp
                part, both = (jnp.sum(w, axis=0, keepdims=True) for w in (e, e * dp))
                total = part if total is None else total + part
                du = both if du is None else du + both
            scale = 1.0 / total
            delta = du * scale
            for j in range(i + 1):
                p = r.st[j] * scale
                r.pb[j * QB : (j + 1) * QB, :] = p.astype(BF16)
                ds = p * (r.dp[j] - delta)
                r.ds[j * QB : (j + 1) * QB, :] = ds.astype(BF16)
            n = (i + 1) * QB
            pb, ds = r.pb[0:n, :], r.ds[0:n, :]
            r.ot[head_rows, here] = mm(r.vt[head_rows, 0:n], pb).astype(BF16)
            r.dqt[head_rows, here] = mm(r.kt[head_rows, 0:n], ds)
            r.dk[0:n, lanes] += mm(ds, qm)
            r.dv[0:n, lanes] += mm(pb, dom)
        return 0

    per_x = T // QB

    def attend(theirs, first, last):
        for k in range(X):
            at = (1 - k if theirs else k) * per_x
            run = functools.partial(head, range(at, at + per_x))

            @pl.when(x == k)
            def _():
                lax.fori_loop(first, last, run, 0)

    attend(False, 0, 2)
    relay("i", "y", "c", "xz", 0)
    relay("o", "z", "y", "", 0)
    relay("o", "z", "y", "", 1)
    attend(False, 2, 4)
    relay("i", "y", "c", "xz", 1)
    r.hmt[...] = r.hm[...].T

    wi = r.wi.reshape(D, FH)
    wo = r.wo.reshape(FH, D)
    gi = r.gi.reshape(D, FH)
    go = r.go.reshape(FH, D)
    FB = 256

    def ff_cols(b):
        return pl.ds(pl.multiple_of(b * FB, FB), FB)

    def ff_forward(b, _):
        cols = ff_cols(b)
        f = mm(r.hm[...], wi[:, cols]) + r.vrow[6:7, cols]
        phi = 0.5 + 0.5 * lax.erf(f * (0.5**0.5))
        r.act[:, cols] = (f * phi).astype(BF16)
        r.slope[:, cols] = phi + f * (jnp.exp(-0.5 * f * f) * (0.5 / np.pi) ** 0.5)
        return 0

    arrived("i", 0)
    lax.fori_loop(0, FH // FB // 2, ff_forward, 0)
    arrived("i", 1)
    lax.fori_loop(FH // FB // 2, FH // FB, ff_forward, 0)

    wait("cot")
    r.cots[rows_mine, :] = r.cot[...]
    r.do2[rows_theirs, :] = mm(r.cots[rows_theirs, :], wd[mine, :], NT).astype(BF16)

    def out_grad(b, _):
        at = ff_cols(b)
        go[at, :] = mm(r.act[:, at], r.cots[...], TN).astype(BF16)
        return 0

    relay("o", "y", "c", "z", 0)
    lax.fori_loop(0, FH // FB, out_grad, 0)
    scatter("o", "c", "", 0)
    scatter("o", "c", "", 1)
    relay("o", "y", "c", "z", 1)

    def send_o(b):
        own_rows = slice(b * 128, (b + 1) * 128)
        to = pl.ds(pl.multiple_of(x * HW + b * 128, 128), 128)
        push(("o", b), r.ot.at[own_rows, rows_theirs], r.of.at[to, :], at_x)
        r.of[to, :] = r.ot[own_rows, rows_mine]
        r.gd.reshape(D, D)[to, :] = mm(r.ot[own_rows, :], r.cots[...]).astype(BF16)
        part = r.gd.at[x * (Z // X) + b, :, :, xo]
        push("gd", part, part, at_x)

    r.vg[...] = jnp.zeros_like(r.vg)
    gq = r.gq.reshape(D, 3 * HW)

    def qkv_back(b):
        def one(i, _):
            at = pl.ds(pl.multiple_of(i * QB, QB), QB)
            cols = slice(b * 128, (b + 1) * 128)
            dq = r.dqt[cols, at].T
            out = (
                turn(dq, at, -1.0) * HD**-0.5,
                turn(r.dk[at, cols], at, -1.0),
                r.dv[at, cols],
            )
            for jj in range(3):
                w = out[jj].astype(BF16)
                to = slice(b * 384 + jj * 128, b * 384 + (jj + 1) * 128)
                r.dqkv[at, to] = w
                r.vg[4:5, to] += jnp.sum(w.astype(F32), axis=0, keepdims=True)
            return 0

        lax.fori_loop(0, S // QB, one, 0)
        cols = chunk("q", b)
        for k in range(D // QB):
            gq[k * QB : (k + 1) * QB, cols] = mm(
                r.ha[:, k * QB : (k + 1) * QB], r.dqkv[:, cols], TN
            ).astype(BF16)
        scatter("q", "c", "", b)

    attend(True, 0, 1)
    arrived("o", 0)
    arrived("o", 1)
    r.mos[...] = mm(r.act[rows_theirs, :], wo[...]).astype(BF16)
    push("mo", r.mos, r.mor, at_x)
    attend(True, 1, 2)
    step("o", "c", "y", "", 0)
    step("o", "c", "y", "", 1)
    send_o(0)
    qkv_back(0)
    attend(True, 2, 4)
    send_o(1)
    step("q", "c", "y", "", 0)
    step("o", "y", "z", "c", 0)
    step("o", "y", "z", "c", 1)
    qkv_back(1)

    def ff_backward(b, _):
        cols = ff_cols(b)
        df = (mm(r.cots[...], wo[cols, :], NT) * r.slope[:, cols]).astype(BF16)
        r.vg[6:7, cols] = jnp.sum(df.astype(F32), axis=0, keepdims=True)
        r.df[:, cols] = df
        gi[:, cols] = mm(r.hmt[...], df).astype(BF16)
        return 0

    lax.fori_loop(0, FH // FB // 2, ff_backward, 0)
    scatter("i", "c", "", 0)
    step("q", "c", "y", "", 1)
    lax.fori_loop(FH // FB // 2, FH // FB, ff_backward, 0)
    scatter("i", "c", "", 1)
    step("i", "c", "y", "", 0)

    def input_grads(base, mine_too):
        def one(i, _):
            at = pl.ds(pl.multiple_of(base + i * QB, QB), QB)
            to = pl.ds(pl.multiple_of(i * QB, QB), QB)
            n = r.n[at, :]
            dm = mm(r.df[at, :], wi[...], NT)
            r.vg[2:3, 0:D] += jnp.sum(dm * n, axis=0, keepdims=True)
            r.vg[3:4, 0:D] += jnp.sum(dm, axis=0, keepdims=True)
            dh = mm(r.dqkv[at, :], wq[...], NT)
            r.vg[0:1, 0:D] += jnp.sum(dh * n, axis=0, keepdims=True)
            r.vg[1:2, 0:D] += jnp.sum(dh, axis=0, keepdims=True)
            u = dh * row(0) + dm * row(2)
            if mine_too:
                r.u[to, :] = u
            else:
                r.us[to, :] = u.astype(BF16)
            return 0

        lax.fori_loop(0, T // QB, one, 0)

    input_grads(xo * T, False)
    for k in range(T // QB):
        part = slice(k * QB, (k + 1) * QB)
        push(("u", k), r.us.at[part, :], r.ur.at[part, :], at_x)
    step("i", "c", "y", "", 1)
    step("q", "y", "z", "c", 0)
    step("q", "y", "z", "c", 1)
    input_grads(x * T, True)

    g_sum = jnp.sum(r.cot[...].astype(F32), axis=0, keepdims=True)
    r.vg[5:6, 0:D] = g_sum
    r.vg[7:8, 0:D] = g_sum
    gv2 = r.gv.reshape(N * 8, 128)

    def collapse(v):
        n = lengths(v)
        j = column(v, n)
        pick = (iota((128, n), 0) == j % widths[v]).astype(F32).astype(BF16)
        left = jnp.where(iota((N, n), 0) == j // widths[v], r.vg[v : v + 1, 0:n], 0.0)
        acc = None
        for _ in range(3):
            low = left.astype(BF16)
            part = mm(low, pick, NT)
            acc = part if acc is None else acc + part
            left = left - low.astype(F32)
        gv2[pl.ds(v, N, stride=8), :] = acc

    for v in range(8):
        collapse(v)
    scatter("v", "c", "")
    wait("gd")
    scatter("d", "c", "x")
    step("i", "y", "z", "c", 0)
    r.mo[...] = mm(r.act[rows_mine, :], wo[...])
    step("i", "y", "z", "c", 1)

    def flat(out, width, k=None, part=D):
        per = width // 128
        n = out.shape[0] // per
        lo = 0 if k is None else k * (part // 128)

        def put(acc):
            for j in range(acc.shape[1] // 128):
                out[pl.ds(lo + j, n, stride=per), :] = acc[:, j * 128 : (j + 1) * 128]

        return put

    step("v", "c", "y")
    step("d", "c", "y", "x")
    add_parts("o", "z", "cy", 0, flat(r.oo, D, 0, CH["o"]))
    add_parts("o", "z", "cy", 1, flat(r.oo, D, 1, CH["o"]))
    at_me = (me["z"], me["y"], me["c"])
    step("v", "y", "z", "c")
    step("d", "y", "z", "cx")
    add_parts("q", "z", "cy", 0)
    add_parts("q", "z", "cy", 1)
    push("sq", r.gq.at[at_me + (xo,)], r.xq, at_x)

    wait(("o", 0))
    wait(("o", 1))
    wait("mo")
    r.out[...] = (
        r.tokens[...].astype(F32)
        + mm(r.of[...], wd[...], TN)
        + row(5)
        + (r.mo[...] + r.mor[...].astype(F32) + row(7))
    ).astype(BF16)
    step("v", "z", "x", "cy")
    add_parts("d", "z", "cyx", None, flat(r.od, D))
    add_parts("i", "z", "cy", 0)
    add_parts("i", "z", "cy", 1)
    push("si", r.gi.at[at_me + (xo,)], r.xi, at_x)


    def final_rows(i, _):
        at = pl.ds(pl.multiple_of(i * RC, RC), RC)
        far = pl.ds(pl.multiple_of(x * T + i * RC, RC), RC)
        u = r.u[at, :] + r.ur[at, :].astype(F32)
        n = r.n[far, :]
        back = u - jnp.mean(u, axis=-1, keepdims=True) - n * jnp.mean(u * n, axis=-1, keepdims=True)
        r.gtok[at, :] = (r.cot[at, :].astype(F32) + back * r.scale[at, 0:1]).astype(BF16)
        return 0

    for k in range(T // QB):
        wait(("u", k))
        lax.fori_loop(k * (QB // RC), (k + 1) * (QB // RC), final_rows, 0)

    def join(mine_ref, got, out, width, place):
        per = width // 128
        n = out.shape[0] // per
        here = mine_ref[at_me + (x,)].astype(F32)
        there = got[...].astype(F32)
        halves = (jnp.where(x == 0, here, there), jnp.where(x == 0, there, here))

        def piece(b, to_high):
            half, m, odd = place(b)
            v = halves[half][:, m * 128 : (m + 1) * 128]
            return pltpu.roll(v, 64, 1) if odd != to_high else v

        for j in range(per):
            both = jnp.where(lane < 64, piece(2 * j, False), piece(2 * j + 1, True))
            out[pl.ds(j, n, stride=per), :] = both

    def place_q(b):
        h, jj = b // 3, b % 3
        return h // HC, (h % HC) // 2 * 3 + jj, h % 2 == 1

    def place_i(b):
        return b % 2, b // 4, (b // 2) % 2 == 1

    wait("sq")
    join(r.gq, r.xq, r.oq, 3 * D, place_q)
    wait("si")
    join(r.gi, r.xi, r.oi, FF, place_i)

    def put_vec(acc):
        r.ov[...] = acc

    add_parts("v", "x", "cyz", None, put_vec)


def rope_table(length):
    lanes = np.arange(128) % HD
    rot = HD // 4
    inverse = np.where(lanes < rot, 1.0 / ROPE_BASE ** (2.0 * (lanes % (rot // 2)) / rot), 0.0)
    high = 32.0 * np.arange(length // 32)[:, None] * inverse
    low = np.arange(32)[:, None] * inverse
    return np.stack([np.cos(high), np.sin(high), np.cos(low), np.sin(low)]).astype(np.float32)


def hand_over(*refs):
    for src, dst in zip(refs[:6], refs[7:13]):
        dst[...] = src[...]
    for v, dst in enumerate(refs[13:]):
        dst[...] = refs[6][v : v + 1, 0 : dst.shape[1]]


def layer(sizes, tokens, cotangent, *params):
    Z, Y, C, X = (sizes[a] for a in AX)
    N = Z * Y * C * X
    T = tokens.shape[1]
    S = T * X
    HW = HEADS // X * HD
    vectors = [params[i] for i in (0, 1, 2, 3, 5, 7, 9, 11)]
    weights = [params[i] for i in (4, 6, 8, 10)]
    flats = [w.reshape(-1, 128) for w in weights]
    full = dict(z=Z, y=Y, c=C, x=X)

    FH = FF // X

    def parts(name, axis, done, slab, dtype):
        free = [full[a] for a in AX if a not in done and a != axis and (a != "x" or name != "o")]
        return pltpu.VMEM((full[axis] - 1, *free, *slab), dtype)

    slabs = {
        "q": (D // N, 3 * HW),
        "d": (D // N, D),
        "i": (D // N, FH),
        "o": (FF // N, D),
        "v": (8, 128),
    }
    orders = {"q": "cyz", "d": "cyz", "i": "cyz", "o": "cyz", "v": "cyzx"}
    keep = types.SimpleNamespace()
    scratch = vars(keep)
    for k, slab in slabs.items():
        kind = F32 if k == "v" else BF16
        devs = (Z, Y, C) if k == "o" else (Z, Y, C, X)
        scratch["w" + k] = pltpu.VMEM((*devs, *slab), kind)
        scratch["g" + k] = pltpu.VMEM((*devs, *slab), kind)
        for n, axis in enumerate(orders[k]):
            done = orders[k][:n] + ("x" if k == "d" else "")
            scratch["r" + k + axis] = parts(k, axis, done, slab, kind)
    keep.xq = pltpu.VMEM(slabs["q"], BF16)
    keep.xi = pltpu.VMEM(slabs["i"], BF16)
    keep.sq = pltpu.VMEM((X, *slabs["q"]), BF16)
    keep.si = pltpu.VMEM((X, *slabs["i"]), BF16)
    keep.tmp = pltpu.VMEM((max(f.shape[0] for f in flats), 128), F32)
    keep.cos = keep.sinl = keep.sinh = pltpu.VMEM((S, 128), F32)
    keep.tok2 = pltpu.VMEM((T, D), BF16)
    keep.cots = pltpu.VMEM((S, D), BF16)
    keep.n = pltpu.VMEM((S, D), F32)
    keep.scale = pltpu.VMEM((T, 128), F32)
    keep.vrow = pltpu.VMEM((8, FH), F32)
    keep.vg = pltpu.VMEM((8, FH), F32)
    keep.ha = keep.hm = pltpu.VMEM((S, D), BF16)
    keep.hmt = pltpu.VMEM((D, S), BF16)
    keep.q = keep.k = keep.v = keep.do2 = pltpu.VMEM((S, HW), BF16)
    keep.kt = keep.vt = keep.ot = pltpu.VMEM((HW, S), BF16)
    keep.dqt = pltpu.VMEM((HW, S), F32)
    keep.dk = pltpu.VMEM((S, HW), F32)
    keep.dv = pltpu.VMEM((S, HW), F32)
    keep.st = pltpu.VMEM((S // QB, QB, QB), F32)
    keep.dp = pltpu.VMEM((S // QB, QB, QB), F32)
    keep.pb = pltpu.VMEM((S, QB), BF16)
    keep.ds = pltpu.VMEM((S, QB), BF16)
    keep.dqkv = pltpu.VMEM((S, 3 * HW), BF16)
    keep.of = pltpu.VMEM((D, T), BF16)
    keep.act = keep.df = pltpu.VMEM((S, FH), BF16)
    keep.slope = pltpu.VMEM((S, FH), F32)
    keep.u = keep.mo = pltpu.VMEM((T, D), F32)
    keep.us = keep.ur = keep.mos = keep.mor = pltpu.VMEM((T, D), BF16)
    copies = 128
    keep.send = pltpu.SemaphoreType.DMA((copies,))
    keep.recv = pltpu.SemaphoreType.DMA((copies,))
    ins = "tokens cot fq fd".split() + "fi fo rope".split() + ["v%d" % v for v in range(8)]
    outs = dict(
        out=jax.ShapeDtypeStruct((T, D), BF16),
        gtok=jax.ShapeDtypeStruct((T, D), BF16),
        oq=jax.ShapeDtypeStruct(flats[0].shape, F32),
        od=jax.ShapeDtypeStruct(flats[1].shape, F32),
        oi=jax.ShapeDtypeStruct(flats[2].shape, F32),
        oo=jax.ShapeDtypeStruct(flats[3].shape, F32),
        ov=jax.ShapeDtypeStruct((8, 128), F32),
    )
    vmem = pl.BlockSpec(memory_space=pltpu.VMEM)
    shown = tokens.reshape(T, D), cotangent.reshape(T, D), *flats, jnp.asarray(rope_table(S))
    shown += tuple(v.reshape(1, -1) for v in vectors)
    for name, a in zip(ins, shown):
        scratch[name] = pltpu.VMEM(a.shape, a.dtype)
    keep.load = pltpu.SemaphoreType.DMA((len(ins),))
    names = ["h" + n for n in ins] + list(outs) + list(scratch)
    out, gtok, gq, gd, gi, go, gv = pl.pallas_call(
        functools.partial(fused, sizes, names),
        out_shape=list(outs.values()),
        in_specs=[pl.BlockSpec(memory_space=pl.ANY)] * len(ins),
        out_specs=[vmem] * len(outs),
        scratch_shapes=list(scratch.values()),
        compiler_params=pltpu.CompilerParams(
            collective_id=0, has_side_effects=True, vmem_limit_bytes=67043328
        ),
        name="layer",
    )(
        *shown
    )
    shapes = [jax.ShapeDtypeStruct(a.shape, a.dtype) for a in (out, gtok, gq, gd, gi, go)]
    shapes += [jax.ShapeDtypeStruct((1, p.shape[0]), F32) for p in vectors]
    out, gtok, gq, gd, gi, go, *v = pl.pallas_call(
        hand_over,
        out_shape=shapes,
        in_specs=[vmem] * 7,
        out_specs=[vmem] * len(shapes),
        name="results",
    )(out, gtok, gq, gd, gi, go, gv)
    v = [a.reshape(-1) for a in v]
    return (
        out.reshape(tokens.shape),
        gtok.reshape(tokens.shape),
        v[0],
        v[1],
        v[2],
        v[3],
        gq.reshape(-1),
        v[4],
        gd.reshape(-1),
        v[5],
        gi.reshape(-1),
        v[6],
        go.reshape(-1),
        v[7],
    )


def solution(mesh):
    n_seq, n_ctx = mesh.shape["seq"], mesh.shape["ctx"]
    if n_ctx != 2 or n_seq % 8 or (D // (n_seq * n_ctx)) % 16:
        return general(mesh)
    sizes = {"z": n_seq // 4, "y": 2, "c": 2, "x": n_ctx}
    flat = P(("seq", "ctx"))
    rows = P("seq", "ctx", None)
    return jax.shard_map(
        functools.partial(layer, sizes),
        mesh=mesh,
        in_specs=(rows, rows) + (flat,) * 12,
        out_specs=(rows, rows) + (flat,) * 12,
        check_vma=False,
    )
```

```python
import functools
import types

import jax
import jax.numpy as jnp
import numpy as np
from jax import lax
from jax.experimental import pallas as pl
from jax.experimental.pallas import tpu as pltpu
from jax.sharding import PartitionSpec as P

D = 512
HEADS = 8
FF = 2048


EPS = 1e-05
BOTH = ("seq", "ctx")
ROPE_BASE = 10000.0
NEG = -1e30


def layer_normalize(values, gain, bias):
    mean = jnp.mean(values, axis=-1, keepdims=True)
    centered = values - mean
    var = jnp.mean(centered * centered, axis=-1, keepdims=True)
    return centered * lax.rsqrt(var + EPS) * gain + bias


def rotate(values, cosine, sine):
    width = cosine.shape[-1]
    half = width // 2
    part = values[..., :width]
    turned = jnp.concatenate([-part[..., half:], part[..., :half]], axis=-1)
    return jnp.concatenate([part * cosine + turned * sine, values[..., width:]], axis=-1)


def gelu_exact(values):
    return jax.nn.gelu(values, approximate=False)


def matrices(mix_flat, proj_flat, expand_flat, reduce_flat):
    return (
        mix_flat.reshape(D, 3 * D),
        proj_flat.reshape(D, D),
        expand_flat.reshape(D, FF),
        reduce_flat.reshape(FF, D),
    )


def body(
    tokens,
    cotangent,
    attn_norm_gain,
    attn_norm_bias,
    mlp_norm_gain,
    mlp_norm_bias,
    qkv_weight,
    qkv_bias,
    dense_weight,
    dense_bias,
    fc_in_weight,
    fc_in_bias,
    fc_out_weight,
    fc_out_bias,
):
    (
        gain_attn,
        attention_shift,
        gain_mlp,
        shift_mlp,
        mix_flat,
        mix_bias,
        proj_flat,
        proj_bias,
        expand_flat,
        expand_bias,
        reduce_flat,
        reduce_bias,
    ) = (
        lax.all_gather(attn_norm_gain, BOTH, axis=0, tiled=True),
        lax.all_gather(attn_norm_bias, BOTH, axis=0, tiled=True),
        lax.all_gather(mlp_norm_gain, BOTH, axis=0, tiled=True),
        lax.all_gather(mlp_norm_bias, BOTH, axis=0, tiled=True),
        lax.all_gather(qkv_weight, BOTH, axis=0, tiled=True),
        lax.all_gather(qkv_bias, BOTH, axis=0, tiled=True),
        lax.all_gather(dense_weight, BOTH, axis=0, tiled=True),
        lax.all_gather(dense_bias, BOTH, axis=0, tiled=True),
        lax.all_gather(fc_in_weight, BOTH, axis=0, tiled=True),
        lax.all_gather(fc_in_bias, BOTH, axis=0, tiled=True),
        lax.all_gather(fc_out_weight, BOTH, axis=0, tiled=True),
        lax.all_gather(fc_out_bias, BOTH, axis=0, tiled=True),
    )
    mix_weight, proj_weight, expand_weight, reduce_weight = matrices(
        mix_flat, proj_flat, expand_flat, reduce_flat
    )
    shape = tokens.shape
    group = shape[1]
    width = shape[2]
    heads = HEADS
    head_dim = width // heads
    rows = tokens.reshape(group, width).astype(jnp.float32)
    attn_in, attn_norm_back = jax.vjp(
        layer_normalize, rows, gain_attn.astype(jnp.float32), attention_shift.astype(jnp.float32)
    )
    mlp_in, mlp_norm_back = jax.vjp(
        layer_normalize, rows, gain_mlp.astype(jnp.float32), shift_mlp.astype(jnp.float32)
    )
    attn_low = attn_in.astype(jnp.bfloat16)
    mlp_low = mlp_in.astype(jnp.bfloat16)
    mixed = jnp.dot(attn_low, mix_weight, preferred_element_type=jnp.float32) + mix_bias.astype(
        jnp.float32
    )
    mixed = mixed.reshape(group, heads, 3, head_dim)
    place = lax.axis_index("ctx")
    blocks_total = lax.axis_size("ctx")
    local_pos = jnp.arange(group, dtype=jnp.int32)
    query_pos = place * group + local_pos
    rot_dims = head_dim // 4
    inverse = 1.0 / ROPE_BASE ** (
        jnp.arange(0, rot_dims, 2, dtype=jnp.int32).astype(jnp.float32) / rot_dims
    )
    angles = query_pos.astype(jnp.float32)[:, None] * inverse[None, :]
    angles = jnp.concatenate([angles, angles], axis=-1)
    cosine = jnp.cos(angles)[:, None, :]
    sine = jnp.sin(angles)[:, None, :]
    scale = head_dim ** (-0.5)

    def turn(query_unrotated, key_raw):
        return (rotate(query_unrotated, cosine, sine) * scale, rotate(key_raw, cosine, sine))

    (query_f, key_f), turn_back = jax.vjp(turn, mixed[:, :, 0], mixed[:, :, 1])
    query = query_f.astype(jnp.bfloat16)
    key_own = key_f.astype(jnp.bfloat16).reshape(group, width)
    value_own = mixed[:, :, 2].astype(jnp.bfloat16).reshape(group, width)
    all_keys, all_values = (
        lax.all_gather(key_own, "ctx", axis=0, tiled=True),
        lax.all_gather(value_own, "ctx", axis=0, tiled=True),
    )
    count = place + 1

    def block(index):
        keys = lax.dynamic_slice_in_dim(all_keys, index * group, group, 0).reshape(
            group, heads, head_dim
        )
        values = lax.dynamic_slice_in_dim(all_values, index * group, group, 0).reshape(
            group, heads, head_dim
        )
        scores = jnp.einsum("qhd,khd->hqk", query, keys, preferred_element_type=jnp.float32)
        allowed = (index * group + local_pos)[None, :] <= query_pos[:, None]
        return (keys, values, scores, allowed[None])

    def max_step(index, carry):
        top, total = carry
        _, _, scores, allowed = block(index)
        new_top = jnp.maximum(top, jnp.max(jnp.where(allowed, scores, NEG), axis=-1))
        terms = jnp.where(allowed, jnp.exp(scores - new_top[:, :, None]), 0.0)
        return (new_top, total * jnp.exp(top - new_top) + jnp.sum(terms, axis=-1))

    start = (jnp.full((heads, group), NEG, jnp.float32), jnp.zeros((heads, group), jnp.float32))
    top, total = lax.fori_loop(0, count, max_step, start)
    log_total = top + jnp.log(total)

    def probs_of(scores, allowed):
        return jnp.where(allowed, jnp.exp(scores - log_total[:, :, None]), 0.0)

    def out_step(index, acc):
        _, values, scores, allowed = block(index)
        probs = probs_of(scores, allowed).astype(jnp.bfloat16)
        return acc + jnp.einsum("hqk,khd->qhd", probs, values, preferred_element_type=jnp.float32)

    heads_out = lax.fori_loop(0, count, out_step, jnp.zeros((group, heads, head_dim), jnp.float32))
    attn_out = heads_out.reshape(group, width).astype(jnp.bfloat16)
    branch_attn = jnp.dot(
        attn_out, proj_weight, preferred_element_type=jnp.float32
    ) + proj_bias.astype(jnp.float32)
    expand = jnp.dot(
        mlp_low, expand_weight, preferred_element_type=jnp.float32
    ) + expand_bias.astype(jnp.float32)
    active_rows, active_back = jax.vjp(gelu_exact, expand)
    active_low = active_rows.astype(jnp.bfloat16)
    branch_mlp = jnp.dot(
        active_low, reduce_weight, preferred_element_type=jnp.float32
    ) + reduce_bias.astype(jnp.float32)
    layer_out = (rows + branch_attn + branch_mlp).astype(jnp.bfloat16).reshape(shape)
    back_mix, back_proj, back_expand, back_reduce = (
        lax.all_gather(qkv_weight, BOTH, axis=0, tiled=True),
        lax.all_gather(dense_weight, BOTH, axis=0, tiled=True),
        lax.all_gather(fc_in_weight, BOTH, axis=0, tiled=True),
        lax.all_gather(fc_out_weight, BOTH, axis=0, tiled=True),
    )
    back_mix, back_proj, back_expand, back_reduce = matrices(
        back_mix, back_proj, back_expand, back_reduce
    )
    grad_rows = cotangent.reshape(group, width)
    grad_float = grad_rows.astype(jnp.float32)
    grad_reduce = jnp.einsum("tf,td->fd", active_low, grad_rows, preferred_element_type=jnp.float32)
    grad_out_bias = jnp.sum(grad_float, axis=0)
    grad_proj = jnp.einsum("te,td->ed", attn_out, grad_rows, preferred_element_type=jnp.float32)
    grad_active = jnp.einsum(
        "td,fd->tf", grad_rows, back_reduce, preferred_element_type=jnp.float32
    )
    grad_expand = active_back(grad_active)[0].astype(jnp.bfloat16)
    grad_expand_w = jnp.einsum(
        "td,tf->df", mlp_low, grad_expand, preferred_element_type=jnp.float32
    )
    grad_expand_b = jnp.sum(grad_expand.astype(jnp.float32), axis=0)
    grad_mlp_in = jnp.einsum(
        "tf,df->td", grad_expand, back_expand, preferred_element_type=jnp.float32
    )
    grad_heads = jnp.einsum("td,ed->te", grad_rows, back_proj, preferred_element_type=jnp.float32)
    grad_heads = grad_heads.astype(jnp.bfloat16).reshape(group, heads, head_dim)

    def delta_step(index, acc):
        _, values, scores, allowed = block(index)
        probs = probs_of(scores, allowed)
        grad_probs = jnp.einsum(
            "qhd,khd->hqk", grad_heads, values, preferred_element_type=jnp.float32
        )
        return acc + jnp.sum(probs * grad_probs, axis=-1)

    delta = lax.fori_loop(0, count, delta_step, jnp.zeros((heads, group), jnp.float32))

    def query_step(index, grad_query):
        keys, values, scores, allowed = block(index)
        probs = probs_of(scores, allowed)
        grad_probs = jnp.einsum(
            "qhd,khd->hqk", grad_heads, values, preferred_element_type=jnp.float32
        )
        grad_scores = (probs * (grad_probs - delta[:, :, None])).astype(jnp.bfloat16)
        return grad_query + jnp.einsum(
            "hqk,khd->qhd", grad_scores, keys, preferred_element_type=jnp.float32
        )

    grad_query = lax.fori_loop(
        0, count, query_step, jnp.zeros((group, heads, head_dim), jnp.float32)
    )
    all_queries, all_grad_heads = (
        lax.all_gather(query.reshape(group, width), "ctx", axis=0, tiled=True),
        lax.all_gather(grad_heads.reshape(group, width), "ctx", axis=0, tiled=True),
    )
    gathered_log_sums, all_delta = (
        lax.all_gather(jnp.transpose(log_total), "ctx", axis=0, tiled=True),
        lax.all_gather(jnp.transpose(delta), "ctx", axis=0, tiled=True),
    )
    keys_mine = key_own.reshape(group, heads, head_dim)
    values_mine = value_own.reshape(group, heads, head_dim)

    def owner_step(index, carry):
        key_acc, value_accumulator = carry
        queries = lax.dynamic_slice_in_dim(all_queries, index * group, group, 0).reshape(
            group, heads, head_dim
        )
        outer_grads = lax.dynamic_slice_in_dim(all_grad_heads, index * group, group, 0).reshape(
            group, heads, head_dim
        )
        lse_rows = jnp.transpose(
            lax.dynamic_slice_in_dim(gathered_log_sums, index * group, group, 0)
        )
        delta_rows = jnp.transpose(lax.dynamic_slice_in_dim(all_delta, index * group, group, 0))
        scores = jnp.einsum("qhd,khd->hqk", queries, keys_mine, preferred_element_type=jnp.float32)
        allowed = (query_pos[None, :] <= (index * group + local_pos)[:, None])[None]
        probs = jnp.where(allowed, jnp.exp(scores - lse_rows[:, :, None]), 0.0)
        grad_probs = jnp.einsum(
            "qhd,khd->hqk", outer_grads, values_mine, preferred_element_type=jnp.float32
        )
        grad_scores = (probs * (grad_probs - delta_rows[:, :, None])).astype(jnp.bfloat16)
        key_acc = key_acc + jnp.einsum(
            "hqk,qhd->khd", grad_scores, queries, preferred_element_type=jnp.float32
        )
        value_accumulator = value_accumulator + jnp.einsum(
            "hqk,qhd->khd",
            probs.astype(jnp.bfloat16),
            outer_grads,
            preferred_element_type=jnp.float32,
        )
        return (key_acc, value_accumulator)

    empty_heads = jnp.zeros((group, heads, head_dim), jnp.float32)
    own_key_grad, own_value_grad = lax.fori_loop(
        place, blocks_total, owner_step, (empty_heads, empty_heads)
    )
    grad_query_raw, grad_key_raw = turn_back((grad_query, own_key_grad))
    grad_mixed = jnp.stack([grad_query_raw, grad_key_raw, own_value_grad], axis=2)
    grad_mixed = grad_mixed.reshape(group, 3 * width).astype(jnp.bfloat16)
    grad_mix_w = jnp.einsum("td,te->de", attn_low, grad_mixed, preferred_element_type=jnp.float32)
    grad_mix_b = jnp.sum(grad_mixed.astype(jnp.float32), axis=0)
    grad_attn_in = jnp.einsum("te,de->td", grad_mixed, back_mix, preferred_element_type=jnp.float32)
    input_attn, gain_attn_grad, shift_attn_grad = attn_norm_back(grad_attn_in)
    input_mlp, gain_mlp_grad, shift_mlp_grad = mlp_norm_back(grad_mlp_in)
    grad_tokens = (grad_float + input_attn + input_mlp).astype(jnp.bfloat16).reshape(shape)
    sums = (
        lax.psum_scatter(gain_attn_grad, BOTH, scatter_dimension=0, tiled=True),
        lax.psum_scatter(shift_attn_grad, BOTH, scatter_dimension=0, tiled=True),
        lax.psum_scatter(gain_mlp_grad, BOTH, scatter_dimension=0, tiled=True),
        lax.psum_scatter(shift_mlp_grad, BOTH, scatter_dimension=0, tiled=True),
        lax.psum_scatter(grad_mix_w.reshape(-1), BOTH, scatter_dimension=0, tiled=True),
        lax.psum_scatter(grad_mix_b, BOTH, scatter_dimension=0, tiled=True),
        lax.psum_scatter(grad_proj.reshape(-1), BOTH, scatter_dimension=0, tiled=True),
        lax.psum_scatter(grad_out_bias, BOTH, scatter_dimension=0, tiled=True),
        lax.psum_scatter(
            grad_expand_w.reshape(-1), BOTH, scatter_dimension=0, tiled=True
        ),
        lax.psum_scatter(grad_expand_b, BOTH, scatter_dimension=0, tiled=True),
        lax.psum_scatter(grad_reduce.reshape(-1), BOTH, scatter_dimension=0, tiled=True),
        lax.psum_scatter(grad_out_bias, BOTH, scatter_dimension=0, tiled=True),
    )
    return (
        layer_out,
        grad_tokens,
        sums[0],
        sums[1],
        sums[2],
        sums[3],
        sums[4],
        sums[5],
        sums[6],
        sums[7],
        sums[8],
        sums[9],
        sums[10],
        sums[11],
    )


def general(mesh):
    return jax.shard_map(
        body,
        mesh=mesh,
        in_specs=(
            P("seq", "ctx", None),
            P("seq", "ctx", None),
            P(BOTH),
            P(BOTH),
            P(BOTH),
            P(BOTH),
            P(BOTH),
            P(BOTH),
            P(BOTH),
            P(BOTH),
            P(BOTH),
            P(BOTH),
            P(BOTH),
            P(BOTH),
        ),
        out_specs=(
            P("seq", "ctx", None),
            P("seq", "ctx", None),
            P(BOTH),
            P(BOTH),
            P(BOTH),
            P(BOTH),
            P(BOTH),
            P(BOTH),
            P(BOTH),
            P(BOTH),
            P(BOTH),
            P(BOTH),
            P(BOTH),
            P(BOTH),
        ),
        check_vma=False,
    )


MESH = pl.DeviceIdType.MESH
F32, BF16 = jnp.float32, jnp.bfloat16
HD = D // HEADS
AX = "zycx"
NN = (((1,), (0,)), ((), ()))
NT = (((1,), (1,)), ((), ()))
TN = (((0,), (0,)), ((), ()))
QB = 256


def mm(a, b, dims=NN):
    return lax.dot_general(a, b, dims, preferred_element_type=F32)


def iota(shape, dim):
    return lax.broadcasted_iota(jnp.int32, shape, dim)


def fused(sizes, names, *refs):
    held = dict(zip(names, refs))
    r = types.SimpleNamespace(**held)
    X = sizes["x"]
    C = sizes["c"]
    Y = sizes["y"]
    Z = sizes["z"]
    N = Z * Y * C * X
    T = held["tokens"].shape[0]
    S = T * X
    HC = HEADS // X
    HW = HC * HD
    FH = FF // X
    CH = dict(q=384, i=FH // 2, o=D // 2, d=D // 2)
    s = lax.axis_index("seq")
    me = {"x": lax.axis_index("ctx"), "c": s % C, "y": (s // C) % Y, "z": s // (C * Y)}
    x = me["x"]
    xo = 1 - x

    def device(at):
        return ((at["z"] * Y + at["y"]) * C + at["c"], at["x"])

    def others(axis):
        n = sizes[axis]
        return [dict(me, **{axis: (me[axis] + d) % n}) for d in range(1, n)]

    flight = {}
    count = [0]

    def push(key, src, dst, at):
        k = count[0]
        count[0] += 1
        cp = pltpu.make_async_remote_copy(
            src_ref=src,
            dst_ref=dst,
            send_sem=r.send.at[k],
            recv_sem=r.recv.at[k],
            device_id=device(at),
            device_id_type=MESH,
        )
        cp.start()
        flight.setdefault(key, []).append(cp)

    def wait(key):
        for cp in flight.pop(key):
            cp.wait()

    def axes(name):
        return AX[: 3 if name == "o" else 4]

    def chunk(name, k):
        if k is None:
            return slice(None)
        w = CH[name]
        return slice(k * w, (k + 1) * w)

    def gather(name, axis, known, k=None):
        ref = held["w" + name]
        spot = tuple(slice(None) if a in known else me[a] for a in axes(name))
        part = ref.at[spot + (slice(None), chunk(name, k))]
        for at in others(axis):
            push(("w", name, axis, k), part, part, at)

    def relay(name, axis, nxt, known, k=None):
        wait(("w", name, axis, k))
        gather(name, nxt, known + axis, k)

    def arrived(name, k=None):
        wait(("w", name, "c", k))

    def scatter(name, axis, done, k=None):
        ref, got = held["g" + name], held["r" + name + axis]
        free = [a for a in axes(name) if a not in done and a != axis]
        cols = (slice(None), chunk(name, k))
        for n, at in enumerate(others(axis)):
            spot = tuple(slice(None) if a in free else at[a] for a in axes(name))
            to = (n,) + (slice(None),) * len(free)
            push(("g", name, axis, k), ref.at[spot + cols], got.at[to + cols], at)

    def add_parts(name, axis, done, k=None, finish=None):
        wait(("g", name, axis, k))
        ref, got = held["g" + name], held["r" + name + axis]
        free = [a for a in axes(name) if a not in done and a != axis]
        cols = (slice(None), chunk(name, k))
        total = 1
        for a in free:
            total *= sizes[a]

        def one(i, _):
            at, rest = dict(me), i
            for a in reversed(free):
                at[a] = rest % sizes[a]
                rest = rest // sizes[a]
            spot = tuple(at[a] for a in axes(name))
            inner = tuple(at[a] for a in free)
            acc = ref[spot + cols].astype(F32)
            for n in range(sizes[axis] - 1):
                acc = acc + got[(n,) + inner + cols].astype(F32)
            if finish is None:
                ref[spot + cols] = acc.astype(ref.dtype)
            else:
                finish(acc)
            return 0

        if total == 1:
            one(0, 0)
        else:
            lax.fori_loop(0, total, one, 0)

    def step(name, axis, nxt, done="", k=None):
        add_parts(name, axis, done, k)
        scatter(name, nxt, done + axis, k)

    barrier = pltpu.get_barrier_semaphore()
    greet = [at for a in AX for at in others(a)]
    for at in greet:
        pl.semaphore_signal(barrier, inc=1, device_id=device(at), device_id_type=MESH)
    loads = {}
    for k, name in enumerate(n for n in names if ("h" + n) in held):
        loads[name] = pltpu.make_async_copy(held["h" + name], held[name], r.load.at[k])
        loads[name].start()

    def loaded(*which):
        for name in which:
            loads[name].wait()

    loaded("fq", "fi", "fd", *["v%d" % v for v in range(8)])

    tmp = r.tmp
    lane = iota((1, 128), 1)

    def own(name):
        return held[name].at[me["z"], me["y"], me["c"], x]

    def block64(b, per, rows, to_high):
        v = tmp[pl.ds(b // 2, rows, stride=per), :]
        return pltpu.roll(v, 64, 1) if (b % 2 == 1) != to_high else v

    def split(src, dst, width, table):
        n = held[src].shape[0]
        per = width // 128
        tmp[0:n, :] = held[src][...].astype(F32)
        for half in range(X):
            for m in range(per // X):
                low, high = table(half, m)
                low = block64(low, per, n // per, False)
                high = block64(high, per, n // per, True)
                dst[half, :, m * 128 : (m + 1) * 128] = jnp.where(lane < 64, low, high).astype(BF16)

    def table_q(half, m):
        h0 = half * HC + 2 * (m // 3)
        return 3 * h0 + m % 3, 3 * (h0 + 1) + m % 3

    def table_i(half, m):
        return 4 * m + half, 4 * m + 2 + half

    def reshard(src, dst, width):
        n = held[src].shape[0]
        k = width // 128
        tmp[0:n, :] = held[src][...].astype(F32)
        for j in range(k):
            dst[:, j * 128 : (j + 1) * 128] = tmp[pl.ds(j, n // k, stride=k), :].astype(BF16)

    split("fq", r.sq, 3 * D, table_q)
    split("fi", r.si, FF, table_i)
    reshard("fd", own("wd"), D)
    vecs = own("wv")
    vecs[...] = jnp.zeros_like(vecs)
    for v in range(8):
        vin = held["v%d" % v]
        vecs[v : v + 1, 0 : vin.shape[1]] = vin[...].astype(F32)
    own("wq")[...] = r.sq[x]
    own("wi")[...] = r.si[x]

    loaded("tokens", "cot", "fo", "rope")
    pl.semaphore_wait(barrier, len(greet))

    rows_mine = pl.ds(pl.multiple_of(x * T, T), T)
    rows_theirs = pl.ds(pl.multiple_of(xo * T, T), T)
    at_x = others("x")[0]
    gather("v", "x", "")
    push("sq", r.sq.at[xo], own("wq"), at_x)
    push("si", r.si.at[xo], own("wi"), at_x)
    gather("d", "x", "")
    push("tok", r.tokens, r.tok2, at_x)
    push("cot", r.cot, r.cots.at[rows_mine, :], at_x)
    reshard("fo", r.wo.at[me["z"], me["y"], me["c"]], D)

    rope = r.rope
    mod = lane % HD

    def rope_rows(i, _):
        ch, sh = rope[0, pl.ds(i, 1), :], rope[1, pl.ds(i, 1), :]
        cl, sl = rope[2], rope[3]
        sine = sh * cl + ch * sl
        at = pl.ds(pl.multiple_of(i * 32, 32), 32)
        r.cos[at, :] = ch * cl - sh * sl
        r.sinl[at, :] = jnp.where(mod < 8, -sine, 0.0)
        r.sinh[at, :] = jnp.where(mod < 8, 0.0, sine)
        return 0

    def turn(u, at, sign):
        return (
            u * r.cos[at, :]
            + sign * (pltpu.roll(u, 120, 1) * r.sinl[at, :] + pltpu.roll(u, 8, 1) * r.sinh[at, :])
        )

    relay("v", "x", "z", "")
    wait("sq")
    gather("q", "z", "x", 0)
    gather("q", "z", "x", 1)
    wait(("w", "d", "x", None))
    gather("d", "z", "x", 0)
    gather("d", "z", "x", 1)
    wait("si")
    gather("i", "z", "x", 0)
    gather("i", "z", "x", 1)
    gather("o", "z", "", 0)
    gather("o", "z", "", 1)
    lax.fori_loop(0, S // 32, rope_rows, 0)

    RC = 128

    def norm_rows(src, base, keep):
        def one(i, _):
            v = src[pl.ds(pl.multiple_of(i * RC, RC), RC), :].astype(F32)
            c = v - jnp.mean(v, axis=-1, keepdims=True)
            scale = lax.rsqrt(jnp.mean(c * c, axis=-1, keepdims=True) + EPS)
            r.n[pl.ds(pl.multiple_of(base + i * RC, RC), RC), :] = c * scale
            if keep:
                r.scale[pl.ds(pl.multiple_of(i * RC, RC), RC), :] = jnp.broadcast_to(scale, (RC, 128))
            return 0

        lax.fori_loop(0, T // RC, one, 0)

    norm_rows(r.tokens, x * T, True)

    relay("v", "z", "y", "x")
    relay("q", "z", "y", "x", 0)
    relay("v", "y", "c", "xz")
    relay("q", "z", "y", "x", 1)
    arrived("v")

    widths = [D // N, D // N, D // N, D // N, 3 * D // N, D // N, FF // N, D // N]

    def column(v, n):
        j = iota((1, n), 1)
        if v == 4:
            head_at = x * HC + 2 * (j // 384) + (j % 128) // HD
            return head_at * (3 * HD) + ((j % 384) // 128) * HD + j % HD
        if v == 6:
            return (j // 64) * 128 + x * 64 + j % 64
        return j

    def lengths(v):
        return {4: 3 * HW, 6: FH}.get(v, D)

    vec2 = r.wv.reshape(N * 8, 128)

    def expand(v):
        n = lengths(v)
        j = column(v, n)
        pick = (iota((128, n), 0) == j % widths[v]).astype(F32).astype(BF16)
        rows_v = vec2[pl.ds(v, N, stride=8), :].astype(BF16)
        spread = mm(rows_v, pick)
        r.vrow[v : v + 1, 0:n] = jnp.sum(
            jnp.where(iota((N, n), 0) == j // widths[v], spread, 0.0), axis=0, keepdims=True
        )

    for v in range(8):
        expand(v)

    def row(v, n=D, off=0):
        return r.vrow[v : v + 1, off : off + n]

    def affine_attn(base):
        def one(i, _):
            at = pl.ds(pl.multiple_of(base + i * RC, RC), RC)
            r.ha[at, :] = (r.n[at, :] * row(0) + row(1)).astype(BF16)
            return 0

        lax.fori_loop(0, T // RC, one, 0)

    def affine_mlp(base):
        def one(i, _):
            at = pl.ds(pl.multiple_of(base + i * RC, RC), RC)
            r.hm[at, :] = (r.n[at, :] * row(2) + row(3)).astype(BF16)
            return 0

        lax.fori_loop(0, T // RC, one, 0)

    affine_attn(x * T)
    relay("d", "z", "y", "x", 0)
    relay("q", "y", "c", "xz", 0)
    affine_mlp(x * T)
    relay("q", "y", "c", "xz", 1)
    relay("d", "z", "y", "x", 1)

    wait("tok")
    norm_rows(r.tok2, xo * T, False)
    affine_attn(xo * T)
    affine_mlp(xo * T)
    relay("i", "z", "y", "x", 0)
    relay("d", "y", "c", "xz", 0)

    wq = r.wq.reshape(D, 3 * HW)

    def qkv(b):
        def one(i, _):
            at = pl.ds(pl.multiple_of(i * QB, QB), QB)
            u = mm(r.ha[at, :], wq[:, chunk("q", b)]) + row(4, 384, b * 384)
            for jj, name in enumerate("qkv"):
                w = u[:, jj * 128 : (jj + 1) * 128]
                if jj < 2:
                    w = turn(w, at, 1.0)
                if jj == 0:
                    w = w * HD**-0.5
                w = w.astype(BF16)
                held[name][at, b * 128 : (b + 1) * 128] = w
                if jj >= 1:
                    held[name + "t"][b * 128 : (b + 1) * 128, at] = w.T
            return 0

        arrived("q", b)
        lax.fori_loop(0, S // QB, one, 0)

    qkv(0)
    relay("i", "z", "y", "x", 1)
    relay("d", "y", "c", "xz", 1)
    qkv(1)
    arrived("d", 0)
    arrived("d", 1)
    wd = r.wd.reshape(D, D)
    mine = pl.ds(pl.multiple_of(x * HW, HW), HW)
    r.do2[rows_mine, :] = mm(r.cot[...], wd[mine, :], NT).astype(BF16)

    r.dk[...] = jnp.zeros_like(r.dk)
    r.dv[...] = jnp.zeros_like(r.dv)
    causal = iota((QB, QB), 0) <= iota((QB, QB), 1)

    def head(blocks, h, _):
        lanes = pl.ds(pl.multiple_of((h // 2) * 128, 128), 128)
        ours = (lane // HD) == h % 2
        head_rows = pl.ds(pl.multiple_of(h * HD, HD), HD)
        for i in blocks:
            here = slice(i * QB, (i + 1) * QB)
            qm = jnp.where(ours, r.q[here, lanes], jnp.zeros((), BF16))
            dom = jnp.where(ours, r.do2[here, lanes], jnp.zeros((), BF16))
            top = None
            for j in range(i + 1):
                st = mm(r.k[j * QB : (j + 1) * QB, lanes], qm, NT)
                if j == i:
                    st = jnp.where(causal, st, NEG)
                r.st[j] = st
                part = jnp.max(st, axis=0, keepdims=True)
                top = part if top is None else jnp.maximum(top, part)
            total = du = None
            for j in range(i + 1):
                e = jnp.exp(r.st[j] - top)
                r.st[j] = e
                dp = mm(r.v[j * QB : (j + 1) * QB, lanes], dom, NT)
                r.dp[j] = dp
                part, both = (jnp.sum(w, axis=0, keepdims=True) for w in (e, e * dp))
                total = part if total is None else total + part
                du = both if du is None else du + both
            scale = 1.0 / total
            delta = du * scale
            for j in range(i + 1):
                p = r.st[j] * scale
                r.pb[j * QB : (j + 1) * QB, :] = p.astype(BF16)
                ds = p * (r.dp[j] - delta)
                r.ds[j * QB : (j + 1) * QB, :] = ds.astype(BF16)
            n = (i + 1) * QB
            pb, ds = r.pb[0:n, :], r.ds[0:n, :]
            r.ot[head_rows, here] = mm(r.vt[head_rows, 0:n], pb).astype(BF16)
            r.dqt[head_rows, here] = mm(r.kt[head_rows, 0:n], ds)
            r.dk[0:n, lanes] += mm(ds, qm)
            r.dv[0:n, lanes] += mm(pb, dom)
        return 0

    per_x = T // QB

    def attend(theirs, first, last):
        for k in range(X):
            at = (1 - k if theirs else k) * per_x
            run = functools.partial(head, range(at, at + per_x))

            @pl.when(x == k)
            def _():
                lax.fori_loop(first, last, run, 0)

    attend(False, 0, 2)
    relay("i", "y", "c", "xz", 0)
    relay("o", "z", "y", "", 0)
    relay("o", "z", "y", "", 1)
    r.hmt[...] = r.hm[...].T

    wi = r.wi.reshape(D, FH)
    wo = r.wo.reshape(FH, D)
    gi = r.gi.reshape(D, FH)
    go = r.go.reshape(FH, D)
    FB = 256

    def ff_cols(b):
        return pl.ds(pl.multiple_of(b * FB, FB), FB)

    def ff_forward(b, _):
        cols = ff_cols(b)
        f = mm(r.hm[...], wi[:, cols]) + r.vrow[6:7, cols]
        phi = 0.5 + 0.5 * lax.erf(f * (0.5**0.5))
        r.act[:, cols] = (f * phi).astype(BF16)
        r.slope[:, cols] = phi + f * (jnp.exp(-0.5 * f * f) * (0.5 / np.pi) ** 0.5)
        return 0

    arrived("i", 0)
    lax.fori_loop(0, FH // FB // 2, ff_forward, 0)
    relay("i", "y", "c", "xz", 1)
    attend(False, 2, 3)
    arrived("i", 1)
    lax.fori_loop(FH // FB // 2, FH // FB, ff_forward, 0)
    attend(False, 3, 4)
    relay("o", "y", "c", "z", 0)

    wait("cot")
    r.cots[rows_mine, :] = r.cot[...]
    r.do2[rows_theirs, :] = mm(r.cots[rows_theirs, :], wd[mine, :], NT).astype(BF16)

    def out_grad(b, _):
        at = ff_cols(b)
        go[at, :] = mm(r.act[:, at], r.cots[...], TN).astype(BF16)
        return 0

    relay("o", "y", "c", "z", 1)
    arrived("o", 0)
    arrived("o", 1)
    r.mos[...] = mm(r.act[rows_theirs, :], wo[...]).astype(BF16)
    push("mo", r.mos, r.mor, at_x)
    lax.fori_loop(0, FH // FB, out_grad, 0)
    scatter("o", "c", "", 0)
    scatter("o", "c", "", 1)

    def send_o(b):
        own_rows = slice(b * 128, (b + 1) * 128)
        to = pl.ds(pl.multiple_of(x * HW + b * 128, 128), 128)
        push(("o", b), r.ot.at[own_rows, rows_theirs], r.of.at[to, :], at_x)
        r.of[to, :] = r.ot[own_rows, rows_mine]
        r.gd.reshape(D, D)[to, :] = mm(r.ot[own_rows, :], r.cots[...]).astype(BF16)
        push(("gc", b), r.gd.at[x * (Z // X) + b, :, 1 - me["c"]], r.dc.at[b], others("c")[0])

    def gd_y(b):
        wait(("gc", b))
        at = (x * (Z // X) + b, slice(None), me["c"])
        r.gd[at] = (r.gd[at].astype(F32) + r.dc[b].astype(F32)).astype(BF16)
        push(("gy", b), r.gd.at[at[0], 1 - me["y"], me["c"]], r.dy.at[b], others("y")[0])

    def gd_x(b):
        wait(("gy", b))
        at = (x * (Z // X) + b, me["y"], me["c"])
        r.gd[at] = (r.gd[at].astype(F32) + r.dy[b].astype(F32)).astype(BF16)
        part = r.gd.at[at + (xo,)]
        push(("gx", b), part, part, at_x)

    r.vg[...] = jnp.zeros_like(r.vg)
    gq = r.gq.reshape(D, 3 * HW)

    def qkv_back(b):
        def one(i, _):
            at = pl.ds(pl.multiple_of(i * QB, QB), QB)
            cols = slice(b * 128, (b + 1) * 128)
            dq = r.dqt[cols, at].T
            out = (
                turn(dq, at, -1.0) * HD**-0.5,
                turn(r.dk[at, cols], at, -1.0),
                r.dv[at, cols],
            )
            for jj in range(3):
                w = out[jj].astype(BF16)
                to = slice(b * 384 + jj * 128, b * 384 + (jj + 1) * 128)
                r.dqkv[at, to] = w
                r.vg[4:5, to] += jnp.sum(w.astype(F32), axis=0, keepdims=True)
            return 0

        lax.fori_loop(0, S // QB, one, 0)
        cols = chunk("q", b)
        for k in range(D // QB):
            gq[k * QB : (k + 1) * QB, cols] = mm(
                r.ha[:, k * QB : (k + 1) * QB], r.dqkv[:, cols], TN
            ).astype(BF16)
        scatter("q", "c", "", b)

    attend(True, 0, 2)
    step("o", "c", "y", "", 0)
    step("o", "c", "y", "", 1)
    send_o(0)
    qkv_back(0)
    attend(True, 2, 4)
    send_o(1)
    gd_y(0)
    step("q", "c", "y", "", 0)
    step("o", "y", "z", "c", 0)
    step("o", "y", "z", "c", 1)
    qkv_back(1)
    gd_x(0)
    gd_y(1)

    def ff_backward(b, _):
        cols = ff_cols(b)
        df = (mm(r.cots[...], wo[cols, :], NT) * r.slope[:, cols]).astype(BF16)
        r.vg[6:7, cols] = jnp.sum(df.astype(F32), axis=0, keepdims=True)
        r.df[:, cols] = df
        gi[:, cols] = mm(r.hmt[...], df).astype(BF16)
        return 0

    lax.fori_loop(0, FH // FB // 2, ff_backward, 0)
    scatter("i", "c", "", 0)
    step("q", "c", "y", "", 1)
    gd_x(1)
    lax.fori_loop(FH // FB // 2, FH // FB, ff_backward, 0)
    scatter("i", "c", "", 1)
    step("i", "c", "y", "", 0)

    def input_grads(base, mine_too):
        def one(i, _):
            at = pl.ds(pl.multiple_of(base + i * QB, QB), QB)
            to = pl.ds(pl.multiple_of(i * QB, QB), QB)
            n = r.n[at, :]
            dm = mm(r.df[at, :], wi[...], NT)
            r.vg[2:3, 0:D] += jnp.sum(dm * n, axis=0, keepdims=True)
            r.vg[3:4, 0:D] += jnp.sum(dm, axis=0, keepdims=True)
            dh = mm(r.dqkv[at, :], wq[...], NT)
            r.vg[0:1, 0:D] += jnp.sum(dh * n, axis=0, keepdims=True)
            r.vg[1:2, 0:D] += jnp.sum(dh, axis=0, keepdims=True)
            u = dh * row(0) + dm * row(2)
            if mine_too:
                r.u[to, :] = u
            else:
                r.us[to, :] = u.astype(BF16)
            return 0

        lax.fori_loop(0, T // QB, one, 0)

    input_grads(xo * T, False)
    for k in range(T // QB):
        part = slice(k * QB, (k + 1) * QB)
        push(("u", k), r.us.at[part, :], r.ur.at[part, :], at_x)
    step("i", "c", "y", "", 1)
    step("q", "y", "z", "c", 0)
    step("q", "y", "z", "c", 1)
    input_grads(x * T, True)

    g_sum = jnp.sum(r.cot[...].astype(F32), axis=0, keepdims=True)
    r.vg[5:6, 0:D] = g_sum
    r.vg[7:8, 0:D] = g_sum
    gv2 = r.gv.reshape(N * 8, 128)

    def collapse(v):
        n = lengths(v)
        j = column(v, n)
        pick = (iota((128, n), 0) == j % widths[v]).astype(F32).astype(BF16)
        left = jnp.where(iota((N, n), 0) == j // widths[v], r.vg[v : v + 1, 0:n], 0.0)
        acc = None
        for _ in range(3):
            low = left.astype(BF16)
            part = mm(low, pick, NT)
            acc = part if acc is None else acc + part
            left = left - low.astype(F32)
        gv2[pl.ds(v, N, stride=8), :] = acc

    for v in range(8):
        collapse(v)
    scatter("v", "c", "")
    wait(("gx", 0))
    wait(("gx", 1))
    scatter("d", "z", "cyx")
    step("i", "y", "z", "c", 0)
    r.mo[...] = mm(r.act[rows_mine, :], wo[...])
    step("i", "y", "z", "c", 1)

    def flat(out, width, k=None, part=D):
        per = width // 128
        n = out.shape[0] // per
        lo = 0 if k is None else k * (part // 128)

        def put(acc):
            for j in range(acc.shape[1] // 128):
                out[pl.ds(lo + j, n, stride=per), :] = acc[:, j * 128 : (j + 1) * 128]

        return put

    step("v", "c", "y")
    add_parts("o", "z", "cy", 0, flat(r.oo, D, 0, CH["o"]))
    add_parts("o", "z", "cy", 1, flat(r.oo, D, 1, CH["o"]))
    at_me = (me["z"], me["y"], me["c"])
    step("v", "y", "z", "c")
    add_parts("q", "z", "cy", 0)
    add_parts("q", "z", "cy", 1)
    push("sq", r.gq.at[at_me + (xo,)], r.xq, at_x)

    wait(("o", 0))
    wait(("o", 1))
    wait("mo")
    r.out[...] = (
        r.tokens[...].astype(F32)
        + mm(r.of[...], wd[...], TN)
        + row(5)
        + (r.mo[...] + r.mor[...].astype(F32) + row(7))
    ).astype(BF16)
    step("v", "z", "x", "cy")
    add_parts("d", "z", "cyx", None, flat(r.od, D))
    add_parts("i", "z", "cy", 0)
    add_parts("i", "z", "cy", 1)
    push("si", r.gi.at[at_me + (xo,)], r.xi, at_x)


    def final_rows(i, _):
        at = pl.ds(pl.multiple_of(i * RC, RC), RC)
        far = pl.ds(pl.multiple_of(x * T + i * RC, RC), RC)
        u = r.u[at, :] + r.ur[at, :].astype(F32)
        n = r.n[far, :]
        back = u - jnp.mean(u, axis=-1, keepdims=True) - n * jnp.mean(u * n, axis=-1, keepdims=True)
        r.gtok[at, :] = (r.cot[at, :].astype(F32) + back * r.scale[at, 0:1]).astype(BF16)
        return 0

    for k in range(T // QB):
        wait(("u", k))
        lax.fori_loop(k * (QB // RC), (k + 1) * (QB // RC), final_rows, 0)

    def join(mine_ref, got, out, width, place):
        per = width // 128
        n = out.shape[0] // per
        here = mine_ref[at_me + (x,)].astype(F32)
        there = got[...].astype(F32)
        halves = (jnp.where(x == 0, here, there), jnp.where(x == 0, there, here))

        def piece(b, to_high):
            half, m, odd = place(b)
            v = halves[half][:, m * 128 : (m + 1) * 128]
            return pltpu.roll(v, 64, 1) if odd != to_high else v

        for j in range(per):
            both = jnp.where(lane < 64, piece(2 * j, False), piece(2 * j + 1, True))
            out[pl.ds(j, n, stride=per), :] = both

    def place_q(b):
        h, jj = b // 3, b % 3
        return h // HC, (h % HC) // 2 * 3 + jj, h % 2 == 1

    def place_i(b):
        return b % 2, b // 4, (b // 2) % 2 == 1

    wait("sq")
    join(r.gq, r.xq, r.oq, 3 * D, place_q)
    wait("si")
    join(r.gi, r.xi, r.oi, FF, place_i)

    def put_vec(acc):
        r.ov[...] = acc

    add_parts("v", "x", "cyz", None, put_vec)


def rope_table(length):
    lanes = np.arange(128) % HD
    rot = HD // 4
    inverse = np.where(lanes < rot, 1.0 / ROPE_BASE ** (2.0 * (lanes % (rot // 2)) / rot), 0.0)
    high = 32.0 * np.arange(length // 32)[:, None] * inverse
    low = np.arange(32)[:, None] * inverse
    return np.stack([np.cos(high), np.sin(high), np.cos(low), np.sin(low)]).astype(np.float32)


def hand_over(*refs):
    for src, dst in zip(refs[:6], refs[7:13]):
        dst[...] = src[...]
    for v, dst in enumerate(refs[13:]):
        dst[...] = refs[6][v : v + 1, 0 : dst.shape[1]]


def layer(sizes, tokens, cotangent, *params):
    Z, Y, C, X = (sizes[a] for a in AX)
    N = Z * Y * C * X
    T = tokens.shape[1]
    S = T * X
    HW = HEADS // X * HD
    vectors = [params[i] for i in (0, 1, 2, 3, 5, 7, 9, 11)]
    weights = [params[i] for i in (4, 6, 8, 10)]
    flats = [w.reshape(-1, 128) for w in weights]
    full = dict(z=Z, y=Y, c=C, x=X)

    FH = FF // X

    def parts(name, axis, done, slab, dtype):
        free = [full[a] for a in AX if a not in done and a != axis and (a != "x" or name != "o")]
        return pltpu.VMEM((full[axis] - 1, *free, *slab), dtype)

    slabs = {
        "q": (D // N, 3 * HW),
        "d": (D // N, D),
        "i": (D // N, FH),
        "o": (FF // N, D),
        "v": (8, 128),
    }
    orders = {"q": "cyz", "d": "z", "i": "cyz", "o": "cyz", "v": "cyzx"}
    keep = types.SimpleNamespace()
    scratch = vars(keep)
    for k, slab in slabs.items():
        kind = F32 if k == "v" else BF16
        devs = (Z, Y, C) if k == "o" else (Z, Y, C, X)
        scratch["w" + k] = pltpu.VMEM((*devs, *slab), kind)
        scratch["g" + k] = pltpu.VMEM((*devs, *slab), kind)
        for n, axis in enumerate(orders[k]):
            done = "cyx" if k == "d" else orders[k][:n]
            scratch["r" + k + axis] = parts(k, axis, done, slab, kind)
    keep.dc = pltpu.VMEM((X, Y, X, *slabs["d"]), BF16)
    keep.dy = pltpu.VMEM((X, X, *slabs["d"]), BF16)
    keep.xq = pltpu.VMEM(slabs["q"], BF16)
    keep.xi = pltpu.VMEM(slabs["i"], BF16)
    keep.sq = pltpu.VMEM((X, *slabs["q"]), BF16)
    keep.si = pltpu.VMEM((X, *slabs["i"]), BF16)
    keep.tmp = pltpu.VMEM((max(f.shape[0] for f in flats), 128), F32)
    keep.cos = keep.sinl = keep.sinh = pltpu.VMEM((S, 128), F32)
    keep.tok2 = pltpu.VMEM((T, D), BF16)
    keep.cots = pltpu.VMEM((S, D), BF16)
    keep.n = pltpu.VMEM((S, D), F32)
    keep.scale = pltpu.VMEM((T, 128), F32)
    keep.vrow = pltpu.VMEM((8, FH), F32)
    keep.vg = pltpu.VMEM((8, FH), F32)
    keep.ha = keep.hm = pltpu.VMEM((S, D), BF16)
    keep.hmt = pltpu.VMEM((D, S), BF16)
    keep.q = keep.k = keep.v = keep.do2 = pltpu.VMEM((S, HW), BF16)
    keep.kt = keep.vt = keep.ot = pltpu.VMEM((HW, S), BF16)
    keep.dqt = pltpu.VMEM((HW, S), F32)
    keep.dk = pltpu.VMEM((S, HW), F32)
    keep.dv = pltpu.VMEM((S, HW), F32)
    keep.st = pltpu.VMEM((S // QB, QB, QB), F32)
    keep.dp = pltpu.VMEM((S // QB, QB, QB), F32)
    keep.pb = pltpu.VMEM((S, QB), BF16)
    keep.ds = pltpu.VMEM((S, QB), BF16)
    keep.dqkv = pltpu.VMEM((S, 3 * HW), BF16)
    keep.of = pltpu.VMEM((D, T), BF16)
    keep.act = keep.df = pltpu.VMEM((S, FH), BF16)
    keep.slope = pltpu.VMEM((S, FH), F32)
    keep.u = keep.mo = pltpu.VMEM((T, D), F32)
    keep.us = keep.ur = keep.mos = keep.mor = pltpu.VMEM((T, D), BF16)
    copies = 128
    keep.send = pltpu.SemaphoreType.DMA((copies,))
    keep.recv = pltpu.SemaphoreType.DMA((copies,))
    ins = "tokens cot fq fd".split() + "fi fo rope".split() + ["v%d" % v for v in range(8)]
    outs = dict(
        out=jax.ShapeDtypeStruct((T, D), BF16),
        gtok=jax.ShapeDtypeStruct((T, D), BF16),
        oq=jax.ShapeDtypeStruct(flats[0].shape, F32),
        od=jax.ShapeDtypeStruct(flats[1].shape, F32),
        oi=jax.ShapeDtypeStruct(flats[2].shape, F32),
        oo=jax.ShapeDtypeStruct(flats[3].shape, F32),
        ov=jax.ShapeDtypeStruct((8, 128), F32),
    )
    vmem = pl.BlockSpec(memory_space=pltpu.VMEM)
    shown = tokens.reshape(T, D), cotangent.reshape(T, D), *flats, jnp.asarray(rope_table(S))
    shown += tuple(v.reshape(1, -1) for v in vectors)
    for name, a in zip(ins, shown):
        scratch[name] = pltpu.VMEM(a.shape, a.dtype)
    keep.load = pltpu.SemaphoreType.DMA((len(ins),))
    names = ["h" + n for n in ins] + list(outs) + list(scratch)
    out, gtok, gq, gd, gi, go, gv = pl.pallas_call(
        functools.partial(fused, sizes, names),
        out_shape=list(outs.values()),
        in_specs=[pl.BlockSpec(memory_space=pl.ANY)] * len(ins),
        out_specs=[vmem] * len(outs),
        scratch_shapes=list(scratch.values()),
        compiler_params=pltpu.CompilerParams(
            collective_id=0, has_side_effects=True, vmem_limit_bytes=67043328
        ),
        name="layer",
    )(
        *shown
    )
    shapes = [jax.ShapeDtypeStruct(a.shape, a.dtype) for a in (out, gtok, gq, gd, gi, go)]
    shapes += [jax.ShapeDtypeStruct((1, p.shape[0]), F32) for p in vectors]
    out, gtok, gq, gd, gi, go, *v = pl.pallas_call(
        hand_over,
        out_shape=shapes,
        in_specs=[vmem] * 7,
        out_specs=[vmem] * len(shapes),
        name="results",
    )(out, gtok, gq, gd, gi, go, gv)
    v = [a.reshape(-1) for a in v]
    return (
        out.reshape(tokens.shape),
        gtok.reshape(tokens.shape),
        v[0],
        v[1],
        v[2],
        v[3],
        gq.reshape(-1),
        v[4],
        gd.reshape(-1),
        v[5],
        gi.reshape(-1),
        v[6],
        go.reshape(-1),
        v[7],
    )


def solution(mesh):
    n_seq, n_ctx = mesh.shape["seq"], mesh.shape["ctx"]
    if n_ctx != 2 or n_seq != 16 or (D // (n_seq * n_ctx)) % 16:
        return general(mesh)
    sizes = {"z": n_seq // 4, "y": 2, "c": 2, "x": n_ctx}
    flat = P(("seq", "ctx"))
    rows = P("seq", "ctx", None)
    return jax.shard_map(
        functools.partial(layer, sizes),
        mesh=mesh,
        in_specs=(rows, rows) + (flat,) * 12,
        out_specs=(rows, rows) + (flat,) * 12,
        check_vma=False,
    )
```

```python
import functools
import types

import jax
import jax.numpy as jnp
import numpy as np
from jax import lax
from jax.experimental import pallas as pl
from jax.experimental.pallas import tpu as pltpu
from jax.sharding import PartitionSpec as P

D = 512
HEADS = 8
FF = 2048


EPS = 1e-05
BOTH = ("seq", "ctx")
ROPE_BASE = 10000.0
NEG = -1e30


def layer_normalize(values, gain, bias):
    mean = jnp.mean(values, axis=-1, keepdims=True)
    centered = values - mean
    var = jnp.mean(centered * centered, axis=-1, keepdims=True)
    return centered * lax.rsqrt(var + EPS) * gain + bias


def rotate(values, cosine, sine):
    width = cosine.shape[-1]
    half = width // 2
    part = values[..., :width]
    turned = jnp.concatenate([-part[..., half:], part[..., :half]], axis=-1)
    return jnp.concatenate([part * cosine + turned * sine, values[..., width:]], axis=-1)


def gelu_exact(values):
    return jax.nn.gelu(values, approximate=False)


def matrices(mix_flat, proj_flat, expand_flat, reduce_flat):
    return (
        mix_flat.reshape(D, 3 * D),
        proj_flat.reshape(D, D),
        expand_flat.reshape(D, FF),
        reduce_flat.reshape(FF, D),
    )


def body(
    tokens,
    cotangent,
    attn_norm_gain,
    attn_norm_bias,
    mlp_norm_gain,
    mlp_norm_bias,
    qkv_weight,
    qkv_bias,
    dense_weight,
    dense_bias,
    fc_in_weight,
    fc_in_bias,
    fc_out_weight,
    fc_out_bias,
):
    (
        gain_attn,
        attention_shift,
        gain_mlp,
        shift_mlp,
        mix_flat,
        mix_bias,
        proj_flat,
        proj_bias,
        expand_flat,
        expand_bias,
        reduce_flat,
        reduce_bias,
    ) = (
        lax.all_gather(attn_norm_gain, BOTH, axis=0, tiled=True),
        lax.all_gather(attn_norm_bias, BOTH, axis=0, tiled=True),
        lax.all_gather(mlp_norm_gain, BOTH, axis=0, tiled=True),
        lax.all_gather(mlp_norm_bias, BOTH, axis=0, tiled=True),
        lax.all_gather(qkv_weight, BOTH, axis=0, tiled=True),
        lax.all_gather(qkv_bias, BOTH, axis=0, tiled=True),
        lax.all_gather(dense_weight, BOTH, axis=0, tiled=True),
        lax.all_gather(dense_bias, BOTH, axis=0, tiled=True),
        lax.all_gather(fc_in_weight, BOTH, axis=0, tiled=True),
        lax.all_gather(fc_in_bias, BOTH, axis=0, tiled=True),
        lax.all_gather(fc_out_weight, BOTH, axis=0, tiled=True),
        lax.all_gather(fc_out_bias, BOTH, axis=0, tiled=True),
    )
    mix_weight, proj_weight, expand_weight, reduce_weight = matrices(
        mix_flat, proj_flat, expand_flat, reduce_flat
    )
    shape = tokens.shape
    group = shape[1]
    width = shape[2]
    heads = HEADS
    head_dim = width // heads
    rows = tokens.reshape(group, width).astype(jnp.float32)
    attn_in, attn_norm_back = jax.vjp(
        layer_normalize, rows, gain_attn.astype(jnp.float32), attention_shift.astype(jnp.float32)
    )
    mlp_in, mlp_norm_back = jax.vjp(
        layer_normalize, rows, gain_mlp.astype(jnp.float32), shift_mlp.astype(jnp.float32)
    )
    attn_low = attn_in.astype(jnp.bfloat16)
    mlp_low = mlp_in.astype(jnp.bfloat16)
    mixed = jnp.dot(attn_low, mix_weight, preferred_element_type=jnp.float32) + mix_bias.astype(
        jnp.float32
    )
    mixed = mixed.reshape(group, heads, 3, head_dim)
    place = lax.axis_index("ctx")
    blocks_total = lax.axis_size("ctx")
    local_pos = jnp.arange(group, dtype=jnp.int32)
    query_pos = place * group + local_pos
    rot_dims = head_dim // 4
    inverse = 1.0 / ROPE_BASE ** (
        jnp.arange(0, rot_dims, 2, dtype=jnp.int32).astype(jnp.float32) / rot_dims
    )
    angles = query_pos.astype(jnp.float32)[:, None] * inverse[None, :]
    angles = jnp.concatenate([angles, angles], axis=-1)
    cosine = jnp.cos(angles)[:, None, :]
    sine = jnp.sin(angles)[:, None, :]
    scale = head_dim ** (-0.5)

    def turn(query_unrotated, key_raw):
        return (rotate(query_unrotated, cosine, sine) * scale, rotate(key_raw, cosine, sine))

    (query_f, key_f), turn_back = jax.vjp(turn, mixed[:, :, 0], mixed[:, :, 1])
    query = query_f.astype(jnp.bfloat16)
    key_own = key_f.astype(jnp.bfloat16).reshape(group, width)
    value_own = mixed[:, :, 2].astype(jnp.bfloat16).reshape(group, width)
    all_keys, all_values = (
        lax.all_gather(key_own, "ctx", axis=0, tiled=True),
        lax.all_gather(value_own, "ctx", axis=0, tiled=True),
    )
    count = place + 1

    def block(index):
        keys = lax.dynamic_slice_in_dim(all_keys, index * group, group, 0).reshape(
            group, heads, head_dim
        )
        values = lax.dynamic_slice_in_dim(all_values, index * group, group, 0).reshape(
            group, heads, head_dim
        )
        scores = jnp.einsum("qhd,khd->hqk", query, keys, preferred_element_type=jnp.float32)
        allowed = (index * group + local_pos)[None, :] <= query_pos[:, None]
        return (keys, values, scores, allowed[None])

    def max_step(index, carry):
        top, total = carry
        _, _, scores, allowed = block(index)
        new_top = jnp.maximum(top, jnp.max(jnp.where(allowed, scores, NEG), axis=-1))
        terms = jnp.where(allowed, jnp.exp(scores - new_top[:, :, None]), 0.0)
        return (new_top, total * jnp.exp(top - new_top) + jnp.sum(terms, axis=-1))

    start = (jnp.full((heads, group), NEG, jnp.float32), jnp.zeros((heads, group), jnp.float32))
    top, total = lax.fori_loop(0, count, max_step, start)
    log_total = top + jnp.log(total)

    def probs_of(scores, allowed):
        return jnp.where(allowed, jnp.exp(scores - log_total[:, :, None]), 0.0)

    def out_step(index, acc):
        _, values, scores, allowed = block(index)
        probs = probs_of(scores, allowed).astype(jnp.bfloat16)
        return acc + jnp.einsum("hqk,khd->qhd", probs, values, preferred_element_type=jnp.float32)

    heads_out = lax.fori_loop(0, count, out_step, jnp.zeros((group, heads, head_dim), jnp.float32))
    attn_out = heads_out.reshape(group, width).astype(jnp.bfloat16)
    branch_attn = jnp.dot(
        attn_out, proj_weight, preferred_element_type=jnp.float32
    ) + proj_bias.astype(jnp.float32)
    expand = jnp.dot(
        mlp_low, expand_weight, preferred_element_type=jnp.float32
    ) + expand_bias.astype(jnp.float32)
    active_rows, active_back = jax.vjp(gelu_exact, expand)
    active_low = active_rows.astype(jnp.bfloat16)
    branch_mlp = jnp.dot(
        active_low, reduce_weight, preferred_element_type=jnp.float32
    ) + reduce_bias.astype(jnp.float32)
    layer_out = (rows + branch_attn + branch_mlp).astype(jnp.bfloat16).reshape(shape)
    back_mix, back_proj, back_expand, back_reduce = (
        lax.all_gather(qkv_weight, BOTH, axis=0, tiled=True),
        lax.all_gather(dense_weight, BOTH, axis=0, tiled=True),
        lax.all_gather(fc_in_weight, BOTH, axis=0, tiled=True),
        lax.all_gather(fc_out_weight, BOTH, axis=0, tiled=True),
    )
    back_mix, back_proj, back_expand, back_reduce = matrices(
        back_mix, back_proj, back_expand, back_reduce
    )
    grad_rows = cotangent.reshape(group, width)
    grad_float = grad_rows.astype(jnp.float32)
    grad_reduce = jnp.einsum("tf,td->fd", active_low, grad_rows, preferred_element_type=jnp.float32)
    grad_out_bias = jnp.sum(grad_float, axis=0)
    grad_proj = jnp.einsum("te,td->ed", attn_out, grad_rows, preferred_element_type=jnp.float32)
    grad_active = jnp.einsum(
        "td,fd->tf", grad_rows, back_reduce, preferred_element_type=jnp.float32
    )
    grad_expand = active_back(grad_active)[0].astype(jnp.bfloat16)
    grad_expand_w = jnp.einsum(
        "td,tf->df", mlp_low, grad_expand, preferred_element_type=jnp.float32
    )
    grad_expand_b = jnp.sum(grad_expand.astype(jnp.float32), axis=0)
    grad_mlp_in = jnp.einsum(
        "tf,df->td", grad_expand, back_expand, preferred_element_type=jnp.float32
    )
    grad_heads = jnp.einsum("td,ed->te", grad_rows, back_proj, preferred_element_type=jnp.float32)
    grad_heads = grad_heads.astype(jnp.bfloat16).reshape(group, heads, head_dim)

    def delta_step(index, acc):
        _, values, scores, allowed = block(index)
        probs = probs_of(scores, allowed)
        grad_probs = jnp.einsum(
            "qhd,khd->hqk", grad_heads, values, preferred_element_type=jnp.float32
        )
        return acc + jnp.sum(probs * grad_probs, axis=-1)

    delta = lax.fori_loop(0, count, delta_step, jnp.zeros((heads, group), jnp.float32))

    def query_step(index, grad_query):
        keys, values, scores, allowed = block(index)
        probs = probs_of(scores, allowed)
        grad_probs = jnp.einsum(
            "qhd,khd->hqk", grad_heads, values, preferred_element_type=jnp.float32
        )
        grad_scores = (probs * (grad_probs - delta[:, :, None])).astype(jnp.bfloat16)
        return grad_query + jnp.einsum(
            "hqk,khd->qhd", grad_scores, keys, preferred_element_type=jnp.float32
        )

    grad_query = lax.fori_loop(
        0, count, query_step, jnp.zeros((group, heads, head_dim), jnp.float32)
    )
    all_queries, all_grad_heads = (
        lax.all_gather(query.reshape(group, width), "ctx", axis=0, tiled=True),
        lax.all_gather(grad_heads.reshape(group, width), "ctx", axis=0, tiled=True),
    )
    gathered_log_sums, all_delta = (
        lax.all_gather(jnp.transpose(log_total), "ctx", axis=0, tiled=True),
        lax.all_gather(jnp.transpose(delta), "ctx", axis=0, tiled=True),
    )
    keys_mine = key_own.reshape(group, heads, head_dim)
    values_mine = value_own.reshape(group, heads, head_dim)

    def owner_step(index, carry):
        key_acc, value_accumulator = carry
        queries = lax.dynamic_slice_in_dim(all_queries, index * group, group, 0).reshape(
            group, heads, head_dim
        )
        outer_grads = lax.dynamic_slice_in_dim(all_grad_heads, index * group, group, 0).reshape(
            group, heads, head_dim
        )
        lse_rows = jnp.transpose(
            lax.dynamic_slice_in_dim(gathered_log_sums, index * group, group, 0)
        )
        delta_rows = jnp.transpose(lax.dynamic_slice_in_dim(all_delta, index * group, group, 0))
        scores = jnp.einsum("qhd,khd->hqk", queries, keys_mine, preferred_element_type=jnp.float32)
        allowed = (query_pos[None, :] <= (index * group + local_pos)[:, None])[None]
        probs = jnp.where(allowed, jnp.exp(scores - lse_rows[:, :, None]), 0.0)
        grad_probs = jnp.einsum(
            "qhd,khd->hqk", outer_grads, values_mine, preferred_element_type=jnp.float32
        )
        grad_scores = (probs * (grad_probs - delta_rows[:, :, None])).astype(jnp.bfloat16)
        key_acc = key_acc + jnp.einsum(
            "hqk,qhd->khd", grad_scores, queries, preferred_element_type=jnp.float32
        )
        value_accumulator = value_accumulator + jnp.einsum(
            "hqk,qhd->khd",
            probs.astype(jnp.bfloat16),
            outer_grads,
            preferred_element_type=jnp.float32,
        )
        return (key_acc, value_accumulator)

    empty_heads = jnp.zeros((group, heads, head_dim), jnp.float32)
    own_key_grad, own_value_grad = lax.fori_loop(
        place, blocks_total, owner_step, (empty_heads, empty_heads)
    )
    grad_query_raw, grad_key_raw = turn_back((grad_query, own_key_grad))
    grad_mixed = jnp.stack([grad_query_raw, grad_key_raw, own_value_grad], axis=2)
    grad_mixed = grad_mixed.reshape(group, 3 * width).astype(jnp.bfloat16)
    grad_mix_w = jnp.einsum("td,te->de", attn_low, grad_mixed, preferred_element_type=jnp.float32)
    grad_mix_b = jnp.sum(grad_mixed.astype(jnp.float32), axis=0)
    grad_attn_in = jnp.einsum("te,de->td", grad_mixed, back_mix, preferred_element_type=jnp.float32)
    input_attn, gain_attn_grad, shift_attn_grad = attn_norm_back(grad_attn_in)
    input_mlp, gain_mlp_grad, shift_mlp_grad = mlp_norm_back(grad_mlp_in)
    grad_tokens = (grad_float + input_attn + input_mlp).astype(jnp.bfloat16).reshape(shape)
    sums = (
        lax.psum_scatter(gain_attn_grad, BOTH, scatter_dimension=0, tiled=True),
        lax.psum_scatter(shift_attn_grad, BOTH, scatter_dimension=0, tiled=True),
        lax.psum_scatter(gain_mlp_grad, BOTH, scatter_dimension=0, tiled=True),
        lax.psum_scatter(shift_mlp_grad, BOTH, scatter_dimension=0, tiled=True),
        lax.psum_scatter(grad_mix_w.reshape(-1), BOTH, scatter_dimension=0, tiled=True),
        lax.psum_scatter(grad_mix_b, BOTH, scatter_dimension=0, tiled=True),
        lax.psum_scatter(grad_proj.reshape(-1), BOTH, scatter_dimension=0, tiled=True),
        lax.psum_scatter(grad_out_bias, BOTH, scatter_dimension=0, tiled=True),
        lax.psum_scatter(
            grad_expand_w.reshape(-1), BOTH, scatter_dimension=0, tiled=True
        ),
        lax.psum_scatter(grad_expand_b, BOTH, scatter_dimension=0, tiled=True),
        lax.psum_scatter(grad_reduce.reshape(-1), BOTH, scatter_dimension=0, tiled=True),
        lax.psum_scatter(grad_out_bias, BOTH, scatter_dimension=0, tiled=True),
    )
    return (
        layer_out,
        grad_tokens,
        sums[0],
        sums[1],
        sums[2],
        sums[3],
        sums[4],
        sums[5],
        sums[6],
        sums[7],
        sums[8],
        sums[9],
        sums[10],
        sums[11],
    )


def general(mesh):
    return jax.shard_map(
        body,
        mesh=mesh,
        in_specs=(
            P("seq", "ctx", None),
            P("seq", "ctx", None),
            P(BOTH),
            P(BOTH),
            P(BOTH),
            P(BOTH),
            P(BOTH),
            P(BOTH),
            P(BOTH),
            P(BOTH),
            P(BOTH),
            P(BOTH),
            P(BOTH),
            P(BOTH),
        ),
        out_specs=(
            P("seq", "ctx", None),
            P("seq", "ctx", None),
            P(BOTH),
            P(BOTH),
            P(BOTH),
            P(BOTH),
            P(BOTH),
            P(BOTH),
            P(BOTH),
            P(BOTH),
            P(BOTH),
            P(BOTH),
            P(BOTH),
            P(BOTH),
        ),
        check_vma=False,
    )


MESH = pl.DeviceIdType.MESH
F32, BF16 = jnp.float32, jnp.bfloat16
HD = D // HEADS
AX = "zycx"
NN = (((1,), (0,)), ((), ()))
NT = (((1,), (1,)), ((), ()))
TN = (((0,), (0,)), ((), ()))
QB = 256


def mm(a, b, dims=NN):
    return lax.dot_general(a, b, dims, preferred_element_type=F32)


def iota(shape, dim):
    return lax.broadcasted_iota(jnp.int32, shape, dim)


def fused(sizes, names, *refs):
    held = dict(zip(names, refs))
    r = types.SimpleNamespace(**held)
    X = sizes["x"]
    C = sizes["c"]
    Y = sizes["y"]
    Z = sizes["z"]
    N = Z * Y * C * X
    T = held["tokens"].shape[0]
    S = T * X
    HC = HEADS // X
    HW = HC * HD
    FH = FF // X
    CH = dict(q=384, i=FH // 2, o=D // 2, d=D // 2)
    s = lax.axis_index("seq")
    me = {"x": lax.axis_index("ctx"), "c": s % C, "y": (s // C) % Y, "z": s // (C * Y)}
    x = me["x"]
    xo = 1 - x

    def device(at):
        return ((at["z"] * Y + at["y"]) * C + at["c"], at["x"])

    def others(axis):
        n = sizes[axis]
        return [dict(me, **{axis: (me[axis] + d) % n}) for d in range(1, n)]

    flight = {}
    count = [0]

    def push(key, src, dst, at):
        k = count[0]
        count[0] += 1
        cp = pltpu.make_async_remote_copy(
            src_ref=src,
            dst_ref=dst,
            send_sem=r.send.at[k],
            recv_sem=r.recv.at[k],
            device_id=device(at),
            device_id_type=MESH,
        )
        cp.start()
        flight.setdefault(key, []).append(cp)

    def wait(key):
        for cp in flight.pop(key):
            cp.wait()

    def axes(name):
        return AX[: 3 if name == "o" else 4]

    def chunk(name, k):
        if k is None:
            return slice(None)
        w = CH[name]
        return slice(k * w, (k + 1) * w)

    def gather(name, axis, known, k=None):
        ref = held["w" + name]
        spot = tuple(slice(None) if a in known else me[a] for a in axes(name))
        part = ref.at[spot + (slice(None), chunk(name, k))]
        for at in others(axis):
            push(("w", name, axis, k), part, part, at)

    def relay(name, axis, nxt, known, k=None):
        wait(("w", name, axis, k))
        gather(name, nxt, known + axis, k)

    def arrived(name, k=None):
        wait(("w", name, "c", k))

    def scatter(name, axis, done, k=None):
        ref, got = held["g" + name], held["r" + name + axis]
        free = [a for a in axes(name) if a not in done and a != axis]
        cols = (slice(None), chunk(name, k))
        for n, at in enumerate(others(axis)):
            spot = tuple(slice(None) if a in free else at[a] for a in axes(name))
            to = (n,) + (slice(None),) * len(free)
            push(("g", name, axis, k), ref.at[spot + cols], got.at[to + cols], at)

    def add_parts(name, axis, done, k=None, finish=None):
        wait(("g", name, axis, k))
        ref, got = held["g" + name], held["r" + name + axis]
        free = [a for a in axes(name) if a not in done and a != axis]
        cols = (slice(None), chunk(name, k))
        total = 1
        for a in free:
            total *= sizes[a]

        def one(i, _):
            at, rest = dict(me), i
            for a in reversed(free):
                at[a] = rest % sizes[a]
                rest = rest // sizes[a]
            spot = tuple(at[a] for a in axes(name))
            inner = tuple(at[a] for a in free)
            acc = ref[spot + cols].astype(F32)
            for n in range(sizes[axis] - 1):
                acc = acc + got[(n,) + inner + cols].astype(F32)
            if finish is None:
                ref[spot + cols] = acc.astype(ref.dtype)
            else:
                finish(acc)
            return 0

        if total == 1:
            one(0, 0)
        else:
            lax.fori_loop(0, total, one, 0)

    def step(name, axis, nxt, done="", k=None):
        add_parts(name, axis, done, k)
        scatter(name, nxt, done + axis, k)

    barrier = pltpu.get_barrier_semaphore()
    greet = [at for a in AX for at in others(a)]
    for at in greet:
        pl.semaphore_signal(barrier, inc=1, device_id=device(at), device_id_type=MESH)
    loads = {}
    for k, name in enumerate(n for n in names if ("h" + n) in held):
        loads[name] = pltpu.make_async_copy(held["h" + name], held[name], r.load.at[k])
        loads[name].start()

    def loaded(*which):
        for name in which:
            loads[name].wait()

    loaded("fq", "fi", "fd", *["v%d" % v for v in range(8)])

    tmp = r.tmp
    lane = iota((1, 128), 1)

    def own(name):
        return held[name].at[me["z"], me["y"], me["c"], x]

    def block64(b, per, rows, to_high):
        v = tmp[pl.ds(b // 2, rows, stride=per), :]
        return pltpu.roll(v, 64, 1) if (b % 2 == 1) != to_high else v

    def split(src, dst, width, table):
        n = held[src].shape[0]
        per = width // 128
        tmp[0:n, :] = held[src][...].astype(F32)
        for half in range(X):
            for m in range(per // X):
                low, high = table(half, m)
                low = block64(low, per, n // per, False)
                high = block64(high, per, n // per, True)
                dst[half, :, m * 128 : (m + 1) * 128] = jnp.where(lane < 64, low, high).astype(BF16)

    def table_q(half, m):
        h0 = half * HC + 2 * (m // 3)
        return 3 * h0 + m % 3, 3 * (h0 + 1) + m % 3

    def table_i(half, m):
        return 4 * m + half, 4 * m + 2 + half

    def reshard(src, dst, width):
        n = held[src].shape[0]
        k = width // 128
        tmp[0:n, :] = held[src][...].astype(F32)
        for j in range(k):
            dst[:, j * 128 : (j + 1) * 128] = tmp[pl.ds(j, n // k, stride=k), :].astype(BF16)

    split("fq", r.sq, 3 * D, table_q)
    split("fi", r.si, FF, table_i)
    reshard("fd", own("wd"), D)
    vecs = own("wv")
    vecs[...] = jnp.zeros_like(vecs)
    for v in range(8):
        vin = held["v%d" % v]
        vecs[v : v + 1, 0 : vin.shape[1]] = vin[...].astype(F32)
    own("wq")[...] = r.sq[x]
    own("wi")[...] = r.si[x]

    loaded("tokens", "cot", "fo", "rope")
    pl.semaphore_wait(barrier, len(greet))

    rows_mine = pl.ds(pl.multiple_of(x * T, T), T)
    rows_theirs = pl.ds(pl.multiple_of(xo * T, T), T)
    at_x = others("x")[0]
    gather("v", "x", "")
    push("sq", r.sq.at[xo], own("wq"), at_x)
    push("si", r.si.at[xo], own("wi"), at_x)
    gather("d", "x", "")
    push("tok", r.tokens, r.tok2, at_x)
    push("cot", r.cot, r.cots.at[rows_mine, :], at_x)
    reshard("fo", r.wo.at[me["z"], me["y"], me["c"]], D)

    rope = r.rope
    mod = lane % HD

    def rope_rows(i, _):
        ch, sh = rope[0, pl.ds(i, 1), :], rope[1, pl.ds(i, 1), :]
        cl, sl = rope[2], rope[3]
        sine = sh * cl + ch * sl
        at = pl.ds(pl.multiple_of(i * 32, 32), 32)
        r.cos[at, :] = ch * cl - sh * sl
        r.sinl[at, :] = jnp.where(mod < 8, -sine, 0.0)
        r.sinh[at, :] = jnp.where(mod < 8, 0.0, sine)
        return 0

    def turn(u, at, sign):
        return (
            u * r.cos[at, :]
            + sign * (pltpu.roll(u, 120, 1) * r.sinl[at, :] + pltpu.roll(u, 8, 1) * r.sinh[at, :])
        )

    relay("v", "x", "z", "")
    wait("sq")
    gather("q", "z", "x", 0)
    gather("q", "z", "x", 1)
    wait(("w", "d", "x", None))
    gather("d", "z", "x", 0)
    gather("d", "z", "x", 1)
    wait("si")
    gather("i", "z", "x", 0)
    gather("i", "z", "x", 1)
    gather("o", "z", "", 0)
    gather("o", "z", "", 1)
    lax.fori_loop(0, S // 32, rope_rows, 0)

    RC = 128

    def norm_rows(src, base, keep):
        def one(i, _):
            v = src[pl.ds(pl.multiple_of(i * RC, RC), RC), :].astype(F32)
            c = v - jnp.mean(v, axis=-1, keepdims=True)
            scale = lax.rsqrt(jnp.mean(c * c, axis=-1, keepdims=True) + EPS)
            r.n[pl.ds(pl.multiple_of(base + i * RC, RC), RC), :] = c * scale
            if keep:
                r.scale[pl.ds(pl.multiple_of(i * RC, RC), RC), :] = jnp.broadcast_to(scale, (RC, 128))
            return 0

        lax.fori_loop(0, T // RC, one, 0)

    norm_rows(r.tokens, x * T, True)

    relay("v", "z", "y", "x")
    relay("q", "z", "y", "x", 0)
    relay("v", "y", "c", "xz")
    relay("q", "z", "y", "x", 1)
    arrived("v")

    widths = [D // N, D // N, D // N, D // N, 3 * D // N, D // N, FF // N, D // N]

    def column(v, n):
        j = iota((1, n), 1)
        if v == 4:
            head_at = x * HC + 2 * (j // 384) + (j % 128) // HD
            return head_at * (3 * HD) + ((j % 384) // 128) * HD + j % HD
        if v == 6:
            return (j // 64) * 128 + x * 64 + j % 64
        return j

    def lengths(v):
        return {4: 3 * HW, 6: FH}.get(v, D)

    vec2 = r.wv.reshape(N * 8, 128)

    def expand(v):
        n = lengths(v)
        j = column(v, n)
        pick = (iota((128, n), 0) == j % widths[v]).astype(F32).astype(BF16)
        rows_v = vec2[pl.ds(v, N, stride=8), :].astype(BF16)
        spread = mm(rows_v, pick)
        r.vrow[v : v + 1, 0:n] = jnp.sum(
            jnp.where(iota((N, n), 0) == j // widths[v], spread, 0.0), axis=0, keepdims=True
        )

    for v in range(8):
        expand(v)

    def row(v, n=D, off=0):
        return r.vrow[v : v + 1, off : off + n]

    def affine_attn(base):
        def one(i, _):
            at = pl.ds(pl.multiple_of(base + i * RC, RC), RC)
            r.ha[at, :] = (r.n[at, :] * row(0) + row(1)).astype(BF16)
            return 0

        lax.fori_loop(0, T // RC, one, 0)

    def affine_mlp(base):
        def one(i, _):
            at = pl.ds(pl.multiple_of(base + i * RC, RC), RC)
            r.hm[at, :] = (r.n[at, :] * row(2) + row(3)).astype(BF16)
            return 0

        lax.fori_loop(0, T // RC, one, 0)

    affine_attn(x * T)
    relay("d", "z", "y", "x", 0)
    relay("q", "y", "c", "xz", 0)
    affine_mlp(x * T)
    relay("q", "y", "c", "xz", 1)
    relay("d", "z", "y", "x", 1)

    wait("tok")
    norm_rows(r.tok2, xo * T, False)
    affine_attn(xo * T)
    affine_mlp(xo * T)
    relay("i", "z", "y", "x", 0)
    relay("d", "y", "c", "xz", 0)

    wq = r.wq.reshape(D, 3 * HW)

    def qkv(b):
        def one(i, _):
            at = pl.ds(pl.multiple_of(i * QB, QB), QB)
            u = mm(r.ha[at, :], wq[:, chunk("q", b)]) + row(4, 384, b * 384)
            for jj, name in enumerate("qkv"):
                w = u[:, jj * 128 : (jj + 1) * 128]
                if jj < 2:
                    w = turn(w, at, 1.0)
                if jj == 0:
                    w = w * HD**-0.5
                w = w.astype(BF16)
                held[name][at, b * 128 : (b + 1) * 128] = w
                if jj >= 1:
                    held[name + "t"][b * 128 : (b + 1) * 128, at] = w.T
            return 0

        arrived("q", b)
        lax.fori_loop(0, S // QB, one, 0)

    qkv(0)
    relay("i", "z", "y", "x", 1)
    relay("d", "y", "c", "xz", 1)
    qkv(1)
    arrived("d", 0)
    arrived("d", 1)
    wd = r.wd.reshape(D, D)
    mine = pl.ds(pl.multiple_of(x * HW, HW), HW)
    r.do2[rows_mine, :] = mm(r.cot[...], wd[mine, :], NT).astype(BF16)

    r.dk[...] = jnp.zeros_like(r.dk)
    r.dv[...] = jnp.zeros_like(r.dv)
    causal = iota((QB, QB), 0) <= iota((QB, QB), 1)

    def head(blocks, h, _):
        lanes = pl.ds(pl.multiple_of((h // 2) * 128, 128), 128)
        ours = (lane // HD) == h % 2
        head_rows = pl.ds(pl.multiple_of(h * HD, HD), HD)
        for i in blocks:
            here = slice(i * QB, (i + 1) * QB)
            qm = jnp.where(ours, r.q[here, lanes], jnp.zeros((), BF16))
            dom = jnp.where(ours, r.do2[here, lanes], jnp.zeros((), BF16))
            top = None
            for j in range(i + 1):
                st = mm(r.k[j * QB : (j + 1) * QB, lanes], qm, NT)
                if j == i:
                    st = jnp.where(causal, st, NEG)
                r.st[j] = st
                part = jnp.max(st, axis=0, keepdims=True)
                top = part if top is None else jnp.maximum(top, part)
            total = du = None
            for j in range(i + 1):
                e = jnp.exp(r.st[j] - top)
                r.st[j] = e
                dp = mm(r.v[j * QB : (j + 1) * QB, lanes], dom, NT)
                r.dp[j] = dp
                part, both = (jnp.sum(w, axis=0, keepdims=True) for w in (e, e * dp))
                total = part if total is None else total + part
                du = both if du is None else du + both
            scale = 1.0 / total
            delta = du * scale
            for j in range(i + 1):
                p = r.st[j] * scale
                r.pb[j * QB : (j + 1) * QB, :] = p.astype(BF16)
                ds = p * (r.dp[j] - delta)
                r.ds[j * QB : (j + 1) * QB, :] = ds.astype(BF16)
            n = (i + 1) * QB
            pb, ds = r.pb[0:n, :], r.ds[0:n, :]
            r.ot[head_rows, here] = mm(r.vt[head_rows, 0:n], pb).astype(BF16)
            r.dqt[head_rows, here] = mm(r.kt[head_rows, 0:n], ds)
            r.dk[0:n, lanes] += mm(ds, qm)
            r.dv[0:n, lanes] += mm(pb, dom)
        return 0

    per_x = T // QB

    def attend(theirs, first, last):
        for k in range(X):
            at = (1 - k if theirs else k) * per_x
            run = functools.partial(head, range(at, at + per_x))

            @pl.when(x == k)
            def _():
                lax.fori_loop(first, last, run, 0)

    attend(False, 0, 2)
    relay("i", "y", "c", "xz", 0)
    relay("o", "z", "y", "", 0)
    relay("o", "z", "y", "", 1)
    attend(False, 2, 4)
    relay("i", "y", "c", "xz", 1)
    r.hmt[...] = r.hm[...].T

    wi = r.wi.reshape(D, FH)
    wo = r.wo.reshape(FH, D)
    gi = r.gi.reshape(D, FH)
    go = r.go.reshape(FH, D)
    FB = 256

    def ff_cols(b):
        return pl.ds(pl.multiple_of(b * FB, FB), FB)

    def ff_forward(b, _):
        cols = ff_cols(b)
        f = mm(r.hm[...], wi[:, cols]) + r.vrow[6:7, cols]
        phi = 0.5 + 0.5 * lax.erf(f * (0.5**0.5))
        r.act[:, cols] = (f * phi).astype(BF16)
        r.slope[:, cols] = phi + f * (jnp.exp(-0.5 * f * f) * (0.5 / np.pi) ** 0.5)
        return 0

    arrived("i", 0)
    lax.fori_loop(0, FH // FB // 2, ff_forward, 0)
    arrived("i", 1)
    lax.fori_loop(FH // FB // 2, FH // FB, ff_forward, 0)

    wait("cot")
    r.cots[rows_mine, :] = r.cot[...]
    r.do2[rows_theirs, :] = mm(r.cots[rows_theirs, :], wd[mine, :], NT).astype(BF16)

    def out_grad(b, _):
        at = ff_cols(b)
        go[at, :] = mm(r.act[:, at], r.cots[...], TN).astype(BF16)
        return 0

    relay("o", "y", "c", "z", 0)
    lax.fori_loop(0, FH // FB, out_grad, 0)
    scatter("o", "c", "", 0)
    scatter("o", "c", "", 1)
    relay("o", "y", "c", "z", 1)

    def send_o(b):
        own_rows = slice(b * 128, (b + 1) * 128)
        to = pl.ds(pl.multiple_of(x * HW + b * 128, 128), 128)
        push(("o", b), r.ot.at[own_rows, rows_theirs], r.of.at[to, :], at_x)
        r.of[to, :] = r.ot[own_rows, rows_mine]
        r.gd.reshape(D, D)[to, :] = mm(r.ot[own_rows, :], r.cots[...]).astype(BF16)
        push(("gc", b), r.gd.at[x * (Z // X) + b, :, 1 - me["c"]], r.dc.at[b], others("c")[0])

    def gd_y(b):
        wait(("gc", b))
        at = (x * (Z // X) + b, slice(None), me["c"])
        r.gd[at] = (r.gd[at].astype(F32) + r.dc[b].astype(F32)).astype(BF16)
        push(("gy", b), r.gd.at[at[0], 1 - me["y"], me["c"]], r.dy.at[b], others("y")[0])

    def gd_x(b):
        wait(("gy", b))
        at = (x * (Z // X) + b, me["y"], me["c"])
        r.gd[at] = (r.gd[at].astype(F32) + r.dy[b].astype(F32)).astype(BF16)
        part = r.gd.at[at + (xo,)]
        push(("gx", b), part, part, at_x)

    r.vg[...] = jnp.zeros_like(r.vg)
    gq = r.gq.reshape(D, 3 * HW)

    def qkv_back(b):
        def one(i, _):
            at = pl.ds(pl.multiple_of(i * QB, QB), QB)
            cols = slice(b * 128, (b + 1) * 128)
            dq = r.dqt[cols, at].T
            out = (
                turn(dq, at, -1.0) * HD**-0.5,
                turn(r.dk[at, cols], at, -1.0),
                r.dv[at, cols],
            )
            for jj in range(3):
                w = out[jj].astype(BF16)
                to = slice(b * 384 + jj * 128, b * 384 + (jj + 1) * 128)
                r.dqkv[at, to] = w
                r.vg[4:5, to] += jnp.sum(w.astype(F32), axis=0, keepdims=True)
            return 0

        lax.fori_loop(0, S // QB, one, 0)
        cols = chunk("q", b)
        for k in range(D // QB):
            gq[k * QB : (k + 1) * QB, cols] = mm(
                r.ha[:, k * QB : (k + 1) * QB], r.dqkv[:, cols], TN
            ).astype(BF16)
        scatter("q", "c", "", b)

    attend(True, 0, 1)
    arrived("o", 0)
    arrived("o", 1)
    r.mos[...] = mm(r.act[rows_theirs, :], wo[...]).astype(BF16)
    push("mo", r.mos, r.mor, at_x)
    attend(True, 1, 2)
    step("o", "c", "y", "", 0)
    step("o", "c", "y", "", 1)
    send_o(0)
    qkv_back(0)
    attend(True, 2, 4)
    send_o(1)
    gd_y(0)
    step("q", "c", "y", "", 0)
    qkv_back(1)
    gd_x(0)
    gd_y(1)

    def ff_backward(b, _):
        cols = ff_cols(b)
        df = (mm(r.cots[...], wo[cols, :], NT) * r.slope[:, cols]).astype(BF16)
        r.vg[6:7, cols] = jnp.sum(df.astype(F32), axis=0, keepdims=True)
        r.df[:, cols] = df
        gi[:, cols] = mm(r.hmt[...], df).astype(BF16)
        return 0

    lax.fori_loop(0, FH // FB // 2, ff_backward, 0)
    scatter("i", "c", "", 0)
    step("q", "c", "y", "", 1)
    gd_x(1)
    lax.fori_loop(FH // FB // 2, FH // FB, ff_backward, 0)
    scatter("i", "c", "", 1)
    step("i", "c", "y", "", 0)

    def input_grads(base, mine_too):
        def one(i, _):
            at = pl.ds(pl.multiple_of(base + i * QB, QB), QB)
            to = pl.ds(pl.multiple_of(i * QB, QB), QB)
            n = r.n[at, :]
            dm = mm(r.df[at, :], wi[...], NT)
            r.vg[2:3, 0:D] += jnp.sum(dm * n, axis=0, keepdims=True)
            r.vg[3:4, 0:D] += jnp.sum(dm, axis=0, keepdims=True)
            dh = mm(r.dqkv[at, :], wq[...], NT)
            r.vg[0:1, 0:D] += jnp.sum(dh * n, axis=0, keepdims=True)
            r.vg[1:2, 0:D] += jnp.sum(dh, axis=0, keepdims=True)
            u = dh * row(0) + dm * row(2)
            if mine_too:
                r.u[to, :] = u
            else:
                r.us[to, :] = u.astype(BF16)
            return 0

        lax.fori_loop(0, T // QB, one, 0)

    input_grads(xo * T, False)
    for k in range(T // QB):
        part = slice(k * QB, (k + 1) * QB)
        push(("u", k), r.us.at[part, :], r.ur.at[part, :], at_x)
    step("i", "c", "y", "", 1)
    step("o", "y", "z", "c", 0)
    step("o", "y", "z", "c", 1)
    step("q", "y", "z", "c", 0)
    step("q", "y", "z", "c", 1)
    input_grads(x * T, True)

    g_sum = jnp.sum(r.cot[...].astype(F32), axis=0, keepdims=True)
    r.vg[5:6, 0:D] = g_sum
    r.vg[7:8, 0:D] = g_sum
    gv2 = r.gv.reshape(N * 8, 128)

    def collapse(v):
        n = lengths(v)
        j = column(v, n)
        pick = (iota((128, n), 0) == j % widths[v]).astype(F32).astype(BF16)
        left = jnp.where(iota((N, n), 0) == j // widths[v], r.vg[v : v + 1, 0:n], 0.0)
        acc = None
        for _ in range(3):
            low = left.astype(BF16)
            part = mm(low, pick, NT)
            acc = part if acc is None else acc + part
            left = left - low.astype(F32)
        gv2[pl.ds(v, N, stride=8), :] = acc

    for v in range(8):
        collapse(v)
    scatter("v", "c", "")
    wait(("gx", 0))
    wait(("gx", 1))
    scatter("d", "z", "cyx")
    step("i", "y", "z", "c", 0)
    r.mo[...] = mm(r.act[rows_mine, :], wo[...])
    step("i", "y", "z", "c", 1)

    def flat(out, width, k=None, part=D):
        per = width // 128
        n = out.shape[0] // per
        lo = 0 if k is None else k * (part // 128)

        def put(acc):
            for j in range(acc.shape[1] // 128):
                out[pl.ds(lo + j, n, stride=per), :] = acc[:, j * 128 : (j + 1) * 128]

        return put

    step("v", "c", "y")
    add_parts("o", "z", "cy", 0, flat(r.oo, D, 0, CH["o"]))
    add_parts("o", "z", "cy", 1, flat(r.oo, D, 1, CH["o"]))
    at_me = (me["z"], me["y"], me["c"])
    step("v", "y", "z", "c")
    add_parts("q", "z", "cy", 0)
    add_parts("q", "z", "cy", 1)
    push("sq", r.gq.at[at_me + (xo,)], r.xq, at_x)

    wait(("o", 0))
    wait(("o", 1))
    wait("mo")
    r.out[...] = (
        r.tokens[...].astype(F32)
        + mm(r.of[...], wd[...], TN)
        + row(5)
        + (r.mo[...] + r.mor[...].astype(F32) + row(7))
    ).astype(BF16)
    step("v", "z", "x", "cy")
    add_parts("d", "z", "cyx", None, flat(r.od, D))
    add_parts("i", "z", "cy", 0)
    add_parts("i", "z", "cy", 1)
    push("si", r.gi.at[at_me + (xo,)], r.xi, at_x)


    def final_rows(i, _):
        at = pl.ds(pl.multiple_of(i * RC, RC), RC)
        far = pl.ds(pl.multiple_of(x * T + i * RC, RC), RC)
        u = r.u[at, :] + r.ur[at, :].astype(F32)
        n = r.n[far, :]
        back = u - jnp.mean(u, axis=-1, keepdims=True) - n * jnp.mean(u * n, axis=-1, keepdims=True)
        r.gtok[at, :] = (r.cot[at, :].astype(F32) + back * r.scale[at, 0:1]).astype(BF16)
        return 0

    for k in range(T // QB):
        wait(("u", k))
        lax.fori_loop(k * (QB // RC), (k + 1) * (QB // RC), final_rows, 0)

    def join(mine_ref, got, out, width, place):
        per = width // 128
        n = out.shape[0] // per
        here = mine_ref[at_me + (x,)].astype(F32)
        there = got[...].astype(F32)
        halves = (jnp.where(x == 0, here, there), jnp.where(x == 0, there, here))

        def piece(b, to_high):
            half, m, odd = place(b)
            v = halves[half][:, m * 128 : (m + 1) * 128]
            return pltpu.roll(v, 64, 1) if odd != to_high else v

        for j in range(per):
            both = jnp.where(lane < 64, piece(2 * j, False), piece(2 * j + 1, True))
            out[pl.ds(j, n, stride=per), :] = both

    def place_q(b):
        h, jj = b // 3, b % 3
        return h // HC, (h % HC) // 2 * 3 + jj, h % 2 == 1

    def place_i(b):
        return b % 2, b // 4, (b // 2) % 2 == 1

    wait("sq")
    join(r.gq, r.xq, r.oq, 3 * D, place_q)
    wait("si")
    join(r.gi, r.xi, r.oi, FF, place_i)

    def put_vec(acc):
        r.ov[...] = acc

    add_parts("v", "x", "cyz", None, put_vec)


def rope_table(length):
    lanes = np.arange(128) % HD
    rot = HD // 4
    inverse = np.where(lanes < rot, 1.0 / ROPE_BASE ** (2.0 * (lanes % (rot // 2)) / rot), 0.0)
    high = 32.0 * np.arange(length // 32)[:, None] * inverse
    low = np.arange(32)[:, None] * inverse
    return np.stack([np.cos(high), np.sin(high), np.cos(low), np.sin(low)]).astype(np.float32)


def hand_over(*refs):
    for src, dst in zip(refs[:6], refs[7:13]):
        dst[...] = src[...]
    for v, dst in enumerate(refs[13:]):
        dst[...] = refs[6][v : v + 1, 0 : dst.shape[1]]


def layer(sizes, tokens, cotangent, *params):
    Z, Y, C, X = (sizes[a] for a in AX)
    N = Z * Y * C * X
    T = tokens.shape[1]
    S = T * X
    HW = HEADS // X * HD
    vectors = [params[i] for i in (0, 1, 2, 3, 5, 7, 9, 11)]
    weights = [params[i] for i in (4, 6, 8, 10)]
    flats = [w.reshape(-1, 128) for w in weights]
    full = dict(z=Z, y=Y, c=C, x=X)

    FH = FF // X

    def parts(name, axis, done, slab, dtype):
        free = [full[a] for a in AX if a not in done and a != axis and (a != "x" or name != "o")]
        return pltpu.VMEM((full[axis] - 1, *free, *slab), dtype)

    slabs = {
        "q": (D // N, 3 * HW),
        "d": (D // N, D),
        "i": (D // N, FH),
        "o": (FF // N, D),
        "v": (8, 128),
    }
    orders = {"q": "cyz", "d": "z", "i": "cyz", "o": "cyz", "v": "cyzx"}
    keep = types.SimpleNamespace()
    scratch = vars(keep)
    for k, slab in slabs.items():
        kind = F32 if k == "v" else BF16
        devs = (Z, Y, C) if k == "o" else (Z, Y, C, X)
        scratch["w" + k] = pltpu.VMEM((*devs, *slab), kind)
        scratch["g" + k] = pltpu.VMEM((*devs, *slab), kind)
        for n, axis in enumerate(orders[k]):
            done = "cyx" if k == "d" else orders[k][:n]
            scratch["r" + k + axis] = parts(k, axis, done, slab, kind)
    keep.dc = pltpu.VMEM((X, Y, X, *slabs["d"]), BF16)
    keep.dy = pltpu.VMEM((X, X, *slabs["d"]), BF16)
    keep.xq = pltpu.VMEM(slabs["q"], BF16)
    keep.xi = pltpu.VMEM(slabs["i"], BF16)
    keep.sq = pltpu.VMEM((X, *slabs["q"]), BF16)
    keep.si = pltpu.VMEM((X, *slabs["i"]), BF16)
    keep.tmp = pltpu.VMEM((max(f.shape[0] for f in flats), 128), F32)
    keep.cos = keep.sinl = keep.sinh = pltpu.VMEM((S, 128), F32)
    keep.tok2 = pltpu.VMEM((T, D), BF16)
    keep.cots = pltpu.VMEM((S, D), BF16)
    keep.n = pltpu.VMEM((S, D), F32)
    keep.scale = pltpu.VMEM((T, 128), F32)
    keep.vrow = pltpu.VMEM((8, FH), F32)
    keep.vg = pltpu.VMEM((8, FH), F32)
    keep.ha = keep.hm = pltpu.VMEM((S, D), BF16)
    keep.hmt = pltpu.VMEM((D, S), BF16)
    keep.q = keep.k = keep.v = keep.do2 = pltpu.VMEM((S, HW), BF16)
    keep.kt = keep.vt = keep.ot = pltpu.VMEM((HW, S), BF16)
    keep.dqt = pltpu.VMEM((HW, S), F32)
    keep.dk = pltpu.VMEM((S, HW), F32)
    keep.dv = pltpu.VMEM((S, HW), F32)
    keep.st = pltpu.VMEM((S // QB, QB, QB), F32)
    keep.dp = pltpu.VMEM((S // QB, QB, QB), F32)
    keep.pb = pltpu.VMEM((S, QB), BF16)
    keep.ds = pltpu.VMEM((S, QB), BF16)
    keep.dqkv = pltpu.VMEM((S, 3 * HW), BF16)
    keep.of = pltpu.VMEM((D, T), BF16)
    keep.act = keep.df = pltpu.VMEM((S, FH), BF16)
    keep.slope = pltpu.VMEM((S, FH), F32)
    keep.u = keep.mo = pltpu.VMEM((T, D), F32)
    keep.us = keep.ur = keep.mos = keep.mor = pltpu.VMEM((T, D), BF16)
    copies = 128
    keep.send = pltpu.SemaphoreType.DMA((copies,))
    keep.recv = pltpu.SemaphoreType.DMA((copies,))
    ins = "tokens cot fq fd".split() + "fi fo rope".split() + ["v%d" % v for v in range(8)]
    outs = dict(
        out=jax.ShapeDtypeStruct((T, D), BF16),
        gtok=jax.ShapeDtypeStruct((T, D), BF16),
        oq=jax.ShapeDtypeStruct(flats[0].shape, F32),
        od=jax.ShapeDtypeStruct(flats[1].shape, F32),
        oi=jax.ShapeDtypeStruct(flats[2].shape, F32),
        oo=jax.ShapeDtypeStruct(flats[3].shape, F32),
        ov=jax.ShapeDtypeStruct((8, 128), F32),
    )
    vmem = pl.BlockSpec(memory_space=pltpu.VMEM)
    shown = tokens.reshape(T, D), cotangent.reshape(T, D), *flats, jnp.asarray(rope_table(S))
    shown += tuple(v.reshape(1, -1) for v in vectors)
    for name, a in zip(ins, shown):
        scratch[name] = pltpu.VMEM(a.shape, a.dtype)
    keep.load = pltpu.SemaphoreType.DMA((len(ins),))
    names = ["h" + n for n in ins] + list(outs) + list(scratch)
    out, gtok, gq, gd, gi, go, gv = pl.pallas_call(
        functools.partial(fused, sizes, names),
        out_shape=list(outs.values()),
        in_specs=[pl.BlockSpec(memory_space=pl.ANY)] * len(ins),
        out_specs=[vmem] * len(outs),
        scratch_shapes=list(scratch.values()),
        compiler_params=pltpu.CompilerParams(
            collective_id=0, has_side_effects=True, vmem_limit_bytes=67043328
        ),
        name="layer",
    )(
        *shown
    )
    shapes = [jax.ShapeDtypeStruct(a.shape, a.dtype) for a in (out, gtok, gq, gd, gi, go)]
    shapes += [jax.ShapeDtypeStruct((1, p.shape[0]), F32) for p in vectors]
    out, gtok, gq, gd, gi, go, *v = pl.pallas_call(
        hand_over,
        out_shape=shapes,
        in_specs=[vmem] * 7,
        out_specs=[vmem] * len(shapes),
        name="results",
    )(out, gtok, gq, gd, gi, go, gv)
    v = [a.reshape(-1) for a in v]
    return (
        out.reshape(tokens.shape),
        gtok.reshape(tokens.shape),
        v[0],
        v[1],
        v[2],
        v[3],
        gq.reshape(-1),
        v[4],
        gd.reshape(-1),
        v[5],
        gi.reshape(-1),
        v[6],
        go.reshape(-1),
        v[7],
    )


def solution(mesh):
    n_seq, n_ctx = mesh.shape["seq"], mesh.shape["ctx"]
    if n_ctx != 2 or n_seq != 16 or (D // (n_seq * n_ctx)) % 16:
        return general(mesh)
    sizes = {"z": n_seq // 4, "y": 2, "c": 2, "x": n_ctx}
    flat = P(("seq", "ctx"))
    rows = P("seq", "ctx", None)
    return jax.shard_map(
        functools.partial(layer, sizes),
        mesh=mesh,
        in_specs=(rows, rows) + (flat,) * 12,
        out_specs=(rows, rows) + (flat,) * 12,
        check_vma=False,
    )
```

```python
import functools
import types

import jax
import jax.numpy as jnp
import numpy as np
from jax import lax
from jax.experimental import pallas as pl
from jax.experimental.pallas import tpu as pltpu
from jax.sharding import PartitionSpec as P

D = 512
HEADS = 8
FF = 2048


EPS = 1e-05
BOTH = ("seq", "ctx")
ROPE_BASE = 10000.0
NEG = -1e30


def layer_normalize(values, gain, bias):
    mean = jnp.mean(values, axis=-1, keepdims=True)
    centered = values - mean
    var = jnp.mean(centered * centered, axis=-1, keepdims=True)
    return centered * lax.rsqrt(var + EPS) * gain + bias


def rotate(values, cosine, sine):
    width = cosine.shape[-1]
    half = width // 2
    part = values[..., :width]
    turned = jnp.concatenate([-part[..., half:], part[..., :half]], axis=-1)
    return jnp.concatenate([part * cosine + turned * sine, values[..., width:]], axis=-1)


def gelu_exact(values):
    return jax.nn.gelu(values, approximate=False)


def matrices(mix_flat, proj_flat, expand_flat, reduce_flat):
    return (
        mix_flat.reshape(D, 3 * D),
        proj_flat.reshape(D, D),
        expand_flat.reshape(D, FF),
        reduce_flat.reshape(FF, D),
    )


def body(
    tokens,
    cotangent,
    attn_norm_gain,
    attn_norm_bias,
    mlp_norm_gain,
    mlp_norm_bias,
    qkv_weight,
    qkv_bias,
    dense_weight,
    dense_bias,
    fc_in_weight,
    fc_in_bias,
    fc_out_weight,
    fc_out_bias,
):
    (
        gain_attn,
        attention_shift,
        gain_mlp,
        shift_mlp,
        mix_flat,
        mix_bias,
        proj_flat,
        proj_bias,
        expand_flat,
        expand_bias,
        reduce_flat,
        reduce_bias,
    ) = (
        lax.all_gather(attn_norm_gain, BOTH, axis=0, tiled=True),
        lax.all_gather(attn_norm_bias, BOTH, axis=0, tiled=True),
        lax.all_gather(mlp_norm_gain, BOTH, axis=0, tiled=True),
        lax.all_gather(mlp_norm_bias, BOTH, axis=0, tiled=True),
        lax.all_gather(qkv_weight, BOTH, axis=0, tiled=True),
        lax.all_gather(qkv_bias, BOTH, axis=0, tiled=True),
        lax.all_gather(dense_weight, BOTH, axis=0, tiled=True),
        lax.all_gather(dense_bias, BOTH, axis=0, tiled=True),
        lax.all_gather(fc_in_weight, BOTH, axis=0, tiled=True),
        lax.all_gather(fc_in_bias, BOTH, axis=0, tiled=True),
        lax.all_gather(fc_out_weight, BOTH, axis=0, tiled=True),
        lax.all_gather(fc_out_bias, BOTH, axis=0, tiled=True),
    )
    mix_weight, proj_weight, expand_weight, reduce_weight = matrices(
        mix_flat, proj_flat, expand_flat, reduce_flat
    )
    shape = tokens.shape
    group = shape[1]
    width = shape[2]
    heads = HEADS
    head_dim = width // heads
    rows = tokens.reshape(group, width).astype(jnp.float32)
    attn_in, attn_norm_back = jax.vjp(
        layer_normalize, rows, gain_attn.astype(jnp.float32), attention_shift.astype(jnp.float32)
    )
    mlp_in, mlp_norm_back = jax.vjp(
        layer_normalize, rows, gain_mlp.astype(jnp.float32), shift_mlp.astype(jnp.float32)
    )
    attn_low = attn_in.astype(jnp.bfloat16)
    mlp_low = mlp_in.astype(jnp.bfloat16)
    mixed = jnp.dot(attn_low, mix_weight, preferred_element_type=jnp.float32) + mix_bias.astype(
        jnp.float32
    )
    mixed = mixed.reshape(group, heads, 3, head_dim)
    place = lax.axis_index("ctx")
    blocks_total = lax.axis_size("ctx")
    local_pos = jnp.arange(group, dtype=jnp.int32)
    query_pos = place * group + local_pos
    rot_dims = head_dim // 4
    inverse = 1.0 / ROPE_BASE ** (
        jnp.arange(0, rot_dims, 2, dtype=jnp.int32).astype(jnp.float32) / rot_dims
    )
    angles = query_pos.astype(jnp.float32)[:, None] * inverse[None, :]
    angles = jnp.concatenate([angles, angles], axis=-1)
    cosine = jnp.cos(angles)[:, None, :]
    sine = jnp.sin(angles)[:, None, :]
    scale = head_dim ** (-0.5)

    def turn(query_unrotated, key_raw):
        return (rotate(query_unrotated, cosine, sine) * scale, rotate(key_raw, cosine, sine))

    (query_f, key_f), turn_back = jax.vjp(turn, mixed[:, :, 0], mixed[:, :, 1])
    query = query_f.astype(jnp.bfloat16)
    key_own = key_f.astype(jnp.bfloat16).reshape(group, width)
    value_own = mixed[:, :, 2].astype(jnp.bfloat16).reshape(group, width)
    all_keys, all_values = (
        lax.all_gather(key_own, "ctx", axis=0, tiled=True),
        lax.all_gather(value_own, "ctx", axis=0, tiled=True),
    )
    count = place + 1

    def block(index):
        keys = lax.dynamic_slice_in_dim(all_keys, index * group, group, 0).reshape(
            group, heads, head_dim
        )
        values = lax.dynamic_slice_in_dim(all_values, index * group, group, 0).reshape(
            group, heads, head_dim
        )
        scores = jnp.einsum("qhd,khd->hqk", query, keys, preferred_element_type=jnp.float32)
        allowed = (index * group + local_pos)[None, :] <= query_pos[:, None]
        return (keys, values, scores, allowed[None])

    def max_step(index, carry):
        top, total = carry
        _, _, scores, allowed = block(index)
        new_top = jnp.maximum(top, jnp.max(jnp.where(allowed, scores, NEG), axis=-1))
        terms = jnp.where(allowed, jnp.exp(scores - new_top[:, :, None]), 0.0)
        return (new_top, total * jnp.exp(top - new_top) + jnp.sum(terms, axis=-1))

    start = (jnp.full((heads, group), NEG, jnp.float32), jnp.zeros((heads, group), jnp.float32))
    top, total = lax.fori_loop(0, count, max_step, start)
    log_total = top + jnp.log(total)

    def probs_of(scores, allowed):
        return jnp.where(allowed, jnp.exp(scores - log_total[:, :, None]), 0.0)

    def out_step(index, acc):
        _, values, scores, allowed = block(index)
        probs = probs_of(scores, allowed).astype(jnp.bfloat16)
        return acc + jnp.einsum("hqk,khd->qhd", probs, values, preferred_element_type=jnp.float32)

    heads_out = lax.fori_loop(0, count, out_step, jnp.zeros((group, heads, head_dim), jnp.float32))
    attn_out = heads_out.reshape(group, width).astype(jnp.bfloat16)
    branch_attn = jnp.dot(
        attn_out, proj_weight, preferred_element_type=jnp.float32
    ) + proj_bias.astype(jnp.float32)
    expand = jnp.dot(
        mlp_low, expand_weight, preferred_element_type=jnp.float32
    ) + expand_bias.astype(jnp.float32)
    active_rows, active_back = jax.vjp(gelu_exact, expand)
    active_low = active_rows.astype(jnp.bfloat16)
    branch_mlp = jnp.dot(
        active_low, reduce_weight, preferred_element_type=jnp.float32
    ) + reduce_bias.astype(jnp.float32)
    layer_out = (rows + branch_attn + branch_mlp).astype(jnp.bfloat16).reshape(shape)
    back_mix, back_proj, back_expand, back_reduce = (
        lax.all_gather(qkv_weight, BOTH, axis=0, tiled=True),
        lax.all_gather(dense_weight, BOTH, axis=0, tiled=True),
        lax.all_gather(fc_in_weight, BOTH, axis=0, tiled=True),
        lax.all_gather(fc_out_weight, BOTH, axis=0, tiled=True),
    )
    back_mix, back_proj, back_expand, back_reduce = matrices(
        back_mix, back_proj, back_expand, back_reduce
    )
    grad_rows = cotangent.reshape(group, width)
    grad_float = grad_rows.astype(jnp.float32)
    grad_reduce = jnp.einsum("tf,td->fd", active_low, grad_rows, preferred_element_type=jnp.float32)
    grad_out_bias = jnp.sum(grad_float, axis=0)
    grad_proj = jnp.einsum("te,td->ed", attn_out, grad_rows, preferred_element_type=jnp.float32)
    grad_active = jnp.einsum(
        "td,fd->tf", grad_rows, back_reduce, preferred_element_type=jnp.float32
    )
    grad_expand = active_back(grad_active)[0].astype(jnp.bfloat16)
    grad_expand_w = jnp.einsum(
        "td,tf->df", mlp_low, grad_expand, preferred_element_type=jnp.float32
    )
    grad_expand_b = jnp.sum(grad_expand.astype(jnp.float32), axis=0)
    grad_mlp_in = jnp.einsum(
        "tf,df->td", grad_expand, back_expand, preferred_element_type=jnp.float32
    )
    grad_heads = jnp.einsum("td,ed->te", grad_rows, back_proj, preferred_element_type=jnp.float32)
    grad_heads = grad_heads.astype(jnp.bfloat16).reshape(group, heads, head_dim)

    def delta_step(index, acc):
        _, values, scores, allowed = block(index)
        probs = probs_of(scores, allowed)
        grad_probs = jnp.einsum(
            "qhd,khd->hqk", grad_heads, values, preferred_element_type=jnp.float32
        )
        return acc + jnp.sum(probs * grad_probs, axis=-1)

    delta = lax.fori_loop(0, count, delta_step, jnp.zeros((heads, group), jnp.float32))

    def query_step(index, grad_query):
        keys, values, scores, allowed = block(index)
        probs = probs_of(scores, allowed)
        grad_probs = jnp.einsum(
            "qhd,khd->hqk", grad_heads, values, preferred_element_type=jnp.float32
        )
        grad_scores = (probs * (grad_probs - delta[:, :, None])).astype(jnp.bfloat16)
        return grad_query + jnp.einsum(
            "hqk,khd->qhd", grad_scores, keys, preferred_element_type=jnp.float32
        )

    grad_query = lax.fori_loop(
        0, count, query_step, jnp.zeros((group, heads, head_dim), jnp.float32)
    )
    all_queries, all_grad_heads = (
        lax.all_gather(query.reshape(group, width), "ctx", axis=0, tiled=True),
        lax.all_gather(grad_heads.reshape(group, width), "ctx", axis=0, tiled=True),
    )
    gathered_log_sums, all_delta = (
        lax.all_gather(jnp.transpose(log_total), "ctx", axis=0, tiled=True),
        lax.all_gather(jnp.transpose(delta), "ctx", axis=0, tiled=True),
    )
    keys_mine = key_own.reshape(group, heads, head_dim)
    values_mine = value_own.reshape(group, heads, head_dim)

    def owner_step(index, carry):
        key_acc, value_accumulator = carry
        queries = lax.dynamic_slice_in_dim(all_queries, index * group, group, 0).reshape(
            group, heads, head_dim
        )
        outer_grads = lax.dynamic_slice_in_dim(all_grad_heads, index * group, group, 0).reshape(
            group, heads, head_dim
        )
        lse_rows = jnp.transpose(
            lax.dynamic_slice_in_dim(gathered_log_sums, index * group, group, 0)
        )
        delta_rows = jnp.transpose(lax.dynamic_slice_in_dim(all_delta, index * group, group, 0))
        scores = jnp.einsum("qhd,khd->hqk", queries, keys_mine, preferred_element_type=jnp.float32)
        allowed = (query_pos[None, :] <= (index * group + local_pos)[:, None])[None]
        probs = jnp.where(allowed, jnp.exp(scores - lse_rows[:, :, None]), 0.0)
        grad_probs = jnp.einsum(
            "qhd,khd->hqk", outer_grads, values_mine, preferred_element_type=jnp.float32
        )
        grad_scores = (probs * (grad_probs - delta_rows[:, :, None])).astype(jnp.bfloat16)
        key_acc = key_acc + jnp.einsum(
            "hqk,qhd->khd", grad_scores, queries, preferred_element_type=jnp.float32
        )
        value_accumulator = value_accumulator + jnp.einsum(
            "hqk,qhd->khd",
            probs.astype(jnp.bfloat16),
            outer_grads,
            preferred_element_type=jnp.float32,
        )
        return (key_acc, value_accumulator)

    empty_heads = jnp.zeros((group, heads, head_dim), jnp.float32)
    own_key_grad, own_value_grad = lax.fori_loop(
        place, blocks_total, owner_step, (empty_heads, empty_heads)
    )
    grad_query_raw, grad_key_raw = turn_back((grad_query, own_key_grad))
    grad_mixed = jnp.stack([grad_query_raw, grad_key_raw, own_value_grad], axis=2)
    grad_mixed = grad_mixed.reshape(group, 3 * width).astype(jnp.bfloat16)
    grad_mix_w = jnp.einsum("td,te->de", attn_low, grad_mixed, preferred_element_type=jnp.float32)
    grad_mix_b = jnp.sum(grad_mixed.astype(jnp.float32), axis=0)
    grad_attn_in = jnp.einsum("te,de->td", grad_mixed, back_mix, preferred_element_type=jnp.float32)
    input_attn, gain_attn_grad, shift_attn_grad = attn_norm_back(grad_attn_in)
    input_mlp, gain_mlp_grad, shift_mlp_grad = mlp_norm_back(grad_mlp_in)
    grad_tokens = (grad_float + input_attn + input_mlp).astype(jnp.bfloat16).reshape(shape)
    sums = (
        lax.psum_scatter(gain_attn_grad, BOTH, scatter_dimension=0, tiled=True),
        lax.psum_scatter(shift_attn_grad, BOTH, scatter_dimension=0, tiled=True),
        lax.psum_scatter(gain_mlp_grad, BOTH, scatter_dimension=0, tiled=True),
        lax.psum_scatter(shift_mlp_grad, BOTH, scatter_dimension=0, tiled=True),
        lax.psum_scatter(grad_mix_w.reshape(-1), BOTH, scatter_dimension=0, tiled=True),
        lax.psum_scatter(grad_mix_b, BOTH, scatter_dimension=0, tiled=True),
        lax.psum_scatter(grad_proj.reshape(-1), BOTH, scatter_dimension=0, tiled=True),
        lax.psum_scatter(grad_out_bias, BOTH, scatter_dimension=0, tiled=True),
        lax.psum_scatter(
            grad_expand_w.reshape(-1), BOTH, scatter_dimension=0, tiled=True
        ),
        lax.psum_scatter(grad_expand_b, BOTH, scatter_dimension=0, tiled=True),
        lax.psum_scatter(grad_reduce.reshape(-1), BOTH, scatter_dimension=0, tiled=True),
        lax.psum_scatter(grad_out_bias, BOTH, scatter_dimension=0, tiled=True),
    )
    return (
        layer_out,
        grad_tokens,
        sums[0],
        sums[1],
        sums[2],
        sums[3],
        sums[4],
        sums[5],
        sums[6],
        sums[7],
        sums[8],
        sums[9],
        sums[10],
        sums[11],
    )


def general(mesh):
    return jax.shard_map(
        body,
        mesh=mesh,
        in_specs=(
            P("seq", "ctx", None),
            P("seq", "ctx", None),
            P(BOTH),
            P(BOTH),
            P(BOTH),
            P(BOTH),
            P(BOTH),
            P(BOTH),
            P(BOTH),
            P(BOTH),
            P(BOTH),
            P(BOTH),
            P(BOTH),
            P(BOTH),
        ),
        out_specs=(
            P("seq", "ctx", None),
            P("seq", "ctx", None),
            P(BOTH),
            P(BOTH),
            P(BOTH),
            P(BOTH),
            P(BOTH),
            P(BOTH),
            P(BOTH),
            P(BOTH),
            P(BOTH),
            P(BOTH),
            P(BOTH),
            P(BOTH),
        ),
        check_vma=False,
    )


MESH = pl.DeviceIdType.MESH
F32, BF16 = jnp.float32, jnp.bfloat16
HD = D // HEADS
AX = "zycx"
NN = (((1,), (0,)), ((), ()))
NT = (((1,), (1,)), ((), ()))
TN = (((0,), (0,)), ((), ()))
QB = 256


def mm(a, b, dims=NN):
    return lax.dot_general(a, b, dims, preferred_element_type=F32)


def iota(shape, dim):
    return lax.broadcasted_iota(jnp.int32, shape, dim)


def fused(sizes, names, *refs):
    held = dict(zip(names, refs))
    r = types.SimpleNamespace(**held)
    X = sizes["x"]
    C = sizes["c"]
    Y = sizes["y"]
    Z = sizes["z"]
    N = Z * Y * C * X
    T = held["tokens"].shape[0]
    S = T * X
    HC = HEADS // X
    HW = HC * HD
    FH = FF // X
    CH = dict(q=384, i=FH // 2, o=D // 2, d=D // 2)
    s = lax.axis_index("seq")
    me = {"x": lax.axis_index("ctx"), "c": s % C, "y": (s // C) % Y, "z": s // (C * Y)}
    x = me["x"]
    xo = 1 - x

    def device(at):
        return ((at["z"] * Y + at["y"]) * C + at["c"], at["x"])

    def others(axis):
        n = sizes[axis]
        return [dict(me, **{axis: (me[axis] + d) % n}) for d in range(1, n)]

    flight = {}
    count = [0]

    def push(key, src, dst, at):
        k = count[0]
        count[0] += 1
        cp = pltpu.make_async_remote_copy(
            src_ref=src,
            dst_ref=dst,
            send_sem=r.send.at[k],
            recv_sem=r.recv.at[k],
            device_id=device(at),
            device_id_type=MESH,
        )
        cp.start()
        flight.setdefault(key, []).append(cp)

    def wait(key):
        for cp in flight.pop(key):
            cp.wait()

    def axes(name):
        return AX[: 3 if name == "o" else 4]

    def chunk(name, k):
        if k is None:
            return slice(None)
        w = CH[name]
        return slice(k * w, (k + 1) * w)

    def gather(name, axis, known, k=None):
        ref = held["w" + name]
        spot = tuple(slice(None) if a in known else me[a] for a in axes(name))
        part = ref.at[spot + (slice(None), chunk(name, k))]
        for at in others(axis):
            push(("w", name, axis, k), part, part, at)

    def relay(name, axis, nxt, known, k=None):
        wait(("w", name, axis, k))
        gather(name, nxt, known + axis, k)

    def arrived(name, k=None):
        wait(("w", name, "c", k))

    def scatter(name, axis, done, k=None):
        ref, got = held["g" + name], held["r" + name + axis]
        free = [a for a in axes(name) if a not in done and a != axis]
        cols = (slice(None), chunk(name, k))
        for n, at in enumerate(others(axis)):
            spot = tuple(slice(None) if a in free else at[a] for a in axes(name))
            to = (n,) + (slice(None),) * len(free)
            push(("g", name, axis, k), ref.at[spot + cols], got.at[to + cols], at)

    def add_parts(name, axis, done, k=None, finish=None):
        wait(("g", name, axis, k))
        ref, got = held["g" + name], held["r" + name + axis]
        free = [a for a in axes(name) if a not in done and a != axis]
        cols = (slice(None), chunk(name, k))
        total = 1
        for a in free:
            total *= sizes[a]

        def one(i, _):
            at, rest = dict(me), i
            for a in reversed(free):
                at[a] = rest % sizes[a]
                rest = rest // sizes[a]
            spot = tuple(at[a] for a in axes(name))
            inner = tuple(at[a] for a in free)
            acc = ref[spot + cols].astype(F32)
            for n in range(sizes[axis] - 1):
                acc = acc + got[(n,) + inner + cols].astype(F32)
            if finish is None:
                ref[spot + cols] = acc.astype(ref.dtype)
            else:
                finish(acc)
            return 0

        if total == 1:
            one(0, 0)
        else:
            lax.fori_loop(0, total, one, 0)

    def step(name, axis, nxt, done="", k=None):
        add_parts(name, axis, done, k)
        scatter(name, nxt, done + axis, k)

    barrier = pltpu.get_barrier_semaphore()
    greet = [at for a in AX for at in others(a)]
    for at in greet:
        pl.semaphore_signal(barrier, inc=1, device_id=device(at), device_id_type=MESH)
    loads = {}
    for k, name in enumerate(n for n in names if ("h" + n) in held):
        loads[name] = pltpu.make_async_copy(held["h" + name], held[name], r.load.at[k])
        loads[name].start()

    def loaded(*which):
        for name in which:
            loads[name].wait()

    loaded("fq", "fi", "fd", *["v%d" % v for v in range(8)])

    tmp = r.tmp
    lane = iota((1, 128), 1)

    def own(name):
        return held[name].at[me["z"], me["y"], me["c"], x]

    def block64(b, per, rows, to_high):
        v = tmp[pl.ds(b // 2, rows, stride=per), :]
        return pltpu.roll(v, 64, 1) if (b % 2 == 1) != to_high else v

    def split(src, dst, width, table):
        n = held[src].shape[0]
        per = width // 128
        tmp[0:n, :] = held[src][...].astype(F32)
        for half in range(X):
            for m in range(per // X):
                low, high = table(half, m)
                low = block64(low, per, n // per, False)
                high = block64(high, per, n // per, True)
                dst[half, :, m * 128 : (m + 1) * 128] = jnp.where(lane < 64, low, high).astype(BF16)

    def table_q(half, m):
        h0 = half * HC + 2 * (m // 3)
        return 3 * h0 + m % 3, 3 * (h0 + 1) + m % 3

    def table_i(half, m):
        return 4 * m + half, 4 * m + 2 + half

    def reshard(src, dst, width):
        n = held[src].shape[0]
        k = width // 128
        tmp[0:n, :] = held[src][...].astype(F32)
        for j in range(k):
            dst[:, j * 128 : (j + 1) * 128] = tmp[pl.ds(j, n // k, stride=k), :].astype(BF16)

    split("fq", r.sq, 3 * D, table_q)
    split("fi", r.si, FF, table_i)
    reshard("fd", own("wd"), D)
    vecs = own("wv")
    vecs[...] = jnp.zeros_like(vecs)
    for v in range(8):
        vin = held["v%d" % v]
        vecs[v : v + 1, 0 : vin.shape[1]] = vin[...].astype(F32)
    own("wq")[...] = r.sq[x]
    own("wi")[...] = r.si[x]

    loaded("tokens", "cot", "fo", "rope")
    pl.semaphore_wait(barrier, len(greet))

    rows_mine = pl.ds(pl.multiple_of(x * T, T), T)
    rows_theirs = pl.ds(pl.multiple_of(xo * T, T), T)
    at_x = others("x")[0]
    gather("v", "x", "")
    push("sq", r.sq.at[xo], own("wq"), at_x)
    push("si", r.si.at[xo], own("wi"), at_x)
    gather("d", "x", "")
    push("tok", r.tokens, r.tok2, at_x)
    push("cot", r.cot, r.cots.at[rows_mine, :], at_x)
    reshard("fo", r.wo.at[me["z"], me["y"], me["c"]], D)

    rope = r.rope
    mod = lane % HD

    def rope_rows(i, _):
        ch, sh = rope[0, pl.ds(i, 1), :], rope[1, pl.ds(i, 1), :]
        cl, sl = rope[2], rope[3]
        sine = sh * cl + ch * sl
        at = pl.ds(pl.multiple_of(i * 32, 32), 32)
        r.cos[at, :] = ch * cl - sh * sl
        r.sinl[at, :] = jnp.where(mod < 8, -sine, 0.0)
        r.sinh[at, :] = jnp.where(mod < 8, 0.0, sine)
        return 0

    def turn(u, at, sign):
        return (
            u * r.cos[at, :]
            + sign * (pltpu.roll(u, 120, 1) * r.sinl[at, :] + pltpu.roll(u, 8, 1) * r.sinh[at, :])
        )

    relay("v", "x", "z", "")
    wait("sq")
    gather("q", "z", "x", 0)
    gather("q", "z", "x", 1)
    wait(("w", "d", "x", None))
    gather("d", "z", "x", 0)
    gather("d", "z", "x", 1)
    wait("si")
    gather("i", "z", "x", 0)
    gather("i", "z", "x", 1)
    gather("o", "z", "", 0)
    gather("o", "z", "", 1)
    lax.fori_loop(0, S // 32, rope_rows, 0)

    RC = 128

    def norm_rows(src, base, keep):
        def one(i, _):
            v = src[pl.ds(pl.multiple_of(i * RC, RC), RC), :].astype(F32)
            c = v - jnp.mean(v, axis=-1, keepdims=True)
            scale = lax.rsqrt(jnp.mean(c * c, axis=-1, keepdims=True) + EPS)
            r.n[pl.ds(pl.multiple_of(base + i * RC, RC), RC), :] = c * scale
            if keep:
                r.scale[pl.ds(pl.multiple_of(i * RC, RC), RC), :] = jnp.broadcast_to(scale, (RC, 128))
            return 0

        lax.fori_loop(0, T // RC, one, 0)

    norm_rows(r.tokens, x * T, True)

    relay("v", "z", "y", "x")
    relay("q", "z", "y", "x", 0)
    relay("v", "y", "c", "xz")
    relay("q", "z", "y", "x", 1)
    arrived("v")

    widths = [D // N, D // N, D // N, D // N, 3 * D // N, D // N, FF // N, D // N]

    def column(v, n):
        j = iota((1, n), 1)
        if v == 4:
            head_at = x * HC + 2 * (j // 384) + (j % 128) // HD
            return head_at * (3 * HD) + ((j % 384) // 128) * HD + j % HD
        if v == 6:
            return (j // 64) * 128 + x * 64 + j % 64
        return j

    def lengths(v):
        return {4: 3 * HW, 6: FH}.get(v, D)

    vec2 = r.wv.reshape(N * 8, 128)

    def expand(v):
        n = lengths(v)
        j = column(v, n)
        pick = (iota((128, n), 0) == j % widths[v]).astype(F32).astype(BF16)
        rows_v = vec2[pl.ds(v, N, stride=8), :].astype(BF16)
        spread = mm(rows_v, pick)
        r.vrow[v : v + 1, 0:n] = jnp.sum(
            jnp.where(iota((N, n), 0) == j // widths[v], spread, 0.0), axis=0, keepdims=True
        )

    for v in range(8):
        expand(v)

    def row(v, n=D, off=0):
        return r.vrow[v : v + 1, off : off + n]

    def affine_attn(base):
        def one(i, _):
            at = pl.ds(pl.multiple_of(base + i * RC, RC), RC)
            r.ha[at, :] = (r.n[at, :] * row(0) + row(1)).astype(BF16)
            return 0

        lax.fori_loop(0, T // RC, one, 0)

    def affine_mlp(base):
        def one(i, _):
            at = pl.ds(pl.multiple_of(base + i * RC, RC), RC)
            r.hm[at, :] = (r.n[at, :] * row(2) + row(3)).astype(BF16)
            return 0

        lax.fori_loop(0, T // RC, one, 0)

    affine_attn(x * T)
    relay("d", "z", "y", "x", 0)
    relay("q", "y", "c", "xz", 0)
    affine_mlp(x * T)
    relay("q", "y", "c", "xz", 1)
    relay("d", "z", "y", "x", 1)

    wait("tok")
    norm_rows(r.tok2, xo * T, False)
    affine_attn(xo * T)
    affine_mlp(xo * T)
    relay("i", "z", "y", "x", 0)
    relay("d", "y", "c", "xz", 0)

    wq = r.wq.reshape(D, 3 * HW)

    def qkv(b):
        def one(i, _):
            at = pl.ds(pl.multiple_of(i * QB, QB), QB)
            u = mm(r.ha[at, :], wq[:, chunk("q", b)]) + row(4, 384, b * 384)
            for jj, name in enumerate("qkv"):
                w = u[:, jj * 128 : (jj + 1) * 128]
                if jj < 2:
                    w = turn(w, at, 1.0)
                if jj == 0:
                    w = w * HD**-0.5
                w = w.astype(BF16)
                held[name][at, b * 128 : (b + 1) * 128] = w
                if jj >= 1:
                    held[name + "t"][b * 128 : (b + 1) * 128, at] = w.T
            return 0

        arrived("q", b)
        lax.fori_loop(0, S // QB, one, 0)

    qkv(0)
    relay("i", "z", "y", "x", 1)
    relay("d", "y", "c", "xz", 1)
    qkv(1)
    arrived("d", 0)
    arrived("d", 1)
    wd = r.wd.reshape(D, D)
    mine = pl.ds(pl.multiple_of(x * HW, HW), HW)
    r.do2[rows_mine, :] = mm(r.cot[...], wd[mine, :], NT).astype(BF16)

    r.dk[...] = jnp.zeros_like(r.dk)
    r.dv[...] = jnp.zeros_like(r.dv)
    causal = iota((QB, QB), 0) <= iota((QB, QB), 1)

    def head(blocks, h, _):
        lanes = pl.ds(pl.multiple_of((h // 2) * 128, 128), 128)
        ours = (lane // HD) == h % 2
        head_rows = pl.ds(pl.multiple_of(h * HD, HD), HD)
        for i in blocks:
            here = slice(i * QB, (i + 1) * QB)
            qm = jnp.where(ours, r.q[here, lanes], jnp.zeros((), BF16))
            dom = jnp.where(ours, r.do2[here, lanes], jnp.zeros((), BF16))
            top = None
            for j in range(i + 1):
                st = mm(r.k[j * QB : (j + 1) * QB, lanes], qm, NT)
                if j == i:
                    st = jnp.where(causal, st, NEG)
                r.st[j] = st
                part = jnp.max(st, axis=0, keepdims=True)
                top = part if top is None else jnp.maximum(top, part)
            total = du = None
            for j in range(i + 1):
                e = jnp.exp(r.st[j] - top)
                r.st[j] = e
                dp = mm(r.v[j * QB : (j + 1) * QB, lanes], dom, NT)
                r.dp[j] = dp
                part, both = (jnp.sum(w, axis=0, keepdims=True) for w in (e, e * dp))
                total = part if total is None else total + part
                du = both if du is None else du + both
            scale = 1.0 / total
            delta = du * scale
            for j in range(i + 1):
                p = r.st[j] * scale
                r.pb[j * QB : (j + 1) * QB, :] = p.astype(BF16)
                ds = p * (r.dp[j] - delta)
                r.ds[j * QB : (j + 1) * QB, :] = ds.astype(BF16)
            n = (i + 1) * QB
            pb, ds = r.pb[0:n, :], r.ds[0:n, :]
            r.ot[head_rows, here] = mm(r.vt[head_rows, 0:n], pb).astype(BF16)
            r.dqt[head_rows, here] = mm(r.kt[head_rows, 0:n], ds)
            r.dk[0:n, lanes] += mm(ds, qm)
            r.dv[0:n, lanes] += mm(pb, dom)
        return 0

    per_x = T // QB

    def attend(theirs, first, last):
        for k in range(X):
            at = (1 - k if theirs else k) * per_x
            run = functools.partial(head, range(at, at + per_x))

            @pl.when(x == k)
            def _():
                lax.fori_loop(first, last, run, 0)

    attend(False, 0, 2)
    relay("i", "y", "c", "xz", 0)
    relay("o", "z", "y", "", 0)
    relay("o", "z", "y", "", 1)
    attend(False, 2, 4)
    relay("i", "y", "c", "xz", 1)
    r.hmt[...] = r.hm[...].T

    wi = r.wi.reshape(D, FH)
    wo = r.wo.reshape(FH, D)
    gi = r.gi.reshape(D, FH)
    go = r.go.reshape(FH, D)
    FB = 256

    def ff_cols(b):
        return pl.ds(pl.multiple_of(b * FB, FB), FB)

    def ff_forward(b, _):
        cols = ff_cols(b)
        f = mm(r.hm[...], wi[:, cols]) + r.vrow[6:7, cols]
        phi = 0.5 + 0.5 * lax.erf(f * (0.5**0.5))
        r.act[:, cols] = (f * phi).astype(BF16)
        r.slope[:, cols] = phi + f * (jnp.exp(-0.5 * f * f) * (0.5 / np.pi) ** 0.5)
        return 0

    arrived("i", 0)
    lax.fori_loop(0, FH // FB // 2, ff_forward, 0)
    arrived("i", 1)
    lax.fori_loop(FH // FB // 2, FH // FB, ff_forward, 0)

    wait("cot")
    r.cots[rows_mine, :] = r.cot[...]
    r.do2[rows_theirs, :] = mm(r.cots[rows_theirs, :], wd[mine, :], NT).astype(BF16)

    def out_grad(b, _):
        at = ff_cols(b)
        go[at, :] = mm(r.act[:, at], r.cots[...], TN).astype(BF16)
        return 0

    relay("o", "y", "c", "z", 0)
    lax.fori_loop(0, FH // FB, out_grad, 0)
    scatter("o", "c", "", 0)
    scatter("o", "c", "", 1)
    relay("o", "y", "c", "z", 1)

    def send_o(b):
        own_rows = slice(b * 128, (b + 1) * 128)
        to = pl.ds(pl.multiple_of(x * HW + b * 128, 128), 128)
        push(("o", b), r.ot.at[own_rows, rows_theirs], r.of.at[to, :], at_x)
        r.of[to, :] = r.ot[own_rows, rows_mine]
        r.gd.reshape(D, D)[to, :] = mm(r.ot[own_rows, :], r.cots[...]).astype(BF16)
        push(("gc", b), r.gd.at[x * (Z // X) + b, :, 1 - me["c"]], r.dc.at[b], others("c")[0])

    def gd_y(b):
        wait(("gc", b))
        at = (x * (Z // X) + b, slice(None), me["c"])
        r.gd[at] = (r.gd[at].astype(F32) + r.dc[b].astype(F32)).astype(BF16)
        push(("gy", b), r.gd.at[at[0], 1 - me["y"], me["c"]], r.dy.at[b], others("y")[0])

    def gd_x(b):
        wait(("gy", b))
        at = (x * (Z // X) + b, me["y"], me["c"])
        r.gd[at] = (r.gd[at].astype(F32) + r.dy[b].astype(F32)).astype(BF16)
        part = r.gd.at[at + (xo,)]
        push(("gx", b), part, part, at_x)

    r.vg[...] = jnp.zeros_like(r.vg)
    gq = r.gq.reshape(D, 3 * HW)

    def qkv_back(b):
        def one(i, _):
            at = pl.ds(pl.multiple_of(i * QB, QB), QB)
            cols = slice(b * 128, (b + 1) * 128)
            dq = r.dqt[cols, at].T
            out = (
                turn(dq, at, -1.0) * HD**-0.5,
                turn(r.dk[at, cols], at, -1.0),
                r.dv[at, cols],
            )
            for jj in range(3):
                w = out[jj].astype(BF16)
                to = slice(b * 384 + jj * 128, b * 384 + (jj + 1) * 128)
                r.dqkv[at, to] = w
                r.vg[4:5, to] += jnp.sum(w.astype(F32), axis=0, keepdims=True)
            return 0

        lax.fori_loop(0, S // QB, one, 0)
        cols = chunk("q", b)
        for k in range(D // QB):
            gq[k * QB : (k + 1) * QB, cols] = mm(
                r.ha[:, k * QB : (k + 1) * QB], r.dqkv[:, cols], TN
            ).astype(BF16)
        scatter("q", "c", "", b)

    attend(True, 0, 1)
    arrived("o", 0)
    arrived("o", 1)
    r.mos[...] = mm(r.act[rows_theirs, :], wo[...]).astype(BF16)
    push("mo", r.mos, r.mor, at_x)
    attend(True, 1, 2)
    step("o", "c", "y", "", 0)
    step("o", "c", "y", "", 1)
    send_o(0)
    qkv_back(0)
    attend(True, 2, 4)
    send_o(1)
    gd_y(0)
    step("q", "c", "y", "", 0)
    step("o", "y", "z", "c", 0)
    step("o", "y", "z", "c", 1)
    qkv_back(1)
    gd_x(0)
    gd_y(1)

    def ff_backward(b, _):
        cols = ff_cols(b)
        df = (mm(r.cots[...], wo[cols, :], NT) * r.slope[:, cols]).astype(BF16)
        r.vg[6:7, cols] = jnp.sum(df.astype(F32), axis=0, keepdims=True)
        r.df[:, cols] = df
        gi[:, cols] = mm(r.hmt[...], df).astype(BF16)
        return 0

    lax.fori_loop(0, FH // FB // 2, ff_backward, 0)
    scatter("i", "c", "", 0)
    step("q", "c", "y", "", 1)
    gd_x(1)
    lax.fori_loop(FH // FB // 2, FH // FB, ff_backward, 0)
    scatter("i", "c", "", 1)
    step("i", "c", "y", "", 0)

    def input_grads(base, mine_too):
        def one(i, _):
            at = pl.ds(pl.multiple_of(base + i * QB, QB), QB)
            to = pl.ds(pl.multiple_of(i * QB, QB), QB)
            n = r.n[at, :]
            dm = mm(r.df[at, :], wi[...], NT)
            r.vg[2:3, 0:D] += jnp.sum(dm * n, axis=0, keepdims=True)
            r.vg[3:4, 0:D] += jnp.sum(dm, axis=0, keepdims=True)
            dh = mm(r.dqkv[at, :], wq[...], NT)
            r.vg[0:1, 0:D] += jnp.sum(dh * n, axis=0, keepdims=True)
            r.vg[1:2, 0:D] += jnp.sum(dh, axis=0, keepdims=True)
            u = dh * row(0) + dm * row(2)
            if mine_too:
                r.u[to, :] = u
            else:
                r.us[to, :] = u.astype(BF16)
            return 0

        lax.fori_loop(0, T // QB, one, 0)

    input_grads(xo * T, False)
    for k in range(T // QB):
        part = slice(k * QB, (k + 1) * QB)
        push(("u", k), r.us.at[part, :], r.ur.at[part, :], at_x)
    step("i", "c", "y", "", 1)
    step("q", "y", "z", "c", 0)
    step("q", "y", "z", "c", 1)
    input_grads(x * T, True)

    g_sum = jnp.sum(r.cot[...].astype(F32), axis=0, keepdims=True)
    r.vg[5:6, 0:D] = g_sum
    r.vg[7:8, 0:D] = g_sum
    gv2 = r.gv.reshape(N * 8, 128)

    def collapse(v):
        n = lengths(v)
        j = column(v, n)
        pick = (iota((128, n), 0) == j % widths[v]).astype(F32).astype(BF16)
        left = jnp.where(iota((N, n), 0) == j // widths[v], r.vg[v : v + 1, 0:n], 0.0)
        acc = None
        for _ in range(3):
            low = left.astype(BF16)
            part = mm(low, pick, NT)
            acc = part if acc is None else acc + part
            left = left - low.astype(F32)
        gv2[pl.ds(v, N, stride=8), :] = acc

    for v in range(8):
        collapse(v)
    scatter("v", "c", "")
    wait(("gx", 0))
    wait(("gx", 1))
    scatter("d", "z", "cyx")
    step("i", "y", "z", "c", 0)
    r.mo[...] = mm(r.act[rows_mine, :], wo[...])
    step("i", "y", "z", "c", 1)

    def flat(out, width, k=None, part=D):
        per = width // 128
        n = out.shape[0] // per
        lo = 0 if k is None else k * (part // 128)

        def put(acc):
            for j in range(acc.shape[1] // 128):
                out[pl.ds(lo + j, n, stride=per), :] = acc[:, j * 128 : (j + 1) * 128]

        return put

    step("v", "c", "y")
    add_parts("o", "z", "cy", 0, flat(r.oo, D, 0, CH["o"]))
    add_parts("o", "z", "cy", 1, flat(r.oo, D, 1, CH["o"]))
    at_me = (me["z"], me["y"], me["c"])
    step("v", "y", "z", "c")
    add_parts("q", "z", "cy", 0)
    add_parts("q", "z", "cy", 1)
    push("sq", r.gq.at[at_me + (xo,)], r.xq, at_x)

    wait(("o", 0))
    wait(("o", 1))
    wait("mo")
    r.out[...] = (
        r.tokens[...].astype(F32)
        + mm(r.of[...], wd[...], TN)
        + row(5)
        + (r.mo[...] + r.mor[...].astype(F32) + row(7))
    ).astype(BF16)
    step("v", "z", "x", "cy")
    add_parts("d", "z", "cyx", None, flat(r.od, D))
    add_parts("i", "z", "cy", 0)
    add_parts("i", "z", "cy", 1)
    push("si", r.gi.at[at_me + (xo,)], r.xi, at_x)


    def final_rows(i, _):
        at = pl.ds(pl.multiple_of(i * RC, RC), RC)
        far = pl.ds(pl.multiple_of(x * T + i * RC, RC), RC)
        u = r.u[at, :] + r.ur[at, :].astype(F32)
        n = r.n[far, :]
        back = u - jnp.mean(u, axis=-1, keepdims=True) - n * jnp.mean(u * n, axis=-1, keepdims=True)
        r.gtok[at, :] = (r.cot[at, :].astype(F32) + back * r.scale[at, 0:1]).astype(BF16)
        return 0

    for k in range(T // QB):
        wait(("u", k))
        lax.fori_loop(k * (QB // RC), (k + 1) * (QB // RC), final_rows, 0)

    def join(mine_ref, got, out, width, place):
        per = width // 128
        n = out.shape[0] // per
        here = mine_ref[at_me + (x,)].astype(F32)
        there = got[...].astype(F32)
        halves = (jnp.where(x == 0, here, there), jnp.where(x == 0, there, here))

        def piece(b, to_high):
            half, m, odd = place(b)
            v = halves[half][:, m * 128 : (m + 1) * 128]
            return pltpu.roll(v, 64, 1) if odd != to_high else v

        for j in range(per):
            both = jnp.where(lane < 64, piece(2 * j, False), piece(2 * j + 1, True))
            out[pl.ds(j, n, stride=per), :] = both

    def place_q(b):
        h, jj = b // 3, b % 3
        return h // HC, (h % HC) // 2 * 3 + jj, h % 2 == 1

    def place_i(b):
        return b % 2, b // 4, (b // 2) % 2 == 1

    wait("sq")
    join(r.gq, r.xq, r.oq, 3 * D, place_q)
    wait("si")
    join(r.gi, r.xi, r.oi, FF, place_i)

    def put_vec(acc):
        r.ov[...] = acc

    add_parts("v", "x", "cyz", None, put_vec)


def rope_table(length):
    lanes = np.arange(128) % HD
    rot = HD // 4
    inverse = np.where(lanes < rot, 1.0 / ROPE_BASE ** (2.0 * (lanes % (rot // 2)) / rot), 0.0)
    high = 32.0 * np.arange(length // 32)[:, None] * inverse
    low = np.arange(32)[:, None] * inverse
    return np.stack([np.cos(high), np.sin(high), np.cos(low), np.sin(low)]).astype(np.float32)


def hand_over(*refs):
    for src, dst in zip(refs[:6], refs[7:13]):
        dst[...] = src[...]
    for v, dst in enumerate(refs[13:]):
        dst[...] = refs[6][v : v + 1, 0 : dst.shape[1]]


def layer(sizes, tokens, cotangent, *params):
    Z, Y, C, X = (sizes[a] for a in AX)
    N = Z * Y * C * X
    T = tokens.shape[1]
    S = T * X
    HW = HEADS // X * HD
    vectors = [params[i] for i in (0, 1, 2, 3, 5, 7, 9, 11)]
    weights = [params[i] for i in (4, 6, 8, 10)]
    flats = [w.reshape(-1, 128) for w in weights]
    full = dict(z=Z, y=Y, c=C, x=X)

    FH = FF // X

    def parts(name, axis, done, slab, dtype):
        free = [full[a] for a in AX if a not in done and a != axis and (a != "x" or name != "o")]
        return pltpu.VMEM((full[axis] - 1, *free, *slab), dtype)

    slabs = {
        "q": (D // N, 3 * HW),
        "d": (D // N, D),
        "i": (D // N, FH),
        "o": (FF // N, D),
        "v": (8, 128),
    }
    orders = {"q": "cyz", "d": "z", "i": "cyz", "o": "cyz", "v": "cyzx"}
    keep = types.SimpleNamespace()
    scratch = vars(keep)
    for k, slab in slabs.items():
        kind = F32 if k == "v" else BF16
        devs = (Z, Y, C) if k == "o" else (Z, Y, C, X)
        scratch["w" + k] = pltpu.VMEM((*devs, *slab), kind)
        scratch["g" + k] = pltpu.VMEM((*devs, *slab), kind)
        for n, axis in enumerate(orders[k]):
            done = "cyx" if k == "d" else orders[k][:n]
            scratch["r" + k + axis] = parts(k, axis, done, slab, kind)
    keep.dc = pltpu.VMEM((X, Y, X, *slabs["d"]), BF16)
    keep.dy = pltpu.VMEM((X, X, *slabs["d"]), BF16)
    keep.xq = pltpu.VMEM(slabs["q"], BF16)
    keep.xi = pltpu.VMEM(slabs["i"], BF16)
    keep.sq = pltpu.VMEM((X, *slabs["q"]), BF16)
    keep.si = pltpu.VMEM((X, *slabs["i"]), BF16)
    keep.tmp = pltpu.VMEM((max(f.shape[0] for f in flats), 128), F32)
    keep.cos = keep.sinl = keep.sinh = pltpu.VMEM((S, 128), F32)
    keep.tok2 = pltpu.VMEM((T, D), BF16)
    keep.cots = pltpu.VMEM((S, D), BF16)
    keep.n = pltpu.VMEM((S, D), F32)
    keep.scale = pltpu.VMEM((T, 128), F32)
    keep.vrow = pltpu.VMEM((8, FH), F32)
    keep.vg = pltpu.VMEM((8, FH), F32)
    keep.ha = keep.hm = pltpu.VMEM((S, D), BF16)
    keep.hmt = pltpu.VMEM((D, S), BF16)
    keep.q = keep.k = keep.v = keep.do2 = pltpu.VMEM((S, HW), BF16)
    keep.kt = keep.vt = keep.ot = pltpu.VMEM((HW, S), BF16)
    keep.dqt = pltpu.VMEM((HW, S), F32)
    keep.dk = pltpu.VMEM((S, HW), F32)
    keep.dv = pltpu.VMEM((S, HW), F32)
    keep.st = pltpu.VMEM((S // QB, QB, QB), F32)
    keep.dp = pltpu.VMEM((S // QB, QB, QB), F32)
    keep.pb = pltpu.VMEM((S, QB), BF16)
    keep.ds = pltpu.VMEM((S, QB), BF16)
    keep.dqkv = pltpu.VMEM((S, 3 * HW), BF16)
    keep.of = pltpu.VMEM((D, T), BF16)
    keep.act = keep.df = pltpu.VMEM((S, FH), BF16)
    keep.slope = pltpu.VMEM((S, FH), F32)
    keep.u = keep.mo = pltpu.VMEM((T, D), F32)
    keep.us = keep.ur = keep.mos = keep.mor = pltpu.VMEM((T, D), BF16)
    copies = 128
    keep.send = pltpu.SemaphoreType.DMA((copies,))
    keep.recv = pltpu.SemaphoreType.DMA((copies,))
    ins = "tokens cot fq fd".split() + "fi fo rope".split() + ["v%d" % v for v in range(8)]
    outs = dict(
        out=jax.ShapeDtypeStruct((T, D), BF16),
        gtok=jax.ShapeDtypeStruct((T, D), BF16),
        oq=jax.ShapeDtypeStruct(flats[0].shape, F32),
        od=jax.ShapeDtypeStruct(flats[1].shape, F32),
        oi=jax.ShapeDtypeStruct(flats[2].shape, F32),
        oo=jax.ShapeDtypeStruct(flats[3].shape, F32),
        ov=jax.ShapeDtypeStruct((8, 128), F32),
    )
    vmem = pl.BlockSpec(memory_space=pltpu.VMEM)
    shown = tokens.reshape(T, D), cotangent.reshape(T, D), *flats, jnp.asarray(rope_table(S))
    shown += tuple(v.reshape(1, -1) for v in vectors)
    for name, a in zip(ins, shown):
        scratch[name] = pltpu.VMEM(a.shape, a.dtype)
    keep.load = pltpu.SemaphoreType.DMA((len(ins),))
    names = ["h" + n for n in ins] + list(outs) + list(scratch)
    out, gtok, gq, gd, gi, go, gv = pl.pallas_call(
        functools.partial(fused, sizes, names),
        out_shape=list(outs.values()),
        in_specs=[pl.BlockSpec(memory_space=pl.ANY)] * len(ins),
        out_specs=[vmem] * len(outs),
        scratch_shapes=list(scratch.values()),
        compiler_params=pltpu.CompilerParams(
            collective_id=0, has_side_effects=True, vmem_limit_bytes=67043328
        ),
        name="layer",
    )(
        *shown
    )
    shapes = [jax.ShapeDtypeStruct(a.shape, a.dtype) for a in (out, gtok, gq, gd, gi, go)]
    shapes += [jax.ShapeDtypeStruct((1, p.shape[0]), F32) for p in vectors]
    out, gtok, gq, gd, gi, go, *v = pl.pallas_call(
        hand_over,
        out_shape=shapes,
        in_specs=[vmem] * 7,
        out_specs=[vmem] * len(shapes),
        name="results",
    )(out, gtok, gq, gd, gi, go, gv)
    v = [a.reshape(-1) for a in v]
    return (
        out.reshape(tokens.shape),
        gtok.reshape(tokens.shape),
        v[0],
        v[1],
        v[2],
        v[3],
        gq.reshape(-1),
        v[4],
        gd.reshape(-1),
        v[5],
        gi.reshape(-1),
        v[6],
        go.reshape(-1),
        v[7],
    )


def solution(mesh):
    n_seq, n_ctx = mesh.shape["seq"], mesh.shape["ctx"]
    if n_ctx != 2 or n_seq != 16 or (D // (n_seq * n_ctx)) % 16:
        return general(mesh)
    sizes = {"z": n_seq // 4, "y": 2, "c": 2, "x": n_ctx}
    flat = P(("seq", "ctx"))
    rows = P("seq", "ctx", None)
    return jax.shard_map(
        functools.partial(layer, sizes),
        mesh=mesh,
        in_specs=(rows, rows) + (flat,) * 12,
        out_specs=(rows, rows) + (flat,) * 12,
        check_vma=False,
    )
```
